32 devices in a mesh: dp: 2 (over x), expert: 8 (over z, y), tensor: 2 (over core).
Axes of the slice: x: 2, y: 2, z: 4, core: 2. Of those that a mesh axis runs over, the one named last changes fastest.
Arguments:
- activations: bfloat16 [4096, 1536], P(('dp', 'expert', 'tensor')), may hold values from -6 to 6
- segments: int32 [16, 256], P(('dp', 'expert')), may hold values from 0 to 3, never falling along the last dimension, each value on 1 to 128 neighbouring positions
- routes: int32 [4096, 8], P(('dp', 'expert', 'tensor')), may hold values from 0 to 15, all different within a row; in each aligned block of 128 rows (0 to 127, 128 to 255, ...) at most 128 rows name the same one
- route_weights: float32 [4096, 8], P(('dp', 'expert', 'tensor')), may hold values from 0.03 to 0.3
- norm_attn_gain: float32 [1536], replicated, may hold values from 0.5 to 1.5
- norm_ffn_gain: float32 [1536], replicated, may hold values from 0.5 to 1.5
- query_weight: bfloat16 [1536, 1536], P(None, 'tensor'), may hold values from -0.15625 to 0.15625
- key_matrix: bfloat16 [1536, 512], P(None, 'tensor'), may hold values from -0.15625 to 0.15625
- value_matrix: bfloat16 [1536, 512], P(None, 'tensor'), may hold values from -0.15625 to 0.15625
- output_projection_weight: bfloat16 [1536, 1536], P('tensor'), may hold values from -0.625 to 0.625
- expert_gate: bfloat16 [16, 1536, 512], P('expert', None, 'tensor'), may hold values from -0.15625 to 0.15625
- expert_up: bfloat16 [16, 1536, 512], P('expert', None, 'tensor'), may hold values from -0.15625 to 0.15625
- expert_down: bfloat16 [16, 512, 1536], P('expert', 'tensor'), may hold values from -0.5 to 0.5
- grad_output: bfloat16 [4096, 1536], P(('dp', 'expert', 'tensor')), may hold values from -6 to 6
Outputs:
- block_out: bfloat16 [4096, 1536], P(('dp', 'expert', 'tensor'))
- grad_input: float32 [4096, 1536], P(('dp', 'expert', 'tensor'))
- grad_norm_attn: float32 [1536], replicated
- grad_norm_ffn: float32 [1536], replicated
- grad_query: float32 [1536, 1536], P(None, 'tensor')
- grad_key: float32 [1536, 512], P(None, 'tensor')
- grad_value: float32 [1536, 512], P(None, 'tensor')
- grad_mixer: float32 [1536, 1536], P('tensor')
- grad_expert_gate: float32 [16, 1536, 512], P('expert', None, 'tensor')
- grad_expert_up: float32 [16, 1536, 512], P('expert', None, 'tensor')
- grad_expert_down: float32 [16, 512, 1536], P('expert', 'tensor')
The draws below stay inside these ranges and needn't reach their ends.
Inputs may be any that keep to these rules, and one draw needn't show every extreme that they name: `routes`: each row names 8 different experts; in the rows of one device (aligned blocks of 128 rows) no expert is named more than 128 times, and one is named exactly 128 times in some block. `segments`: each sequence's numbers never fall; 4 documents of 1 to 128 positions, one of exactly 128.
All inputs are finite; a program needn't handle non-finite values.
Results may differ from the reference program's by a relative error of at most 0.01.
Values may be sent and summed in bfloat16 or wider, within the bound.
No kernel may reach another device: no remote copies, remote signals or barrier semaphores. Data moves between devices by JAX's collectives and lax.ppermute only.
A program may use at most 320 MiB of HBM per device.

```python
import math
import jax
import jax.numpy as jnp
import numpy as np
from jax import lax

MODEL_DIM = 1536
QUERY_HEADS = 24
KEY_VALUE_HEADS = 8
HEAD_DIM = 64
EXPERT_HIDDEN = 512
TOP = 8
SEQUENCE_TOKENS = 256
SEGS = 4
SEG_MOST = 128
TOK_DEV = 128
NSEQ = 16
TOKENS = 4096
EXPERT_WINDOW = 16
CAP = 128
N_TENSOR = 2


def block_levels(own_key, shape, cuts, least, high):
    gain, own = 1.0, jax.random.fold_in(own_key, 6)
    for dim, blocks in cuts:
        steps = jnp.exp(jax.random.uniform(jax.random.fold_in(own, dim), (blocks,), jnp.float32, least / len(cuts), high / len(cuts)))
        gain = gain * jnp.repeat(steps, shape[dim] // blocks).reshape([-1 if axis == dim else 1 for axis in range(len(shape))])
    return gain


def length_profile(number_of, total, limit, lean):
    loads = [(1 << 20) // math.isqrt(rank ** lean) + 1 for rank in range(2, number_of + 1)]
    rest, given = total - limit - (number_of - 1), [1] * (number_of - 1)
    while rest > 0:
        candidates = [i for i in range(number_of - 1) if given[i] < limit]
        mass, left = sum([loads[i] for i in candidates]), rest
        for i in candidates:
            addition = min(limit - given[i], max(1, left * loads[i] // mass), rest)
            given[i] = given[i] + addition
            rest = rest - addition
    return np.array([limit] + given)


def ragged_sizes(rng, amount, total, reach, slope):
    if amount == 2:
        one = jax.random.randint(rng, (), max(1, total - reach), min(reach, total - 1) + 1)
        return jnp.stack([one, total - one])
    tallies = jnp.asarray(length_profile(amount, total, reach, slope), jnp.int32)
    pairs = (amount - 1) // 2
    giver, sink = tallies[1:1 + 2 * pairs:2], tallies[2:2 + 2 * pairs:2]
    room = jnp.minimum(giver - 1, reach - sink)
    moved = jax.random.randint(jax.random.fold_in(rng, 1), (pairs,), 0, 1 << 20) % (room + 1)
    tallies = tallies.at[1:1 + 2 * pairs:2].set(giver - moved).at[2:2 + 2 * pairs:2].set(sink + moved)
    return tallies[jax.random.permutation(jax.random.fold_in(rng, 2), amount)]


def deal_out(stream_key, own, number, rows, number_of, top, bound, slope):
    order = jax.random.permutation(stream_key, number_of)
    crowded, ordinary = shares(number_of, rows * top, bound, slope, True), shares(number_of, rows * top, bound, slope, False)
    places = jnp.arange(number_of)

    def named(tallies, rotation):
        used = int((tallies > 0).sum())
        fixed = max(1, used // 4)
        moved = fixed + (places - fixed + rotation * (used - fixed)) % max(1, number_of - fixed)
        return jnp.zeros((number_of,), jnp.int32).at[order[jnp.where(places < fixed, places, moved)]].set(jnp.asarray(tallies, jnp.int32))

    tallies = jnp.where(number % 4 == 0, named(crowded, number // 4), named(ordinary, number - number // 4 - 1))
    mixed = jax.random.permutation(jax.random.fold_in(own, 3), number_of)
    source_of, taker = mixed[0:number_of // 2 * 2:2], mixed[1:number_of // 2 * 2:2]
    slack = jnp.minimum(tallies[source_of] - 1, bound - tallies[taker]) // 2
    slack = jnp.where((source_of == order[0]) | (taker == order[0]) | (tallies[taker] == 0), 0, jnp.maximum(slack, 0))
    moved = jax.random.randint(jax.random.fold_in(own, 4), (number_of // 2,), 0, 1 << 20) % (slack + 1)
    tallies = tallies.at[source_of].add(-moved).at[taker].add(moved)
    items = jnp.searchsorted(jnp.cumsum(tallies), jnp.arange(rows * top), side="right").astype(jnp.int32)
    grid = items.reshape(top, rows).T
    grid = grid[jax.random.permutation(jax.random.fold_in(own, 1), rows)]
    rotation = jax.random.randint(jax.random.fold_in(own, 2), (rows, 1), 0, top)
    return jnp.take_along_axis(grid, (jnp.arange(top)[None, :] + rotation) % top, axis=1)


def shares(count, total, most, slope, full):
    portions = [(1 << 20) // math.isqrt(standing ** slope) + 1 for standing in range(1, count + 1)]
    largest = most if full else min(most, max(-(-total // count), total * portions[0] // sum(portions)))
    least = 1 if total - largest >= count - 1 else 0
    holding, spare = [largest] + [least] * (count - 1), total - largest - least * (count - 1)
    while spare > 0:
        candidates = [i for i in range(1, count) if holding[i] < largest] or [i for i in range(1, count) if holding[i] < most]
        whole, left = sum([portions[i] for i in candidates]), spare
        for i in candidates:
            extra = min(most - holding[i], max(1, left * portions[i] // whole), spare)
            holding[i] = holding[i] + extra
            spare = spare - extra
    return np.array(holding)


def normal_values(rng, extent, width, most, cuts=(), kind=jnp.bfloat16):
    result = width * jax.random.normal(rng, extent, jnp.float32)
    if cuts:
        result = result * block_levels(rng, extent, cuts, -0.22, 0.18)
    return jnp.clip(result, -most, most).astype(kind)


def setup_inputs(seed: int = 0) -> dict:
    keys = jax.random.split(jax.random.key(seed), 15)
    activations = normal_values(keys[0], (TOKENS, MODEL_DIM), 1.0, 6.0, ((0, 32),))
    segments = jax.vmap(lambda own: jnp.searchsorted(jnp.cumsum(ragged_sizes(own, SEGS, SEQUENCE_TOKENS, SEG_MOST, 2)), jnp.arange(SEQUENCE_TOKENS), side="right"))(jax.random.split(keys[1], NSEQ)).reshape((NSEQ, SEQUENCE_TOKENS)).astype(jnp.int32)
    routes_keys = jax.random.split(jax.random.fold_in(keys[2], 1), TOKENS // TOK_DEV)
    routes_turns = jax.random.permutation(jax.random.fold_in(keys[2], 3), TOKENS // TOK_DEV)
    routes = jax.vmap(lambda own, number: deal_out(jax.random.fold_in(keys[2], 2), own, number, TOK_DEV, EXPERT_WINDOW, TOP, CAP, 2))(routes_keys, routes_turns).reshape((TOKENS, TOP))
    route_weights = jnp.clip(jnp.exp(math.log(0.3) - 2.3025852 * jax.random.uniform(keys[3], (TOKENS, TOP), jnp.float32) ** block_levels(keys[3], (TOKENS, TOP), ((0, 32),), -0.2, 0.2)), 0.03, 0.3)
    norm_attn_gain = jnp.clip(1.0 + 0.1 * jax.random.normal(keys[4], (MODEL_DIM,), jnp.float32), 0.5, 1.5)
    norm_ffn_gain = jnp.clip(1.0 + 0.1 * jax.random.normal(keys[5], (MODEL_DIM,), jnp.float32), 0.5, 1.5)
    query_weight = normal_values(keys[6], (MODEL_DIM, QUERY_HEADS * HEAD_DIM), MODEL_DIM ** -0.5, 0.15625, ((1, 2),))
    key_matrix = normal_values(keys[7], (MODEL_DIM, KEY_VALUE_HEADS * HEAD_DIM), MODEL_DIM ** -0.5, 0.15625, ((1, 2),))
    value_matrix = normal_values(keys[8], (MODEL_DIM, KEY_VALUE_HEADS * HEAD_DIM), MODEL_DIM ** -0.5, 0.15625, ((1, 2),))
    output_projection_weight = normal_values(keys[9], (QUERY_HEADS * HEAD_DIM, MODEL_DIM), (QUERY_HEADS * HEAD_DIM // 16) ** -0.5, 0.625, ((0, 2),))
    expert_gate = normal_values(keys[10], (EXPERT_WINDOW, MODEL_DIM, EXPERT_HIDDEN), MODEL_DIM ** -0.5, 0.15625, ((0, 8), (2, 2)))
    expert_up = normal_values(keys[11], (EXPERT_WINDOW, MODEL_DIM, EXPERT_HIDDEN), MODEL_DIM ** -0.5, 0.15625, ((0, 8), (2, 2)))
    expert_down = normal_values(keys[12], (EXPERT_WINDOW, EXPERT_HIDDEN, MODEL_DIM), (EXPERT_HIDDEN // 4) ** -0.5, 0.5, ((0, 8), (1, 2)))
    grad_output = normal_values(keys[13], (TOKENS, MODEL_DIM), 1.0, 6.0, ((0, 32),))
    return {"activations": activations, "segments": segments, "routes": routes, "route_weights": route_weights, "norm_attn_gain": norm_attn_gain, "norm_ffn_gain": norm_ffn_gain, "query_weight": query_weight, "key_matrix": key_matrix, "value_matrix": value_matrix, "output_projection_weight": output_projection_weight, "expert_gate": expert_gate, "expert_up": expert_up, "expert_down": expert_down, "grad_output": grad_output}


EPS = 1e-05
ATTN_SCALE = 0.015625
THETA = 10000.0
NEG_FILL = -1e+30

def rounded_values(array_in):
    return lax.optimization_barrier(array_in.astype(jnp.bfloat16))

def expand_heads(array_in):
    return array_in.astype(jnp.float32)

def norm_forward(values, gain_vector):
    inv_scale = lax.rsqrt(lax.optimization_barrier(jnp.mean(values * values, axis=-1, keepdims=True)) + EPS)
    return (values * inv_scale * gain_vector, inv_scale)

def norm_backward(values, inv_scale, gain_vector, upstream):
    weighted = upstream * gain_vector
    inner = lax.optimization_barrier(jnp.mean(weighted * values, axis=-1, keepdims=True))
    value_gradient = inv_scale * weighted - values * (inv_scale * inv_scale * inv_scale) * inner
    grad_gain = lax.optimization_barrier(jnp.sum(upstream * values * inv_scale, axis=0))
    return (value_gradient, grad_gain)

def rope_tables(length, head_size):
    position = jnp.arange(length, dtype=jnp.float32)
    frequency = THETA ** (-jnp.arange(head_size // 2, dtype=jnp.float32) * 2.0 / head_size)
    angle_table = position[:, None] * frequency[None, :]
    return (jnp.cos(angle_table)[:, None, :], jnp.sin(angle_table)[:, None, :])

def apply_rotary(field_in, cosine_lookup, sine_lookup):
    half_size = field_in.shape[-1] // 2
    first_half = field_in[..., :half_size]
    second_half = field_in[..., half_size:]
    return jnp.concatenate([first_half * cosine_lookup - second_half * sine_lookup, second_half * cosine_lookup + first_half * sine_lookup], axis=-1)

def invert_rotary(field_in, cosine_lookup, sine_lookup):
    half_size = field_in.shape[-1] // 2
    first_half = field_in[..., :half_size]
    second_half = field_in[..., half_size:]
    return jnp.concatenate([first_half * cosine_lookup + second_half * sine_lookup, second_half * cosine_lookup - first_half * sine_lookup], axis=-1)

def mask_block(row_start, block_rows, seg_ids):
    length = seg_ids.shape[0]
    row_pos = row_start + jnp.arange(block_rows, dtype=jnp.int32)
    key_pos = jnp.arange(length, dtype=jnp.int32)
    row_seg = lax.dynamic_slice_in_dim(seg_ids, row_start, block_rows, 0)
    return (key_pos[None, :] <= row_pos[:, None]) & (seg_ids[None, :] == row_seg[:, None])

def block_scores(query_blk, key_heads, row_start, seg_ids):
    scores = jnp.einsum('qhgd,khd->hgqk', expand_heads(query_blk), expand_heads(key_heads)) * ATTN_SCALE
    allowed = mask_block(row_start, query_blk.shape[0], seg_ids)
    return jnp.where(allowed, scores, NEG_FILL)

def attend_block(query_blk, key_heads, value_head_rows, row_start, seg_ids):
    scores = block_scores(query_blk, key_heads, row_start, seg_ids)
    top_score = lax.optimization_barrier(jnp.max(scores, axis=-1, keepdims=True))
    exp_total = lax.optimization_barrier(jnp.sum(jnp.exp(scores - top_score), axis=-1, keepdims=True))
    log_total = top_score + jnp.log(exp_total)
    weights_soft = jnp.exp(scores - log_total)
    mixed_heads = jnp.einsum('hgqk,khd->qhgd', expand_heads(rounded_values(weights_soft)), expand_heads(value_head_rows))
    return (rounded_values(mixed_heads), log_total[..., 0])

def attend_back(query_blk, key_heads, value_head_rows, log_total, grad_blk, mixed_blk, row_start, seg_ids):
    scores = block_scores(query_blk, key_heads, row_start, seg_ids)
    weights_soft = jnp.exp(scores - log_total[..., None])
    row_delta = jnp.einsum('qhgd,qhgd->hgq', expand_heads(grad_blk), expand_heads(mixed_blk))
    grad_soft = jnp.einsum('qhgd,khd->hgqk', expand_heads(grad_blk), expand_heads(value_head_rows))
    grad_scores = rounded_values(weights_soft * (grad_soft - row_delta[..., None]) * ATTN_SCALE)
    grad_queries = jnp.einsum('hgqk,khd->qhgd', expand_heads(grad_scores), expand_heads(key_heads))
    key_gradient = jnp.einsum('hgqk,qhgd->khd', expand_heads(grad_scores), expand_heads(query_blk))
    value_gradient = jnp.einsum('hgqk,qhgd->khd', expand_heads(rounded_values(weights_soft)), expand_heads(grad_blk))
    return (grad_queries, key_gradient, value_gradient)

def route_index(route_blk, expert_count, capacity):
    flat_routes = route_blk.reshape(-1)
    onehot = (flat_routes[:, None] == jnp.arange(expert_count, dtype=jnp.int32)[None, :]).astype(jnp.int32)
    earlier = jnp.cumsum(onehot, axis=0) - onehot
    slot_rank = lax.optimization_barrier(jnp.sum(earlier * onehot, axis=1))
    return (flat_routes * capacity + slot_rank).astype(jnp.int32)

def reference(activations, segments, routes, route_weights, norm_attn_gain, norm_ffn_gain, query_weight, key_matrix, value_matrix, output_projection_weight, expert_gate, expert_up, expert_down, grad_output):
    group_factor = QUERY_HEADS // KEY_VALUE_HEADS
    cosine_lookup, sine_lookup = rope_tables(SEQUENCE_TOKENS, HEAD_DIM)
    seq_acts = activations.reshape(NSEQ, SEQUENCE_TOKENS, MODEL_DIM)
    seq_routes = routes.reshape(NSEQ, N_TENSOR, TOK_DEV, TOP)
    seq_weights = route_weights.reshape(NSEQ, N_TENSOR, TOK_DEV, TOP)
    seq_grads = grad_output.reshape(NSEQ, SEQUENCE_TOKENS, MODEL_DIM)

    def moe_block(h_block, route_blk, weight_blk, upstream_blk):
        slot_index = route_index(route_blk, EXPERT_WINDOW, CAP)
        row_copies = jnp.repeat(h_block, TOP, axis=0)
        buffer = jnp.zeros((EXPERT_WINDOW * CAP, MODEL_DIM), jnp.bfloat16).at[slot_index].set(row_copies).reshape(EXPERT_WINDOW, CAP, MODEL_DIM)
        pre_gate = jnp.einsum('ecd,edf->ecf', expand_heads(buffer), expand_heads(expert_gate))
        pre_up = jnp.einsum('ecd,edf->ecf', expand_heads(buffer), expand_heads(expert_up))
        activated = rounded_values(jax.nn.silu(pre_gate) * pre_up)
        expert_out = rounded_values(jnp.einsum('ecf,efd->ecd', expand_heads(activated), expand_heads(expert_down)))
        picked = expand_heads(expert_out.reshape(-1, MODEL_DIM)[slot_index].reshape(TOK_DEV, TOP, MODEL_DIM))
        expert_mix = lax.optimization_barrier(jnp.sum(weight_blk[:, :, None] * picked, axis=1))
        grad_copies = rounded_values(weight_blk[:, :, None] * upstream_blk[:, None, :]).reshape(-1, MODEL_DIM)
        grad_buffer = jnp.zeros((EXPERT_WINDOW * CAP, MODEL_DIM), jnp.bfloat16).at[slot_index].set(grad_copies).reshape(EXPERT_WINDOW, CAP, MODEL_DIM)
        grad_down = jnp.einsum('ecf,ecd->efd', expand_heads(activated), expand_heads(grad_buffer))
        grad_act = jnp.einsum('ecd,efd->ecf', expand_heads(grad_buffer), expand_heads(expert_down))
        gate_sigmoid = jax.nn.sigmoid(pre_gate)
        grad_pre_gate = rounded_values(grad_act * pre_up * gate_sigmoid * (1.0 + pre_gate * (1.0 - gate_sigmoid)))
        grad_pre_up = rounded_values(grad_act * pre_gate * gate_sigmoid)
        grad_gate = jnp.einsum('ecd,ecf->edf', expand_heads(buffer), expand_heads(grad_pre_gate))
        grad_up = jnp.einsum('ecd,ecf->edf', expand_heads(buffer), expand_heads(grad_pre_up))
        grad_rows = rounded_values(jnp.einsum('ecf,edf->ecd', expand_heads(grad_pre_gate), expand_heads(expert_gate)) + jnp.einsum('ecf,edf->ecd', expand_heads(grad_pre_up), expand_heads(expert_up)))
        picked_grad = expand_heads(grad_rows.reshape(-1, MODEL_DIM)[slot_index].reshape(TOK_DEV, TOP, MODEL_DIM))
        grad_h = lax.optimization_barrier(jnp.sum(weight_blk[:, :, None] * picked_grad, axis=1))
        return (expert_mix, grad_h, grad_gate, grad_up, grad_down)

    def one_sequence(running, inputs):
        seq_in, seg_ids, route_blk, weight_blk, upstream_in = inputs
        x_in = expand_heads(seq_in)
        normed_one, scale_one = norm_forward(x_in, norm_attn_gain)
        hidden_first = rounded_values(normed_one)
        query_unrotated = jnp.dot(hidden_first, query_weight, preferred_element_type=jnp.float32).reshape(SEQUENCE_TOKENS, QUERY_HEADS, HEAD_DIM)
        query_head_rows = rounded_values(apply_rotary(query_unrotated, cosine_lookup, sine_lookup)).reshape(SEQUENCE_TOKENS, KEY_VALUE_HEADS, group_factor, HEAD_DIM)
        key_unrotated = jnp.dot(hidden_first, key_matrix, preferred_element_type=jnp.float32).reshape(SEQUENCE_TOKENS, KEY_VALUE_HEADS, HEAD_DIM)
        key_heads = rounded_values(apply_rotary(key_unrotated, cosine_lookup, sine_lookup))
        value_head_rows = rounded_values(jnp.dot(hidden_first, value_matrix, preferred_element_type=jnp.float32)).reshape(SEQUENCE_TOKENS, KEY_VALUE_HEADS, HEAD_DIM)
        mixed_heads, log_total = attend_block(query_head_rows, key_heads, value_head_rows, 0, seg_ids)
        mixed_flat = mixed_heads.reshape(SEQUENCE_TOKENS, QUERY_HEADS * HEAD_DIM)
        residual = x_in + jnp.dot(mixed_flat, output_projection_weight, preferred_element_type=jnp.float32)
        normed_two, scale_two = norm_forward(residual, norm_ffn_gain)
        h_two = rounded_values(normed_two)
        upstream = expand_heads(upstream_in)
        expert_mix, grad_h, grad_gate, grad_up, grad_down = jax.vmap(moe_block)(h_two.reshape(N_TENSOR, TOK_DEV, MODEL_DIM), route_blk, weight_blk, upstream.reshape(N_TENSOR, TOK_DEV, MODEL_DIM))
        seq_out = rounded_values(residual + expert_mix.reshape(SEQUENCE_TOKENS, MODEL_DIM))
        grad_norm_part, grad_ffn_gain = norm_backward(residual, scale_two, norm_ffn_gain, grad_h.reshape(SEQUENCE_TOKENS, MODEL_DIM))
        grad_resid = upstream + grad_norm_part
        residual_gradient_second = rounded_values(grad_resid)
        grad_mix_w = jnp.einsum('sa,sb->ab', expand_heads(mixed_flat), expand_heads(residual_gradient_second))
        mixed_gradient = rounded_values(jnp.einsum('im,dm->id', expand_heads(residual_gradient_second), expand_heads(output_projection_weight))).reshape(SEQUENCE_TOKENS, KEY_VALUE_HEADS, group_factor, HEAD_DIM)
        grad_queries, key_gradient, value_gradient = attend_back(query_head_rows, key_heads, value_head_rows, log_total, mixed_gradient, mixed_heads, 0, seg_ids)
        grad_q_rows = rounded_values(invert_rotary(grad_queries.reshape(SEQUENCE_TOKENS, QUERY_HEADS, HEAD_DIM), cosine_lookup, sine_lookup)).reshape(SEQUENCE_TOKENS, QUERY_HEADS * HEAD_DIM)
        grad_key_rows = rounded_values(invert_rotary(key_gradient, cosine_lookup, sine_lookup)).reshape(SEQUENCE_TOKENS, KEY_VALUE_HEADS * HEAD_DIM)
        grad_value_rows = rounded_values(value_gradient).reshape(SEQUENCE_TOKENS, KEY_VALUE_HEADS * HEAD_DIM)
        grad_q_w = jnp.einsum('sd,sa->da', expand_heads(hidden_first), expand_heads(grad_q_rows))
        grad_k_w = jnp.einsum('sd,sa->da', expand_heads(hidden_first), expand_heads(grad_key_rows))
        grad_v_w = jnp.einsum('sd,sa->da', expand_heads(hidden_first), expand_heads(grad_value_rows))
        grad_h_one = jnp.einsum('sa,da->sd', expand_heads(grad_q_rows), expand_heads(query_weight)) + jnp.einsum('sa,da->sd', expand_heads(grad_key_rows), expand_heads(key_matrix)) + jnp.einsum('sa,da->sd', expand_heads(grad_value_rows), expand_heads(value_matrix))
        grad_x_part, grad_attn_gain = norm_backward(x_in, scale_one, norm_attn_gain, grad_h_one)
        grad_seq = grad_resid + grad_x_part
        updates = (grad_attn_gain, grad_ffn_gain, grad_q_w, grad_k_w, grad_v_w, grad_mix_w, lax.optimization_barrier(jnp.sum(grad_gate, axis=0)), lax.optimization_barrier(jnp.sum(grad_up, axis=0)), lax.optimization_barrier(jnp.sum(grad_down, axis=0)))
        running = tuple((total + piece for total, piece in zip(running, updates)))
        return (running, (seq_out, grad_seq))
    start_offset = (jnp.zeros((MODEL_DIM,), jnp.float32), jnp.zeros((MODEL_DIM,), jnp.float32), jnp.zeros((MODEL_DIM, QUERY_HEADS * HEAD_DIM), jnp.float32), jnp.zeros((MODEL_DIM, KEY_VALUE_HEADS * HEAD_DIM), jnp.float32), jnp.zeros((MODEL_DIM, KEY_VALUE_HEADS * HEAD_DIM), jnp.float32), jnp.zeros((QUERY_HEADS * HEAD_DIM, MODEL_DIM), jnp.float32), jnp.zeros((EXPERT_WINDOW, MODEL_DIM, EXPERT_HIDDEN), jnp.float32), jnp.zeros((EXPERT_WINDOW, MODEL_DIM, EXPERT_HIDDEN), jnp.float32), jnp.zeros((EXPERT_WINDOW, EXPERT_HIDDEN, MODEL_DIM), jnp.float32))
    totals, (outs_seq, grads_seq) = lax.scan(one_sequence, start_offset, (seq_acts, segments, seq_routes, seq_weights, seq_grads))
    return (outs_seq.reshape(TOKENS, MODEL_DIM), grads_seq.reshape(TOKENS, MODEL_DIM), totals[0], totals[1], totals[2], totals[3], totals[4], totals[5], totals[6], totals[7], totals[8])
```

```python
import jax
import jax.numpy as jnp
from jax import lax
from jax.sharding import PartitionSpec as P

HEAD_DIM = 64
EPS = 1e-05
ATTN_SCALE = 0.015625
THETA = 10000.0
NEG_FILL = -1e30
F32 = jnp.float32
BF16 = jnp.bfloat16


def swap(values):
    return lax.ppermute(values, "tensor", [(0, 1), (1, 0)])


def norm_forward(values, gain_vector):
    inv_scale = lax.rsqrt(jnp.mean(values * values, axis=-1, keepdims=True) + EPS)
    return (values * inv_scale * gain_vector, inv_scale)


def norm_backward(values, inv_scale, gain_vector, upstream):
    weighted = upstream * gain_vector
    inner = jnp.mean(weighted * values, axis=-1, keepdims=True)
    value_gradient = inv_scale * weighted - values * (inv_scale * inv_scale * inv_scale) * inner
    grad_gain = jnp.sum(upstream * values * inv_scale, axis=0)
    return (value_gradient, grad_gain)


def rope_tables(position):
    frequency = THETA ** (-jnp.arange(HEAD_DIM // 2, dtype=F32) * 2.0 / HEAD_DIM)
    angle_table = position.astype(F32)[:, None] * frequency[None, :]
    return (jnp.cos(angle_table)[:, None, :], jnp.sin(angle_table)[:, None, :])


def rotate(field_in, cosine, sine):
    first, second = jnp.split(field_in, 2, axis=-1)
    return jnp.concatenate([first * cosine - second * sine, second * cosine + first * sine], axis=-1)


def dot(spec, left, right):
    return jnp.einsum(spec, left, right, preferred_element_type=F32)


def body(
    activations,
    segments,
    routes,
    route_weights,
    norm_attn_gain,
    norm_ffn_gain,
    query_weight,
    key_matrix,
    value_matrix,
    output_projection_weight,
    expert_gate,
    expert_up,
    expert_down,
    grad_output,
):
    tensor_rank = lax.axis_index("tensor")
    rows, width = activations.shape
    experts_here = expert_gate.shape[0]
    expert_count = experts_here * lax.axis_size("expert")
    length = segments.shape[1]
    heads_q = query_weight.shape[1] // HEAD_DIM
    heads_kv = key_matrix.shape[1] // HEAD_DIM
    group = heads_q // heads_kv

    position = (jnp.arange(length, dtype=jnp.int32) + tensor_rank * rows) % length
    seg_ids = jnp.where(tensor_rank == 0, segments[0], jnp.roll(segments[0], rows))
    cosine, sine = rope_tables(position)
    allowed = (position[None, :] <= position[:, None]) & (seg_ids[None, :] == seg_ids[:, None])

    gate = jnp.concatenate([expert_gate, swap(expert_gate)], axis=2)
    up = jnp.concatenate([expert_up, swap(expert_up)], axis=2)
    down = jnp.concatenate([expert_down, swap(expert_down)], axis=1)
    upstream_all = lax.all_gather(grad_output, "expert", axis=0, tiled=True)
    named = routes[:, :, None] == jnp.arange(expert_count, dtype=jnp.int32)
    weight_table = jnp.sum(jnp.where(named, route_weights[:, :, None], 0.0), axis=1)
    weights_all = lax.all_gather(weight_table, "expert", axis=0, tiled=True)
    first_expert = lax.axis_index("expert") * experts_here
    weights_here = lax.dynamic_slice_in_dim(weights_all, first_expert, experts_here, 1).T

    x_in = jnp.concatenate([activations, swap(activations)], axis=0).astype(F32)
    normed_one, scale_one = norm_forward(x_in, norm_attn_gain)
    hidden_first = normed_one.astype(BF16)
    queries = dot("td,da->ta", hidden_first, query_weight).reshape(length, heads_q, HEAD_DIM)
    queries = rotate(queries, cosine, sine).astype(BF16).reshape(length, heads_kv, group, HEAD_DIM)
    keys = dot("td,da->ta", hidden_first, key_matrix).reshape(length, heads_kv, HEAD_DIM)
    keys = rotate(keys, cosine, sine).astype(BF16)
    value_rows = dot("td,da->ta", hidden_first, value_matrix).astype(BF16)
    value_rows = value_rows.reshape(length, heads_kv, HEAD_DIM)
    scores = jnp.where(allowed, dot("qhgd,khd->hgqk", queries, keys) * ATTN_SCALE, NEG_FILL)
    top_score = jnp.max(scores, axis=-1, keepdims=True)
    log_total = top_score + jnp.log(jnp.sum(jnp.exp(scores - top_score), axis=-1, keepdims=True))
    mixed = dot("hgqk,khd->qhgd", jnp.exp(scores - log_total).astype(BF16), value_rows).astype(BF16)
    mixed_flat = mixed.reshape(length, heads_q * HEAD_DIM)
    attn_part = dot("ta,ad->td", mixed_flat, output_projection_weight)
    residual = x_in[:rows] + attn_part[:rows] + swap(attn_part[rows:])
    normed_two, scale_two = norm_forward(residual, norm_ffn_gain)
    tokens_in = lax.all_gather(normed_two.astype(BF16), "expert", axis=0, tiled=True)

    pre_gate = dot("td,edf->etf", tokens_in, gate)
    pre_up = dot("td,edf->etf", tokens_in, up)
    gate_sigmoid = jax.nn.sigmoid(pre_gate)
    activated = (pre_gate * gate_sigmoid * pre_up).astype(BF16)
    expert_out = dot("etf,efd->etd", activated, down).astype(BF16)
    mix_part = jnp.sum(weights_here[:, :, None] * expert_out.astype(F32), axis=0).astype(BF16)
    grad_rows = (weights_here[:, :, None] * upstream_all.astype(F32)[None]).astype(BF16)
    grad_act = dot("etd,efd->etf", grad_rows, down)
    grad_pre_gate = (
        grad_act * pre_up * gate_sigmoid * (1.0 + pre_gate * (1.0 - gate_sigmoid))
    ).astype(BF16)
    grad_pre_up = (grad_act * pre_gate * gate_sigmoid).astype(BF16)
    grad_in = dot("etf,edf->etd", grad_pre_gate, gate) + dot("etf,edf->etd", grad_pre_up, up)
    grad_part = jnp.sum(weights_here[:, :, None] * grad_in, axis=0).astype(BF16)
    grad_h_own = lax.psum_scatter(grad_part, "expert", scatter_dimension=0, tiled=True)
    expert_mix = lax.psum_scatter(mix_part, "expert", scatter_dimension=0, tiled=True)
    block_out = (residual + expert_mix.astype(F32)).astype(BF16)

    def expert_sum(whole, axis):
        own, other = jnp.split(whole, 2, axis=axis)
        half = own + swap(other.astype(BF16)).astype(F32)
        return lax.psum(half.astype(BF16), "dp").astype(F32)

    gate_sum = expert_sum(dot("td,etf->edf", tokens_in, grad_pre_gate), 2)
    up_sum = expert_sum(dot("td,etf->edf", tokens_in, grad_pre_up), 2)
    down_sum = expert_sum(dot("etf,etd->efd", activated, grad_rows), 1)

    upstream_own = grad_output.astype(F32)
    grad_norm_part, grad_ffn_gain = norm_backward(
        residual, scale_two, norm_ffn_gain, grad_h_own.astype(F32)
    )
    grad_resid = upstream_own + grad_norm_part
    resid_own = grad_resid.astype(BF16)
    resid_full = jnp.concatenate([resid_own, swap(resid_own)], axis=0)
    grad_mix_w = dot("sa,sb->ab", mixed_flat, resid_full)
    mixed_grad = dot("im,dm->id", resid_full, output_projection_weight).astype(BF16)
    mixed_grad = mixed_grad.reshape(length, heads_kv, group, HEAD_DIM)
    probs = jnp.exp(scores - log_total)
    row_delta = dot("qhgd,qhgd->hgq", mixed_grad, mixed)
    grad_soft = dot("qhgd,khd->hgqk", mixed_grad, value_rows)
    grad_scores = (probs * (grad_soft - row_delta[..., None]) * ATTN_SCALE).astype(BF16)
    grad_queries = dot("hgqk,khd->qhgd", grad_scores, keys)
    grad_keys = dot("hgqk,qhgd->khd", grad_scores, queries)
    grad_values = dot("hgqk,qhgd->khd", probs.astype(BF16), mixed_grad)
    grad_q_rows = rotate(grad_queries.reshape(length, heads_q, HEAD_DIM), cosine, -sine)
    grad_q_rows = grad_q_rows.astype(BF16).reshape(length, -1)
    grad_k_rows = rotate(grad_keys, cosine, -sine).astype(BF16).reshape(length, -1)
    grad_v_rows = grad_values.astype(BF16).reshape(length, -1)
    grad_q_w = dot("sd,sa->da", hidden_first, grad_q_rows)
    grad_k_w = dot("sd,sa->da", hidden_first, grad_k_rows)
    grad_v_w = dot("sd,sa->da", hidden_first, grad_v_rows)
    grad_h_part = (
        dot("sa,da->sd", grad_q_rows, query_weight)
        + dot("sa,da->sd", grad_k_rows, key_matrix)
        + dot("sa,da->sd", grad_v_rows, value_matrix)
    )
    grad_h_one = grad_h_part[:rows] + swap(grad_h_part[rows:])
    grad_x_part, grad_attn_gain = norm_backward(
        x_in[:rows], scale_one[:rows], norm_attn_gain, grad_h_one
    )
    grad_input = grad_resid + grad_x_part
    dense = [t.astype(BF16) for t in (grad_q_w, grad_k_w, grad_v_w, grad_mix_w)]
    dense = [t.astype(F32) for t in lax.psum(dense, ("dp", "expert"))]
    gains = lax.psum(jnp.stack([grad_attn_gain, grad_ffn_gain]), ("dp", "expert", "tensor"))
    return (
        block_out,
        grad_input,
        gains[0],
        gains[1],
        *dense,
        gate_sum,
        up_sum,
        down_sum,
    )


def solution(mesh):
    tokens = P(("dp", "expert", "tensor"), None)
    whole = P()
    columns = P(None, "tensor")
    hidden_last = P("expert", None, "tensor")
    hidden_mid = P("expert", "tensor", None)
    mixer = P("tensor", None)
    return jax.shard_map(
        body,
        mesh=mesh,
        in_specs=(
            tokens,
            P(("dp", "expert"), None),
            tokens,
            tokens,
            whole,
            whole,
            columns,
            columns,
            columns,
            mixer,
            hidden_last,
            hidden_last,
            hidden_mid,
            tokens,
        ),
        out_specs=(
            tokens,
            tokens,
            whole,
            whole,
            columns,
            columns,
            columns,
            mixer,
            hidden_last,
            hidden_last,
            hidden_mid,
        ),
        check_vma=False,
    )
```

```python
import functools

import jax
import jax.numpy as jnp
import numpy as np
from jax import lax
from jax.experimental import pallas as pl
from jax.experimental.pallas import tpu as pltpu
from jax.sharding import PartitionSpec as P

HEAD_DIM = 64
EPS = 1e-05
ATTN_SCALE = 0.015625
THETA = 10000.0
NEG_FILL = -1e30
F32 = jnp.float32
BF16 = jnp.bfloat16
NO_COST = pl.CostEstimate(flops=1, bytes_accessed=1, transcendentals=0)


def after(values, token):
    return lax.optimization_barrier((values, token))[0]


def swap(values):
    return lax.ppermute(values, "tensor", [(0, 1), (1, 0)])


def shift_dp(values, step):
    count = lax.axis_size("dp")
    return lax.ppermute(values, "dp", [(i, (i + step) % count) for i in range(count)])


def grid_sizes():
    count = lax.axis_size("expert")
    outer = 4 if count % 4 == 0 else count
    return outer, count // outer


def shift_outer(values):
    outer, inner = grid_sizes()
    pairs = [(((o + 1) % outer) * inner + i, o * inner + i) for o in range(outer) for i in range(inner)]
    return lax.ppermute(values, "expert", pairs)


def shift_inner(values):
    outer, inner = grid_sizes()
    pairs = [(o * inner + (i + 1) % inner, o * inner + i) for o in range(outer) for i in range(inner)]
    return lax.ppermute(values, "expert", pairs)


def inner_line(block):
    line = [block]
    for _ in range(1, grid_sizes()[1]):
        line.append(shift_inner(line[-1]))
    return line


def inner_sum(parts):
    inner, total = len(parts), parts[1 % len(parts)]
    for j in range(2, inner + 1):
        total = shift_inner(total.astype(BF16)).astype(F32) + parts[j % inner].astype(F32)
    return total


def together(*values):
    return lax.optimization_barrier(values)


def sum_all(values):
    for axis in ("tensor", "expert", "dp"):
        count, bit = lax.axis_size(axis), 1
        while bit < count:
            values = values + lax.ppermute(values, axis, [(i, i ^ bit) for i in range(count)])
            bit *= 2
    return values


def norm_forward(values, gain_vector):
    inv_scale = lax.rsqrt(jnp.mean(values * values, axis=-1, keepdims=True) + EPS)
    return (values * inv_scale * gain_vector, inv_scale)


def norm_backward(values, inv_scale, gain_vector, upstream):
    weighted = upstream * gain_vector
    inner = jnp.mean(weighted * values, axis=-1, keepdims=True)
    value_gradient = inv_scale * weighted - values * (inv_scale * inv_scale * inv_scale) * inner
    grad_gain = jnp.sum(upstream * values * inv_scale, axis=0)
    return (value_gradient, grad_gain)


def dot(spec, left, right, kind=F32):
    return jnp.einsum(spec, left, right, preferred_element_type=kind)

def dot_t(left, right):
    return lax.dot_general(left, right, (((1,), (1,)), ((), ())), preferred_element_type=F32)


def full_spec(*shape):
    return pl.BlockSpec(shape, lambda *_: (0,) * len(shape))


def rope_tables(length, width):
    half = HEAD_DIM // 2
    frequency = (THETA ** (-np.arange(half, dtype=np.float32) * 2.0 / HEAD_DIM)).astype(np.float32)
    angle = np.arange(length, dtype=np.float32)[:, None] * frequency[None, :]
    cosine, sine = np.cos(angle.astype(np.float64)), np.sin(angle.astype(np.float64))
    cosine = np.concatenate([cosine, cosine], axis=1)
    sine = np.concatenate([-sine, sine], axis=1)
    copies = width // HEAD_DIM
    return np.tile(cosine, (1, copies)).astype(np.float32), np.tile(sine, (1, copies)).astype(np.float32)


def turn(values, cosine, sine):
    width, half = values.shape[1], HEAD_DIM // 2
    copies = width // cosine.shape[1]
    lane = lax.broadcasted_iota(jnp.int32, values.shape, 1)
    first = lax.rem(lane, HEAD_DIM) < half
    other = jnp.where(first, pltpu.roll(values, width - half, 1), pltpu.roll(values, half, 1))
    return values * jnp.concatenate([cosine] * copies, 1) + other * jnp.concatenate([sine] * copies, 1)


def masked_scores(query, key, allowed):
    return jnp.where(allowed, dot_t(query, key) * ATTN_SCALE, NEG_FILL)


def allowed_pairs(segs):
    length = segs.shape[1]
    row = lax.broadcasted_iota(jnp.int32, (length, length), 0)
    column = lax.broadcasted_iota(jnp.int32, (length, length), 1)
    seg_row = segs.astype(F32)
    seg_column = jnp.sum(jnp.where(row == column, seg_row, 0.0), axis=1, keepdims=True)
    return (column <= row) & (seg_row == seg_column)


def row_places(meta, rows):
    own = pl.ds(pl.multiple_of(meta[0] * rows, rows), rows)
    other = pl.ds(pl.multiple_of((1 - meta[0]) * rows, rows), rows)
    return own, other


def attend_kernel(
    meta, own_ref, other_ref, gain_ref, segs, cos_ref, sin_ref, wq, wk, wv, wo,
    hidden_out, q_out, k_out, v_out, mixed_out, log_out, own_out, other_out, x_s, part_s,
):
    rows = own_ref.shape[0]
    own, other = row_places(meta, rows)
    x_s[own, :] = own_ref[...].astype(F32)
    x_s[other, :] = other_ref[...].astype(F32)
    x = x_s[...]
    scale = lax.rsqrt(jnp.mean(x * x, axis=-1, keepdims=True) + EPS)
    hidden = (x * scale * gain_ref[...]).astype(BF16)
    hidden_out[...] = hidden
    cosine, sine = cos_ref[...], sin_ref[...]
    q_out[...] = turn(jnp.dot(hidden, wq[...], preferred_element_type=F32), cosine, sine).astype(BF16)
    k_out[...] = turn(jnp.dot(hidden, wk[...], preferred_element_type=F32), cosine, sine).astype(BF16)
    v_out[...] = jnp.dot(hidden, wv[...], preferred_element_type=F32).astype(BF16)
    allowed = allowed_pairs(segs[...])
    heads, heads_kv = wq.shape[1] // HEAD_DIM, wk.shape[1] // HEAD_DIM
    group = heads // heads_kv
    for g in range(heads_kv):
        key = k_out[:, g * HEAD_DIM : (g + 1) * HEAD_DIM]
        value = v_out[:, g * HEAD_DIM : (g + 1) * HEAD_DIM]
        for h in range(g * group, (g + 1) * group):
            at = slice(h * HEAD_DIM, (h + 1) * HEAD_DIM)
            scores = masked_scores(q_out[:, at], key, allowed)
            top = jnp.max(scores, axis=-1, keepdims=True)
            log_total = top + jnp.log(jnp.sum(jnp.exp(scores - top), axis=-1, keepdims=True))
            log_out[:, h : h + 1] = log_total
            prob = jnp.exp(scores - log_total).astype(BF16)
            mixed_out[:, at] = jnp.dot(prob, value, preferred_element_type=F32).astype(BF16)
    part_s[...] = jnp.dot(mixed_out[...], wo[...], preferred_element_type=F32)
    own_out[...] = part_s[own, :]
    other_out[...] = part_s[other, :]


def attend(meta, own, other, gain, segs, wq, wk, wv, wo):
    rows, width = own.shape
    length = segs.shape[1]
    cosine, sine = rope_tables(length, 128)
    operands = (own, other, gain[None, :], segs, cosine, sine, wq, wk, wv, wo)
    shapes = [
        ((length, width), BF16),
        ((length, wq.shape[1]), BF16),
        ((length, wk.shape[1]), BF16),
        ((length, wv.shape[1]), BF16),
        ((length, wq.shape[1]), BF16),
        ((length, 128), F32),
        ((rows, width), F32),
        ((rows, width), F32),
    ]
    return pl.pallas_call(
        attend_kernel,
        out_shape=[jax.ShapeDtypeStruct(*shape) for shape in shapes],
        grid_spec=pltpu.PrefetchScalarGridSpec(
            num_scalar_prefetch=1,
            grid=(1,),
            in_specs=[full_spec(*t.shape) for t in operands],
            out_specs=[full_spec(*shape) for shape, _ in shapes],
            scratch_shapes=[pltpu.VMEM((length, width), F32)] * 2,
        ),
        compiler_params=pltpu.CompilerParams(vmem_limit_bytes=56 * 1024 * 1024),
        cost_estimate=NO_COST,
    )(meta, *operands)


def attend_back_kernel(
    shares, meta, b_ref, segs, cos_ref, sin_ref, wq, wk, wv, wo,
    q_ref, k_ref, v_ref, mixed_ref, log_ref, *refs,
):
    share_outs, (own_out, other_out, grad_s, dq_s, part_s) = refs[:shares], refs[shares:]
    own, other = row_places(meta, own_out.shape[0])
    grad_s[...] = dot_t(b_ref[...], wo[...]).astype(BF16)
    cosine, sine = cos_ref[...], -sin_ref[...]
    allowed = allowed_pairs(segs[...])
    wide, narrow = wq.shape[1], wk.shape[1]
    heads, heads_kv = wide // HEAD_DIM, narrow // HEAD_DIM
    group = heads // heads_kv

    def transposed_dot(left, right):
        return lax.dot_general(left, right, (((0,), (0,)), ((), ())), preferred_element_type=F32)

    for g in range(heads_kv):
        there = slice(g * HEAD_DIM, (g + 1) * HEAD_DIM)
        key, value = k_ref[:, there], v_ref[:, there]
        grad_key = grad_value = 0.0
        for h in range(g * group, (g + 1) * group):
            at = slice(h * HEAD_DIM, (h + 1) * HEAD_DIM)
            query, grad = q_ref[:, at], grad_s[:, at]
            prob = jnp.exp(masked_scores(query, key, allowed) - log_ref[:, h : h + 1])
            delta = jnp.sum(grad.astype(F32) * mixed_ref[:, at].astype(F32), axis=-1, keepdims=True)
            grad_scores = (prob * (dot_t(grad, value) - delta) * ATTN_SCALE).astype(BF16)
            dq_s[:, at] = jnp.dot(grad_scores, key, preferred_element_type=F32)
            grad_key = grad_key + transposed_dot(grad_scores, query)
            grad_value = grad_value + transposed_dot(prob.astype(BF16), grad)
        dq_s[:, wide + g * HEAD_DIM : wide + (g + 1) * HEAD_DIM] = grad_key
        at = wide + narrow + g * HEAD_DIM
        dq_s[:, at : at + HEAD_DIM] = grad_value
    dq = turn(dq_s[:, :wide], cosine, sine).astype(BF16)
    dk = turn(dq_s[:, wide : wide + narrow], cosine, sine).astype(BF16)
    dv = dq_s[:, wide + narrow :].astype(BF16)
    part_s[...] = dot_t(dq, wq[...]) + dot_t(dk, wk[...]) + dot_t(dv, wv[...])
    own_out[...] = part_s[own, :]
    other_out[...] = part_s[other, :]
    for r in range(shares):

        @pl.when(meta[1] == r)
        def _():
            for step in range(shares):
                at = 0
                for part in (dq, dk, dv):
                    size = part.shape[1] // shares
                    index = (r + step) % shares
                    share_outs[step][:, at : at + size] = part[:, index * size : (index + 1) * size]
                    at += size


def attend_back(meta, shares, resid, segs, wq, wk, wv, wo, q, k, v, mixed, log_total):
    length, width = resid.shape
    cosine, sine = rope_tables(length, 128)
    operands = (resid, segs, cosine, sine, wq, wk, wv, wo, q, k, v, mixed, log_total)
    columns = wq.shape[1] + wk.shape[1] + wv.shape[1]
    shapes = [((length, columns // shares), BF16)] * shares
    shapes += [((length // 2, width), F32)] * 2
    return pl.pallas_call(
        functools.partial(attend_back_kernel, shares),
        out_shape=[jax.ShapeDtypeStruct(*shape) for shape in shapes],
        grid_spec=pltpu.PrefetchScalarGridSpec(
            num_scalar_prefetch=1,
            grid=(1,),
            in_specs=[full_spec(*t.shape) for t in operands],
            out_specs=[full_spec(*shape) for shape, _ in shapes],
            scratch_shapes=[
                pltpu.VMEM((length, wq.shape[1]), BF16),
                pltpu.VMEM((length, columns), F32),
                pltpu.VMEM((length, width), F32),
            ],
        ),
        compiler_params=pltpu.CompilerParams(vmem_limit_bytes=56 * 1024 * 1024),
        cost_estimate=NO_COST,
    )(meta, *operands)


def expert_kernel(inner, aliased, experts, meta, *refs):
    blocks, payloads, refs = refs[:inner], refs[inner : 2 * inner], refs[2 * inner :]
    weight_refs, refs = refs[:6], refs[6 + aliased :]
    tokens_out, upstream_out, mix_out = refs[:3]
    used_out, gate_out, up_out = refs[3:5], refs[5:7], refs[7:9]
    in_out = refs[9 : 9 + inner]
    table, mix_total, in_total = refs[9 + inner :]
    rows, width = blocks[0].shape
    expert = pl.program_id(0)

    def place(j):
        return pl.ds(pl.multiple_of(lax.rem(meta[1] + j, inner) * rows, rows), rows)

    @pl.when(expert == 0)
    def _():
        for j in range(inner):
            tokens_out[place(j), :] = blocks[j][...]
            upstream_out[place(j), :] = payloads[j][:, :width]
            table[place(j), :] = payloads[j][:, width:].astype(F32)
        mix_total[...] = jnp.zeros_like(mix_total)
        in_total[...] = jnp.zeros_like(in_total)

    lane = lax.broadcasted_iota(jnp.int32, table.shape, 1)
    wanted = (lax.rem(lane, experts) == meta[2] + expert) & (lane < 3 * experts)
    weight = jnp.sum(jnp.where(wanted, table[...], 0.0), axis=1, keepdims=True)
    for half in range(2):
        gate, up, down = (weight_refs[2 * i + half][0] for i in range(3))
        pre_gate = jnp.dot(tokens_out[...], gate, preferred_element_type=F32)
        pre_up = jnp.dot(tokens_out[...], up, preferred_element_type=F32)
        grad_act = dot_t(upstream_out[...], down) * weight
        gate_sigmoid = 1.0 / (1.0 + jnp.exp(-pre_gate))
        silu = pre_gate * gate_sigmoid
        used = (silu * pre_up * weight).astype(BF16)
        grad_gate = grad_act * pre_up * gate_sigmoid * (1.0 + pre_gate * (1.0 - gate_sigmoid))
        grad_up = grad_act * silu
        used_out[half][0] = used
        gate_out[half][0] = grad_gate.astype(BF16)
        up_out[half][0] = grad_up.astype(BF16)
        mix_total[...] += jnp.dot(used, down, preferred_element_type=F32)
        in_total[...] += dot_t((grad_gate * weight).astype(BF16), gate) + dot_t(
            (grad_up * weight).astype(BF16), up
        )

    @pl.when(expert == pl.num_programs(0) - 1)
    def _():
        mix_out[...] = mix_total[...].astype(BF16)
        for j in range(inner):
            in_out[j][...] = in_total[place(j), :].astype(BF16)


def run_experts(meta, blocks, payloads, expert_weights, buffers, total, expert_count):
    inner = len(blocks)
    rows, width = blocks[0].shape
    experts, half = expert_weights[0].shape[0], expert_weights[0].shape[2]
    chunk = inner * rows
    extra = payloads[0].shape[1] - width
    by_chunk = pl.BlockSpec((chunk, width), lambda e, m: (m[0], 0))
    per_expert = pl.BlockSpec((1, chunk, half), lambda e, m: (e, m[0], 0))
    spread = pl.BlockSpec((1, width, half), lambda e, m: (e, 0, 0))
    tall = pl.BlockSpec((1, half, width), lambda e, m: (e, 0, 0))
    shapes = [jax.ShapeDtypeStruct((total, width), BF16)] * 3
    shapes += [jax.ShapeDtypeStruct((experts, total, half), BF16)] * 6
    first = 1 + 2 * inner + 6
    return pl.pallas_call(
        functools.partial(expert_kernel, inner, len(buffers), expert_count),
        out_shape=shapes + [jax.ShapeDtypeStruct((rows, width), BF16)] * inner,
        grid_spec=pltpu.PrefetchScalarGridSpec(
            num_scalar_prefetch=1,
            grid=(experts,),
            in_specs=[full_spec(rows, width)] * inner
            + [full_spec(rows, width + extra)] * inner
            + [spread] * 4
            + [tall] * 2
            + [pl.BlockSpec(memory_space=pl.ANY)] * len(buffers),
            out_specs=[by_chunk] * 3 + [per_expert] * 6 + [full_spec(rows, width)] * inner,
            scratch_shapes=[
                pltpu.VMEM((chunk, extra), F32),
                pltpu.VMEM((chunk, width), F32),
                pltpu.VMEM((chunk, width), F32),
            ],
        ),
        input_output_aliases={first + i: i for i in range(len(buffers))},
        compiler_params=pltpu.CompilerParams(vmem_limit_bytes=56 * 1024 * 1024),
        cost_estimate=NO_COST,
    )(meta, *blocks, *payloads, *expert_weights, *buffers)


def place_kernel(sizes, aliased, meta, block_ref, *refs):
    at = 0
    for size, out in zip(sizes, refs[aliased:]):
        out[...] = block_ref[0, :, at : at + size].astype(F32)
        at += size


def place_line(meta, pieces, sizes, shapes, buffers):
    count, rows, width = pieces.shape
    low = [pl.BlockSpec((rows, size), lambda i, m: (m[4 * i], m[4 * i + 1])) for size in sizes[:-1]]
    low.append(pl.BlockSpec((rows, sizes[-1]), lambda i, m: (m[4 * i + 2], m[4 * i + 3])))
    return pl.pallas_call(
        functools.partial(place_kernel, sizes, len(buffers)),
        out_shape=[jax.ShapeDtypeStruct(shape, F32) for shape in shapes],
        grid_spec=pltpu.PrefetchScalarGridSpec(
            num_scalar_prefetch=1,
            grid=(count,),
            in_specs=[pl.BlockSpec((1, rows, width), lambda i, m: (i, 0, 0))]
            + [pl.BlockSpec(memory_space=pl.ANY)] * len(buffers),
            out_specs=low,
        ),
        input_output_aliases={2 + i: i for i in range(len(buffers))},
        cost_estimate=NO_COST,
    )(meta, pieces, *buffers)


def body(
    activations,
    segments,
    routes,
    route_weights,
    norm_attn_gain,
    norm_ffn_gain,
    query_weight,
    key_matrix,
    value_matrix,
    output_projection_weight,
    expert_gate,
    expert_up,
    expert_down,
    grad_output,
):
    tensor_rank = lax.axis_index("tensor")
    dp_rank = lax.axis_index("dp")
    dp_count = lax.axis_size("dp")
    outer, inner = grid_sizes()
    outer_rank = lax.axis_index("expert") // inner
    inner_rank = lax.axis_index("expert") % inner
    rows, width = activations.shape
    experts_here = expert_gate.shape[0]
    expert_count = experts_here * lax.axis_size("expert")

    named = routes[:, :, None] == jnp.arange(expert_count, dtype=jnp.int32)
    weight_table = jnp.sum(jnp.where(named, route_weights[:, :, None], 0.0), axis=1)
    high = lax.reduce_precision(weight_table, 8, 7)
    middle = lax.reduce_precision(weight_table - high, 8, 7)
    low = weight_table - high - middle
    table = jnp.concatenate([high, middle, low], axis=1).astype(BF16)
    table = jnp.pad(table, ((0, 0), (0, -table.shape[1] % 128)))
    payload = jnp.concatenate([grad_output, table], axis=1)
    up_line, up_next = together(inner_line(payload), shift_outer(payload))
    heads_meta = jnp.stack([tensor_rank, dp_rank]).astype(jnp.int32)
    attn_weights = (query_weight, key_matrix, value_matrix, output_projection_weight)
    hidden, q, k, v, mixed, log_total, attn_own, attn_other = attend(
        heads_meta, activations, swap(activations), norm_attn_gain, segments, *attn_weights
    )
    x_own = activations.astype(F32)
    attn_own, attn_other, up_line, up_next = together(attn_own, attn_other, up_line, up_next)
    residual = x_own + attn_own + swap(attn_other)
    normed_two, scale_two = norm_forward(residual, norm_ffn_gain)

    expert_weights = []
    for weights_own in (expert_gate, expert_up, expert_down):
        expert_weights += [weights_own, swap(weights_own)]
    first_expert = lax.axis_index("expert") * experts_here

    upstream, tokens = {0: up_line}, {}
    next_up, next_tokens = up_next, normed_two.astype(BF16)
    buffers, in_parts, lines, running = [], {}, {}, None
    peers = halves = None
    for turn_index in range(1, outer + 4):
        step = {}
        if turn_index < outer:
            step["up_line"] = inner_line(next_up)
            if turn_index + 1 < outer:
                step["up_next"] = shift_outer(next_up)
        if turn_index - 1 < outer:
            step["line"] = inner_line(next_tokens)
            if turn_index < outer:
                step["next"] = shift_outer(next_tokens)
        summed = [turn_index - 3] if 1 <= turn_index - 3 < outer else []
        summed += [0] if turn_index == outer + 1 else []
        if summed:
            step["sums"] = {i: inner_sum(in_parts[i]) for i in summed}
        at = turn_index - 4
        if 1 <= at < outer:
            held = lines[at] if running is None else running.astype(F32) + lines[at].astype(F32)
            step["running"] = shift_outer(held.astype(BF16))
        chunk = turn_index - 2
        if 0 <= chunk < outer:
            meta = [(outer_rank + chunk) % outer, inner_rank, first_expert]
            step["made"] = run_experts(
                jnp.stack(meta).astype(jnp.int32), tokens[chunk], upstream[chunk],
                expert_weights, buffers, outer * inner * rows, expert_count,
            )
        if chunk == outer:
            tokens_all, upstream_all, mix_all, *pairs = buffers
            jobs = [
                ("etf,td->edf", pairs[2:4], tokens_all),
                ("etf,td->edf", pairs[4:6], tokens_all),
                ("etf,td->efd", pairs[0:2], upstream_all),
            ]
            step["peers"] = [dot(spec, pair[1], side, BF16) for spec, pair, side in jobs]
        if chunk == outer + 1:
            step["halves"] = [
                (dot(spec, pair[0], side) + swap(other).astype(F32)).astype(BF16)
                for (spec, pair, side), other in zip(jobs, peers)
            ]
        (step,) = together(step)
        if "up_line" in step:
            upstream[turn_index] = step["up_line"]
        next_up = step.get("up_next")
        if "line" in step:
            tokens[turn_index - 1] = step["line"]
        next_tokens = step.get("next")
        lines.update(step.get("sums", {}))
        running = step.get("running", running)
        if "made" in step:
            buffers, in_parts[chunk] = list(step["made"][:9]), step["made"][9:]
        peers = step.get("peers", peers)
        halves = step.get("halves", halves)
    grad_h_own = running.astype(F32) + lines[0].astype(F32)

    def sum_dp(half):
        bit, found = 1, []
        while bit < dp_count:
            found.append(lax.ppermute(half, "dp", [(i, i ^ bit) for i in range(dp_count)]))
            bit *= 2
            if bit < dp_count:
                half = (half.astype(F32) + found.pop().astype(F32)).astype(BF16)
        return half, *found

    def total(pair):
        return sum(t.astype(F32) for t in pair)

    grad_norm_part, grad_ffn_gain = norm_backward(residual, scale_two, norm_ffn_gain, grad_h_own)
    grad_resid = grad_output.astype(F32) + grad_norm_part
    resid_own = grad_resid.astype(BF16)
    resid_other = swap(resid_own)
    resid_full = jnp.where(
        tensor_rank == 0,
        jnp.concatenate([resid_own, resid_other], axis=0),
        jnp.concatenate([resid_other, resid_own], axis=0),
    )
    expert_mix = lax.psum_scatter(
        after(mix_all, resid_full), "expert", scatter_dimension=0, tiled=True
    )
    *shares, dh_own, dh_other = attend_back(
        heads_meta, dp_count, resid_full, segments, *attn_weights, q, k, v, mixed, log_total,
    )

    hidden_all, mixed_all = [hidden], [mixed]
    for step in range(1, dp_count):
        other = shift_dp(activations, step)
        other = jnp.concatenate([other, swap(other)], axis=0)
        other = jnp.where(tensor_rank == 0, other, jnp.roll(other, rows, 0)).astype(F32)
        hidden_all.append(norm_forward(other, norm_attn_gain)[0].astype(BF16))
        mixed_all.append(shift_dp(mixed, step))
    length, share_width = resid_full.shape[0], width // dp_count

    def columns(index):
        return lax.dynamic_slice_in_dim(resid_full, index * share_width, share_width, 1)

    resid_shares = [columns(dp_rank)]
    for step in range(1, dp_count):
        resid_shares.append(shift_dp(columns((dp_rank + step) % dp_count), step))
    shares, resid_shares = together(shares, resid_shares)
    all_shares = [shares[0]] + [shift_dp(shares[step], step) for step in range(1, dp_count)]
    gate_pair = sum_dp(after(halves[0], all_shares))
    qkv_part = dot("sd,sa->da", jnp.concatenate(hidden_all, 0), jnp.concatenate(all_shares, 0), BF16)
    parts = width // mixed.shape[1]
    mix_part = dot(
        "sa,shb->hab",
        jnp.concatenate(mixed_all, 0),
        jnp.concatenate(resid_shares, 0).reshape(length * dp_count, parts, share_width // parts),
        BF16,
    )
    dense_part = jnp.concatenate([qkv_part, mix_part.reshape(width, -1)], axis=1)
    block = width // (outer * inner)

    def row_terms(part, step):
        start = (outer_rank + step) % outer * inner
        return [
            lax.dynamic_slice_in_dim(part, (start + (inner_rank + j) % inner) * block, block, 0)
            for j in range(inner)
        ]

    held, running = {}, None
    for turn_index in range(outer):
        step = {"line": inner_sum(row_terms(dense_part, (turn_index + 1) % outer))}
        if turn_index:
            value = held[turn_index]
            value = value if running is None else running.astype(F32) + value.astype(F32)
            step["running"] = shift_outer(value.astype(BF16))
        if turn_index == outer - 1:
            step["gate"] = gate_pair
        step, dense_part = together(step, dense_part)
        held[(turn_index + 1) % outer] = step["line"]
        running = step.get("running")
        gate_pair = step.get("gate", gate_pair)
    reduced = (running.astype(F32) + held[0].astype(F32)).astype(BF16)
    sizes = [t.shape[1] // dp_count for t in (query_weight, key_matrix, value_matrix)]
    sizes.append(share_width // parts)
    shapes = [t.shape for t in (query_weight, key_matrix, value_matrix)] + [(width // parts, width)]
    expert_mix, residual = after((expert_mix, residual), reduced)
    block_out = (residual + expert_mix.astype(F32)).astype(BF16)
    grad_h_one = dh_own + swap(dh_other)
    scale_one = lax.rsqrt(jnp.mean(x_own * x_own, axis=-1, keepdims=True) + EPS)
    grad_x_part, grad_attn_gain = norm_backward(x_own, scale_one, norm_attn_gain, grad_h_one)
    grad_input = grad_resid + grad_x_part
    gains = sum_all(jnp.stack([grad_attn_gain, grad_ffn_gain]))
    if all(size % 128 == 0 for size in sizes):
        pieces = [reduced] + [shift_dp(reduced, step) for step in range(1, dp_count)]
        (pieces,) = together(pieces)
        up_pair = sum_dp(after(halves[1], pieces))
        dense, turn_next, lines = [], jnp.stack(pieces), {}
        for turn_index in range(outer + 1):
            step = {"line": inner_line(turn_next)} if turn_next is not None else {}
            if turn_index + 1 < outer:
                step["next"] = shift_outer(turn_next)
            if turn_index:
                made = dense
                for j in range(inner):
                    index = (outer_rank + turn_index - 1) % outer * inner + (inner_rank + j) % inner
                    meta = []
                    for turn in range(dp_count):
                        share = (dp_rank - turn) % dp_count
                        per = outer * inner // parts
                        meta += [index, share, index % per, share * parts + index // per]
                    made = place_line(
                        jnp.stack(meta).astype(jnp.int32), lines[turn_index - 1][j], sizes, shapes, made
                    )
                step["made"] = made
            if turn_index == 2:
                step["up"] = up_pair
            if turn_index == outer:
                step["finished"] = (block_out, grad_input, gains)
            (step,) = together(step)
            if turn_index == 2:
                up_pair = step["up"]
                down_pair = sum_dp(after(halves[2], up_pair))
            lines[turn_index] = step.get("line")
            turn_next, dense = step.get("next"), step.get("made", [])
            block_out, grad_input, gains = step.get("finished", (block_out, grad_input, gains))
        gate_sum, up_sum = total(gate_pair), total(up_pair)
        down_sum = total(down_pair)
    else:
        up_pair, down_pair = (sum_dp(half) for half in halves[1:])
        gate_sum, up_sum, down_sum = (total(pair) for pair in (gate_pair, up_pair, down_pair))
        gathered = lax.all_gather(reduced, ("dp", "expert"), axis=0, tiled=True)
        gathered = gathered.reshape(dp_count, width, -1).astype(F32)
        starts = [sum(sizes[:i]) for i in range(len(sizes))]
        dense = [gathered[:, :, at : at + size] for at, size in zip(starts, sizes)]
        dense[:-1] = [t.transpose(1, 0, 2).reshape(width, -1) for t in dense[:-1]]
        mix_w = dense[-1].reshape(dp_count, parts, width // parts, -1)
        dense[-1] = mix_w.transpose(2, 0, 1, 3).reshape(width // parts, width)
    return (
        block_out,
        grad_input,
        gains[0],
        gains[1],
        *dense,
        gate_sum,
        up_sum,
        down_sum,
    )


def solution(mesh):
    tokens = P(("dp", "expert", "tensor"), None)
    whole = P()
    columns = P(None, "tensor")
    hidden_last = P("expert", None, "tensor")
    hidden_mid = P("expert", "tensor", None)
    mixer = P("tensor", None)
    return jax.shard_map(
        body,
        mesh=mesh,
        in_specs=(
            tokens,
            P(("dp", "expert"), None),
            tokens,
            tokens,
            whole,
            whole,
            columns,
            columns,
            columns,
            mixer,
            hidden_last,
            hidden_last,
            hidden_mid,
            tokens,
        ),
        out_specs=(
            tokens,
            tokens,
            whole,
            whole,
            columns,
            columns,
            columns,
            mixer,
            hidden_last,
            hidden_last,
            hidden_mid,
        ),
        check_vma=False,
    )
```

```python
import functools

import jax
import jax.numpy as jnp
import numpy as np
from jax import lax
from jax.experimental import pallas as pl
from jax.experimental.pallas import tpu as pltpu
from jax.sharding import PartitionSpec as P

HEAD_DIM = 64
EPS = 1e-05
ATTN_SCALE = 0.015625
THETA = 10000.0
NEG_FILL = -1e30
F32 = jnp.float32
BF16 = jnp.bfloat16
NO_COST = pl.CostEstimate(flops=1, bytes_accessed=1, transcendentals=0)


def after(values, token):
    return lax.optimization_barrier((values, token))[0]


def swap(values):
    return lax.ppermute(values, "tensor", [(0, 1), (1, 0)])


def shift_dp(values, step):
    count = lax.axis_size("dp")
    return lax.ppermute(values, "dp", [(i, (i + step) % count) for i in range(count)])


def grid_sizes():
    count = lax.axis_size("expert")
    return 4, count // 4


def shift_outer(values, step=1):
    outer, inner = grid_sizes()
    pairs = [(((o + step) % outer) * inner + i, o * inner + i) for o in range(outer) for i in range(inner)]
    return lax.ppermute(values, "expert", pairs)


def shift_inner(values):
    outer, inner = grid_sizes()
    pairs = [(o * inner + (i + 1) % inner, o * inner + i) for o in range(outer) for i in range(inner)]
    return lax.ppermute(values, "expert", pairs)


def inner_line(block):
    line = [block]
    for _ in range(1, grid_sizes()[1]):
        line.append(shift_inner(line[-1]))
    return line


def inner_sum(parts):
    inner, total = len(parts), parts[1 % len(parts)]
    for j in range(2, inner + 1):
        total = shift_inner(total.astype(BF16)).astype(F32) + parts[j % inner].astype(F32)
    return total


def together(*values):
    return lax.optimization_barrier(values)


def hops_of_all():
    bits = {}
    for axis in ("tensor", "expert", "dp"):
        count = lax.axis_size(axis)
        bits[axis] = [(axis, 1 << i) for i in range(count.bit_length() - 1)]
    return bits["tensor"] + bits["dp"] + bits["expert"]


def exchange(values, hop):
    axis, bit = hop
    return lax.ppermute(values, axis, [(i, i ^ bit) for i in range(lax.axis_size(axis))])


def norm_forward(values, gain_vector):
    inv_scale = lax.rsqrt(jnp.mean(values * values, axis=-1, keepdims=True) + EPS)
    return (values * inv_scale * gain_vector, inv_scale)


def norm_backward(values, inv_scale, gain_vector, upstream):
    weighted = upstream * gain_vector
    inner = jnp.mean(weighted * values, axis=-1, keepdims=True)
    value_gradient = inv_scale * weighted - values * (inv_scale * inv_scale * inv_scale) * inner
    grad_gain = jnp.sum(upstream * values * inv_scale, axis=0)
    return (value_gradient, grad_gain)


def dot(spec, left, right, kind=F32):
    return jnp.einsum(spec, left, right, preferred_element_type=kind)

def dot_t(left, right):
    return lax.dot_general(left, right, (((1,), (1,)), ((), ())), preferred_element_type=F32)


def full_spec(*shape):
    return pl.BlockSpec(shape, lambda *_: (0,) * len(shape))


def rope_tables(length, width):
    half = HEAD_DIM // 2
    frequency = (THETA ** (-np.arange(half, dtype=np.float32) * 2.0 / HEAD_DIM)).astype(np.float32)
    angle = np.arange(length, dtype=np.float32)[:, None] * frequency[None, :]
    cosine, sine = np.cos(angle.astype(np.float64)), np.sin(angle.astype(np.float64))
    cosine = np.concatenate([cosine, cosine], axis=1)
    sine = np.concatenate([-sine, sine], axis=1)
    copies = width // HEAD_DIM
    return np.tile(cosine, (1, copies)).astype(np.float32), np.tile(sine, (1, copies)).astype(np.float32)


def turn(values, cosine, sine):
    width, half = values.shape[1], HEAD_DIM // 2
    copies = width // cosine.shape[1]
    lane = lax.broadcasted_iota(jnp.int32, values.shape, 1)
    first = lax.rem(lane, HEAD_DIM) < half
    other = jnp.where(first, pltpu.roll(values, width - half, 1), pltpu.roll(values, half, 1))
    return values * jnp.concatenate([cosine] * copies, 1) + other * jnp.concatenate([sine] * copies, 1)


def masked_scores(query, key, allowed):
    return jnp.where(allowed, dot_t(query, key) * ATTN_SCALE, NEG_FILL)


def allowed_pairs(segs):
    length = segs.shape[1]
    row = lax.broadcasted_iota(jnp.int32, (length, length), 0)
    column = lax.broadcasted_iota(jnp.int32, (length, length), 1)
    seg_row = segs.astype(F32)
    seg_column = jnp.sum(jnp.where(row == column, seg_row, 0.0), axis=1, keepdims=True)
    return (column <= row) & (seg_row == seg_column)


def row_places(meta, rows):
    own = pl.ds(pl.multiple_of(meta[0] * rows, rows), rows)
    other = pl.ds(pl.multiple_of((1 - meta[0]) * rows, rows), rows)
    return own, other


def attend_kernel(
    meta, own_ref, other_ref, gain_ref, segs, cos_ref, sin_ref, wq, wk, wv, wo,
    hidden_out, q_out, k_out, v_out, mixed_out, log_out, own_out, other_out, x_s, part_s,
):
    rows = own_ref.shape[0]
    own, other = row_places(meta, rows)
    x_s[own, :] = own_ref[...].astype(F32)
    x_s[other, :] = other_ref[...].astype(F32)
    x = x_s[...]
    scale = lax.rsqrt(jnp.mean(x * x, axis=-1, keepdims=True) + EPS)
    hidden = (x * scale * gain_ref[...]).astype(BF16)
    hidden_out[...] = hidden
    cosine, sine = cos_ref[...], sin_ref[...]
    q_out[...] = turn(jnp.dot(hidden, wq[...], preferred_element_type=F32), cosine, sine).astype(BF16)
    k_out[...] = turn(jnp.dot(hidden, wk[...], preferred_element_type=F32), cosine, sine).astype(BF16)
    v_out[...] = jnp.dot(hidden, wv[...], preferred_element_type=F32).astype(BF16)
    allowed = allowed_pairs(segs[...])
    heads, heads_kv = wq.shape[1] // HEAD_DIM, wk.shape[1] // HEAD_DIM
    group = heads // heads_kv
    for g in range(heads_kv):
        key = k_out[:, g * HEAD_DIM : (g + 1) * HEAD_DIM]
        value = v_out[:, g * HEAD_DIM : (g + 1) * HEAD_DIM]
        for h in range(g * group, (g + 1) * group):
            at = slice(h * HEAD_DIM, (h + 1) * HEAD_DIM)
            scores = masked_scores(q_out[:, at], key, allowed)
            top = jnp.max(scores, axis=-1, keepdims=True)
            log_total = top + jnp.log(jnp.sum(jnp.exp(scores - top), axis=-1, keepdims=True))
            log_out[:, h : h + 1] = log_total
            prob = jnp.exp(scores - log_total).astype(BF16)
            mixed_out[:, at] = jnp.dot(prob, value, preferred_element_type=F32).astype(BF16)
    part_s[...] = jnp.dot(mixed_out[...], wo[...], preferred_element_type=F32)
    own_out[...] = part_s[own, :]
    other_out[...] = part_s[other, :]


def attend(meta, own, other, gain, segs, wq, wk, wv, wo):
    rows, width = own.shape
    length = segs.shape[1]
    cosine, sine = rope_tables(length, 128)
    operands = (own, other, gain[None, :], segs, cosine, sine, wq, wk, wv, wo)
    shapes = [
        ((length, width), BF16),
        ((length, wq.shape[1]), BF16),
        ((length, wk.shape[1]), BF16),
        ((length, wv.shape[1]), BF16),
        ((length, wq.shape[1]), BF16),
        ((length, 128), F32),
        ((rows, width), F32),
        ((rows, width), F32),
    ]
    return pl.pallas_call(
        attend_kernel,
        out_shape=[jax.ShapeDtypeStruct(*shape) for shape in shapes],
        grid_spec=pltpu.PrefetchScalarGridSpec(
            num_scalar_prefetch=1,
            grid=(1,),
            in_specs=[full_spec(*t.shape) for t in operands],
            out_specs=[full_spec(*shape) for shape, _ in shapes],
            scratch_shapes=[pltpu.VMEM((length, width), F32)] * 2,
        ),
        compiler_params=pltpu.CompilerParams(vmem_limit_bytes=56 * 1024 * 1024),
        cost_estimate=NO_COST,
    )(meta, *operands)


def attend_back_kernel(
    shares, meta, b_ref, segs, cos_ref, sin_ref, wq, wk, wv, wo,
    q_ref, k_ref, v_ref, mixed_ref, log_ref, *refs,
):
    share_outs, (own_out, other_out, grad_s, dq_s, part_s) = refs[:shares], refs[shares:]
    own, other = row_places(meta, own_out.shape[0])
    grad_s[...] = dot_t(b_ref[...], wo[...]).astype(BF16)
    cosine, sine = cos_ref[...], -sin_ref[...]
    allowed = allowed_pairs(segs[...])
    wide, narrow = wq.shape[1], wk.shape[1]
    heads, heads_kv = wide // HEAD_DIM, narrow // HEAD_DIM
    group = heads // heads_kv

    def transposed_dot(left, right):
        return lax.dot_general(left, right, (((0,), (0,)), ((), ())), preferred_element_type=F32)

    for g in range(heads_kv):
        there = slice(g * HEAD_DIM, (g + 1) * HEAD_DIM)
        key, value = k_ref[:, there], v_ref[:, there]
        grad_key = grad_value = 0.0
        for h in range(g * group, (g + 1) * group):
            at = slice(h * HEAD_DIM, (h + 1) * HEAD_DIM)
            query, grad = q_ref[:, at], grad_s[:, at]
            prob = jnp.exp(masked_scores(query, key, allowed) - log_ref[:, h : h + 1])
            delta = jnp.sum(grad.astype(F32) * mixed_ref[:, at].astype(F32), axis=-1, keepdims=True)
            grad_scores = (prob * (dot_t(grad, value) - delta) * ATTN_SCALE).astype(BF16)
            dq_s[:, at] = jnp.dot(grad_scores, key, preferred_element_type=F32)
            grad_key = grad_key + transposed_dot(grad_scores, query)
            grad_value = grad_value + transposed_dot(prob.astype(BF16), grad)
        dq_s[:, wide + g * HEAD_DIM : wide + (g + 1) * HEAD_DIM] = grad_key
        at = wide + narrow + g * HEAD_DIM
        dq_s[:, at : at + HEAD_DIM] = grad_value
    dq = turn(dq_s[:, :wide], cosine, sine).astype(BF16)
    dk = turn(dq_s[:, wide : wide + narrow], cosine, sine).astype(BF16)
    dv = dq_s[:, wide + narrow :].astype(BF16)
    part_s[...] = dot_t(dq, wq[...]) + dot_t(dk, wk[...]) + dot_t(dv, wv[...])
    own_out[...] = part_s[own, :]
    other_out[...] = part_s[other, :]
    for r in range(shares):

        @pl.when(meta[1] == r)
        def _():
            for step in range(shares):
                at = 0
                for part in (dq, dk, dv):
                    size = part.shape[1] // shares
                    index = (r + step) % shares
                    share_outs[step][:, at : at + size] = part[:, index * size : (index + 1) * size]
                    at += size


def attend_back(meta, shares, resid, segs, wq, wk, wv, wo, q, k, v, mixed, log_total):
    length, width = resid.shape
    cosine, sine = rope_tables(length, 128)
    operands = (resid, segs, cosine, sine, wq, wk, wv, wo, q, k, v, mixed, log_total)
    columns = wq.shape[1] + wk.shape[1] + wv.shape[1]
    shapes = [((length, columns // shares), BF16)] * shares
    shapes += [((length // 2, width), F32)] * 2
    return pl.pallas_call(
        functools.partial(attend_back_kernel, shares),
        out_shape=[jax.ShapeDtypeStruct(*shape) for shape in shapes],
        grid_spec=pltpu.PrefetchScalarGridSpec(
            num_scalar_prefetch=1,
            grid=(1,),
            in_specs=[full_spec(*t.shape) for t in operands],
            out_specs=[full_spec(*shape) for shape, _ in shapes],
            scratch_shapes=[
                pltpu.VMEM((length, wq.shape[1]), BF16),
                pltpu.VMEM((length, columns), F32),
                pltpu.VMEM((length, width), F32),
            ],
        ),
        compiler_params=pltpu.CompilerParams(vmem_limit_bytes=56 * 1024 * 1024),
        cost_estimate=NO_COST,
    )(meta, *operands)


def expert_kernel(inner, aliased, experts, meta, *refs):
    blocks, ups, tables = (refs[i * inner : (i + 1) * inner] for i in range(3))
    refs = refs[3 * inner :]
    weight_refs, refs = refs[:6], refs[6 + aliased :]
    tokens_out, upstream_out, mix_out = refs[:3]
    used_out, gate_out, up_out = refs[3:5], refs[5:7], refs[7:9]
    in_out = refs[9 : 9 + inner]
    table, mix_total, in_total = refs[9 + inner :]
    rows, width = blocks[0].shape
    expert = pl.program_id(0)

    def place(j):
        return pl.ds(pl.multiple_of(lax.rem(meta[1] + j, inner) * rows, rows), rows)

    @pl.when(expert == 0)
    def _():
        for j in range(inner):
            tokens_out[place(j), :] = blocks[j][...]
            upstream_out[place(j), :] = ups[j][...]
            table[place(j), :] = tables[j][...].astype(F32)
        mix_total[...] = jnp.zeros_like(mix_total)
        in_total[...] = jnp.zeros_like(in_total)

    lane = lax.broadcasted_iota(jnp.int32, table.shape, 1)
    wanted = (lax.rem(lane, experts) == meta[2] + expert) & (lane < 3 * experts)
    weight = jnp.sum(jnp.where(wanted, table[...], 0.0), axis=1, keepdims=True)
    for half in range(2):
        gate, up, down = (weight_refs[2 * i + half][0] for i in range(3))
        pre_gate = jnp.dot(tokens_out[...], gate, preferred_element_type=F32)
        pre_up = jnp.dot(tokens_out[...], up, preferred_element_type=F32)
        grad_act = dot_t(upstream_out[...], down) * weight
        gate_sigmoid = 1.0 / (1.0 + jnp.exp(-pre_gate))
        silu = pre_gate * gate_sigmoid
        used = (silu * pre_up * weight).astype(BF16)
        grad_gate = grad_act * pre_up * gate_sigmoid * (1.0 + pre_gate * (1.0 - gate_sigmoid))
        grad_up = grad_act * silu
        used_out[half][0] = used
        gate_out[half][0] = grad_gate.astype(BF16)
        up_out[half][0] = grad_up.astype(BF16)
        mix_total[...] += jnp.dot(used, down, preferred_element_type=F32)
        in_total[...] += dot_t((grad_gate * weight).astype(BF16), gate) + dot_t(
            (grad_up * weight).astype(BF16), up
        )

    @pl.when(expert == pl.num_programs(0) - 1)
    def _():
        mix_out[...] = mix_total[...].astype(BF16)
        for j in range(inner):
            in_out[j][...] = in_total[place(j), :].astype(BF16)


def run_experts(meta, blocks, payloads, expert_weights, buffers, total, expert_count):
    inner, rows, width = len(blocks), blocks[0].shape[0], expert_weights[0].shape[1]
    firsts = [t.shape[1] // width - 1 for t in payloads]
    experts, half = expert_weights[0].shape[0], expert_weights[0].shape[2]
    chunk = inner * rows
    extra = 128
    by_chunk = pl.BlockSpec((chunk, width), lambda e, m: (m[0], 0))
    per_expert = pl.BlockSpec((1, chunk, half), lambda e, m: (e, m[0], 0))
    spread = pl.BlockSpec((1, width, half), lambda e, m: (e, 0, 0))
    tall = pl.BlockSpec((1, half, width), lambda e, m: (e, 0, 0))
    shapes = [jax.ShapeDtypeStruct((total, width), BF16)] * 3
    shapes += [jax.ShapeDtypeStruct((experts, total, half), BF16)] * 6
    first = 1 + 3 * inner + 6
    return pl.pallas_call(
        functools.partial(expert_kernel, inner, len(buffers), expert_count),
        out_shape=shapes + [jax.ShapeDtypeStruct((rows, width), BF16)] * inner,
        grid_spec=pltpu.PrefetchScalarGridSpec(
            num_scalar_prefetch=1,
            grid=(experts,),
            in_specs=[full_spec(rows, width)] * inner
            + [pl.BlockSpec((rows, width), lambda e, m, at=at: (0, at)) for at in firsts]
            + [
                pl.BlockSpec((rows, extra), lambda e, m, at=at: (0, (at + 1) * (width // extra)))
                for at in firsts
            ]
            + [spread] * 4
            + [tall] * 2
            + [pl.BlockSpec(memory_space=pl.ANY)] * len(buffers),
            out_specs=[by_chunk] * 3 + [per_expert] * 6 + [full_spec(rows, width)] * inner,
            scratch_shapes=[
                pltpu.VMEM((chunk, extra), F32),
                pltpu.VMEM((chunk, width), F32),
                pltpu.VMEM((chunk, width), F32),
            ],
        ),
        input_output_aliases={first + i: i for i in range(len(buffers))},
        compiler_params=pltpu.CompilerParams(vmem_limit_bytes=56 * 1024 * 1024),
        cost_estimate=NO_COST,
    )(meta, *blocks, *payloads, *payloads, *expert_weights, *buffers)


def weight_grads_kernel(summed, tokens, gate, up, upstream, used, *refs):
    added, outs = refs[: 3 if summed else 0], refs[3 if summed else 0 :]

    def store(index, at, value):
        if summed:
            value = value + added[index][at].astype(F32)
        outs[index][at] = value.astype(BF16)

    def product(left, right):
        return lax.dot_general(left, right, (((0,), (0,)), ((), ())), preferred_element_type=F32)

    for e in range(gate.shape[0]):
        store(0, e, product(tokens[...], gate[e]))
        store(1, e, product(tokens[...], up[e]))
    store(2, 0, product(used[0], upstream[...]))


def weight_grads(tokens, upstream, used, gate, up, added):
    (experts, total, half), width = gate.shape, tokens.shape[1]
    steps = 2 * experts
    high, low = width // steps, half // 2
    spread = pl.BlockSpec((experts, high, half), lambda r: (0, r, 0))
    tall = pl.BlockSpec((1, low, width), lambda r: (lax.div(r, 2), lax.rem(r, 2), 0))
    shapes = [(experts, width, half)] * 2 + [(experts, half, width)]
    return pl.pallas_call(
        functools.partial(weight_grads_kernel, bool(added)),
        out_shape=[jax.ShapeDtypeStruct(shape, BF16) for shape in shapes],
        grid=(steps,),
        in_specs=[
            pl.BlockSpec((total, high), lambda r: (0, r)),
            full_spec(experts, total, half),
            full_spec(experts, total, half),
            full_spec(total, width),
            pl.BlockSpec((1, total, low), lambda r: (lax.div(r, 2), 0, lax.rem(r, 2))),
        ]
        + ([spread, spread, tall] if added else []),
        out_specs=[spread, spread, tall],
        compiler_params=pltpu.CompilerParams(vmem_limit_bytes=56 * 1024 * 1024),
        cost_estimate=NO_COST,
    )(tokens, gate, up, upstream, used, *added)


def place_kernel(sizes, aliased, meta, block_ref, *refs):
    at = 0
    for size, out in zip(sizes, refs[aliased:]):
        out[...] = block_ref[0, :, at : at + size].astype(F32)
        at += size


def place_line(meta, pieces, sizes, shapes, buffers):
    count, rows, width = pieces.shape
    low = [pl.BlockSpec((rows, size), lambda i, m: (m[4 * i], m[4 * i + 1])) for size in sizes[:-1]]
    low.append(pl.BlockSpec((rows, sizes[-1]), lambda i, m: (m[4 * i + 2], m[4 * i + 3])))
    return pl.pallas_call(
        functools.partial(place_kernel, sizes, len(buffers)),
        out_shape=[jax.ShapeDtypeStruct(shape, F32) for shape in shapes],
        grid_spec=pltpu.PrefetchScalarGridSpec(
            num_scalar_prefetch=1,
            grid=(count,),
            in_specs=[pl.BlockSpec((1, rows, width), lambda i, m: (i, 0, 0))]
            + [pl.BlockSpec(memory_space=pl.ANY)] * len(buffers),
            out_specs=low,
        ),
        input_output_aliases={2 + i: i for i in range(len(buffers))},
        cost_estimate=NO_COST,
    )(meta, pieces, *buffers)


def dense_kernel(count, inner, meta, *refs):
    hidden, mixed, shares, resids = (refs[i * count : (i + 1) * count] for i in range(4))
    outs, scratch = refs[4 * count : -1], refs[-1]
    size, step = shares[0].shape[1], pl.program_id(0)

    def summed(lefts, rights):
        return sum(
            lax.dot_general(
                left[...], right[...], (((0,), (0,)), ((), ())), preferred_element_type=F32
            )
            for left, right in zip(lefts, rights)
        )

    scratch[:, :size] = summed(hidden, shares).astype(BF16)
    scratch[:, size:] = summed(mixed, resids).astype(BF16)
    rows = outs[0].shape[0]
    for k in range(len(outs) // inner):

        @pl.when(lax.rem(meta[0] + k, len(outs) // inner) == step)
        def _():
            for j in range(inner):
                start = pl.multiple_of(lax.rem(meta[1] + j, inner) * rows, rows)
                outs[k * inner + j][...] = scratch[pl.ds(start, rows), :]


def dense_blocks(meta, hidden, mixed, shares, resids, outer, inner):
    count, (length, width), size = len(hidden), hidden[0].shape, shares[0].shape[1]
    high, wide = width // outer, mixed[0].shape[1]
    part = resids[0].shape[1] * wide // width
    per = wide // high
    block = (high // inner, size + part)
    return pl.pallas_call(
        functools.partial(dense_kernel, count, inner),
        out_shape=[jax.ShapeDtypeStruct(block, BF16)] * (outer * inner),
        grid_spec=pltpu.PrefetchScalarGridSpec(
            num_scalar_prefetch=1,
            grid=(outer,),
            in_specs=[pl.BlockSpec((length, high), lambda r, m: (0, r))] * count
            + [pl.BlockSpec((length, high), lambda r, m: (0, lax.rem(r, per)))] * count
            + [full_spec(length, size)] * count
            + [pl.BlockSpec((length, part), lambda r, m: (0, lax.div(r, per)))] * count,
            out_specs=[full_spec(*block)] * (outer * inner),
            scratch_shapes=[pltpu.VMEM((high, size + part), BF16)],
        ),
        compiler_params=pltpu.CompilerParams(vmem_limit_bytes=56 * 1024 * 1024),
        cost_estimate=NO_COST,
    )(meta, *hidden, *mixed, *shares, *resids)


def body(
    activations,
    segments,
    routes,
    route_weights,
    norm_attn_gain,
    norm_ffn_gain,
    query_weight,
    key_matrix,
    value_matrix,
    output_projection_weight,
    expert_gate,
    expert_up,
    expert_down,
    grad_output,
):
    tensor_rank = lax.axis_index("tensor")
    dp_rank = lax.axis_index("dp")
    dp_count = lax.axis_size("dp")
    outer, inner = grid_sizes()
    outer_rank = lax.axis_index("expert") // inner
    inner_rank = lax.axis_index("expert") % inner
    rows, width = activations.shape
    experts_here = expert_gate.shape[0]
    expert_count = experts_here * lax.axis_size("expert")

    named = routes[:, :, None] == jnp.arange(expert_count, dtype=jnp.int32)
    weight_table = jnp.sum(jnp.where(named, route_weights[:, :, None], 0.0), axis=1)
    high = lax.reduce_precision(weight_table, 8, 7)
    middle = lax.reduce_precision(weight_table - high, 8, 7)
    low = weight_table - high - middle
    table = jnp.concatenate([high, middle, low], axis=1).astype(BF16)
    table = jnp.pad(table, ((0, 0), (0, -table.shape[1] % 128)))
    payload = jnp.concatenate([grad_output, table], axis=1)
    up_one, up_line = shift_outer(payload, 1), inner_line(payload)
    heads_meta = jnp.stack([tensor_rank, dp_rank]).astype(jnp.int32)
    attn_weights = (query_weight, key_matrix, value_matrix, output_projection_weight)
    hidden, q, k, v, mixed, log_total, attn_own, attn_other = attend(
        heads_meta, activations, swap(activations), norm_attn_gain, segments, *attn_weights
    )
    x_own = activations.astype(F32)
    attn_own, attn_other, up_one, up_line = together(attn_own, attn_other, up_one, up_line)
    residual = x_own + attn_own + swap(attn_other)
    normed_two, scale_two = norm_forward(residual, norm_ffn_gain)

    expert_weights = []
    for weights_own in (expert_gate, expert_up, expert_down):
        expert_weights += [weights_own, swap(weights_own)]
    first_expert = lax.axis_index("expert") * experts_here

    h_own = normed_two.astype(BF16)
    h_one, h_line = shift_outer(h_own, 1), inner_line(h_own)
    h_one, h_line, up_one = together(h_one, h_line, up_one)
    both = jnp.concatenate([h_one, up_one], axis=1)

    def experts_on(chunk, buffers, blocks, payloads):
        meta = jnp.stack([(outer_rank + chunk) % outer, inner_rank, first_expert])
        made = run_experts(
            meta.astype(jnp.int32), blocks, payloads, expert_weights, buffers,
            outer * inner * rows, expert_count,
        )
        return list(made[:9]), made[9:]

    def line_sum(parts):
        return inner_sum(parts).astype(BF16)

    others_rows = [shift_dp(activations, step) for step in range(1, dp_count)]
    line, both = inner_line(both), shift_outer(both, 1)
    made = experts_on(0, [], h_line, up_line)
    made, line, both = together(made, line, both)
    buffers, in_zero = made
    made = experts_on(1, buffers, line, line)
    line, both = inner_line(both), shift_outer(both, 1)
    made, line, both = together(made, line, both)
    buffers, parts = made
    made = experts_on(2, buffers, line, line)
    line, sum_one = inner_line(both), line_sum(parts)
    made, line, sum_one = together(made, line, sum_one)
    buffers, parts = made
    sum_one, sum_two = shift_outer(sum_one, -1), line_sum(parts)
    made = experts_on(3, buffers, line, line)
    made, sum_one, sum_two, in_zero = together(made, sum_one, sum_two, in_zero)
    buffers, parts = made
    tokens_all, upstream_all, mix_all, *pairs = buffers
    sides = [[pairs[at + half] for at in (0, 2, 4)] for half in range(2)]
    peers = weight_grads(tokens_all, upstream_all, *sides[1], [])
    sum_two, sum_three, sum_zero = shift_outer(sum_two, -2), line_sum(parts), inner_sum(in_zero)
    sum_two, sum_three, sum_zero, peers = together(sum_two, sum_three, sum_zero, peers)
    hidden_all = [hidden]
    for step in range(1, dp_count):
        other = jnp.concatenate([others_rows[step - 1], swap(others_rows[step - 1])], axis=0)
        other = jnp.where(tensor_rank == 0, other, jnp.roll(other, rows, 0)).astype(F32)
        hidden_all.append(norm_forward(other, norm_attn_gain)[0].astype(BF16))
    sum_three, arrived, hidden_all = together(
        shift_outer(sum_three, -3), [swap(peer) for peer in peers], hidden_all
    )
    grad_h_own = sum_zero.astype(F32)
    for term in (sum_one, sum_two, sum_three):
        grad_h_own = grad_h_own + term.astype(F32)

    def sum_dp(half):
        bit, found = 1, []
        while bit < dp_count:
            found.append(lax.ppermute(half, "dp", [(i, i ^ bit) for i in range(dp_count)]))
            bit *= 2
            if bit < dp_count:
                half = (half.astype(F32) + found.pop().astype(F32)).astype(BF16)
        return half, *found

    def total(pair):
        return sum(t.astype(F32) for t in pair)

    grad_norm_part, _ = norm_backward(residual, scale_two, norm_ffn_gain, grad_h_own)
    grad_resid = grad_output.astype(F32) + grad_norm_part
    resid_own = grad_resid.astype(BF16)
    resid_other = swap(resid_own)
    resid_full = jnp.where(
        tensor_rank == 0,
        jnp.concatenate([resid_own, resid_other], axis=0),
        jnp.concatenate([resid_other, resid_own], axis=0),
    )
    expert_mix = lax.psum_scatter(
        after(mix_all, sum_three), "expert", scatter_dimension=0, tiled=True
    )
    *shares, dh_own, dh_other = attend_back(
        heads_meta, dp_count, resid_full, segments, *attn_weights, q, k, v, mixed, log_total,
    )

    mixed_all = [mixed] + [shift_dp(mixed, step) for step in range(1, dp_count)]
    length, share_width = resid_full.shape[0], width // dp_count

    def columns(index):
        return lax.dynamic_slice_in_dim(resid_full, index * share_width, share_width, 1)

    resid_shares = [columns(dp_rank)]
    for step in range(1, dp_count):
        resid_shares.append(shift_dp(columns((dp_rank + step) % dp_count), step))
    shares, resid_shares = together(shares, resid_shares)
    all_shares = [shares[0]] + [shift_dp(shares[step], step) for step in range(1, dp_count)]
    halves = weight_grads(tokens_all, upstream_all, *sides[0], arrived)
    all_shares, halves = together(all_shares, halves)
    parts = width // mixed.shape[1]
    sizes = [t.shape[1] // dp_count for t in (query_weight, key_matrix, value_matrix)]
    sizes.append(share_width // parts)
    aligned = all(size % 128 == 0 for size in sizes)
    block = width // (outer * inner)
    def row_terms(part, step):
        start = (outer_rank + step) % outer * inner
        return [
            lax.dynamic_slice_in_dim(part, (start + (inner_rank + j) % inner) * block, block, 0)
            for j in range(inner)
        ]

    if aligned:
        meta = jnp.stack([outer_rank, inner_rank]).astype(jnp.int32)
        made = dense_blocks(meta, hidden_all, mixed_all, all_shares, resid_shares, outer, inner)
        terms = [made[k * inner : (k + 1) * inner] for k in range(outer)]
    else:
        qkv_part = dot(
            "sd,sa->da", jnp.concatenate(hidden_all, 0), jnp.concatenate(all_shares, 0), BF16
        )
        mix_part = dot(
            "sa,shb->hab",
            jnp.concatenate(mixed_all, 0),
            jnp.concatenate(resid_shares, 0).reshape(length * dp_count, parts, share_width // parts),
            BF16,
        )
        dense_part = jnp.concatenate([qkv_part, mix_part.reshape(width, -1)], axis=1)
        terms = [row_terms(dense_part, k) for k in range(outer)]
    terms, halves = together(terms, halves)
    gate_half, up_half, down_half = halves
    gate_pair, up_pair = sum_dp(gate_half), sum_dp(up_half)
    two, dh_other = line_sum(terms[2]), swap(dh_other)
    two, dh_other, terms = together(two, dh_other, terms)
    scale_one = lax.rsqrt(jnp.mean(x_own * x_own, axis=-1, keepdims=True) + EPS)
    grad_x_part, grad_attn_gain = norm_backward(
        x_own, scale_one, norm_attn_gain, dh_own + dh_other
    )
    grad_input = grad_resid + grad_x_part
    late = after((grad_h_own, residual, scale_two), terms)
    grad_ffn_gain = jnp.sum(late[0] * late[1] * late[2], axis=0)
    gains, hops = jnp.stack([grad_attn_gain, grad_ffn_gain]), hops_of_all()
    two, one, three = shift_outer(two, -2), line_sum(terms[1]), line_sum(terms[3])
    two, one, three, terms, gate_pair, expert_mix = together(
        two, one, three, terms, gate_pair, expert_mix
    )
    one, three, zero = shift_outer(one, -1), shift_outer(three, -3), inner_sum(terms[0])
    one, three, zero, other, grad_input = together(
        one, three, zero, exchange(gains, hops[0]), grad_input
    )
    gains, hops = gains + other, hops[1:]
    reduced = zero.astype(F32)
    for term in (one, two, three):
        reduced = reduced + term.astype(F32)
    reduced = reduced.astype(BF16)
    shapes = [t.shape for t in (query_weight, key_matrix, value_matrix)] + [(width // parts, width)]
    residual = after(residual, reduced)
    block_out = (residual + expert_mix.astype(F32)).astype(BF16)
    if aligned:
        per, dense = outer * inner // parts, []

        def place(pieces, found, dense):
            meta = []
            for k, j, turn in found:
                index = (outer_rank + k) % outer * inner + (inner_rank + j) % inner
                share = (dp_rank - turn) % dp_count
                meta += [index, share, index % per, share * parts + index // per]
            return place_line(jnp.stack(meta).astype(jnp.int32), pieces, sizes, shapes, dense)

        others = range(1, dp_count)
        step = {
            "line": inner_line(reduced[None]),
            "next": shift_outer(reduced[None]),
            "others": [shift_dp(reduced, turn)[None] for turn in others],
            "gains": exchange(gains, hops[0]),
            "block_out": block_out,
            "pair": up_pair,
        }
        (step,) = together(step)
        up_pair = step["pair"]
        block_out, gains, hops = step["block_out"], gains + step["gains"], hops[1:]
        lines = [step["line"]]
        held = jnp.concatenate([step["next"], *step["others"]], axis=0)
        down_pair = sum_dp(after(down_half, step["others"]))
        for k in range(1, outer + 1):
            step = {"line": inner_line(held), "gains": exchange(gains, hops[0]) if hops else gains}
            if k < outer:
                step["next"] = shift_outer(held if k + 1 < outer else held[1:])
            before = [(k - 1, turn) for turn in ([0] if k == 1 else [0, *others])]
            before = [(at - 1 if turn else at, turn) for at, turn in before]
            made = dense
            for j, pieces in enumerate(lines[-1]):
                made = place(pieces, [(at, j, turn) for at, turn in before], made)
            step["dense"] = made
            if k == 1:
                step["done"] = total(gate_pair)
            if k == 2:
                step["done"] = total(up_pair)
            if k == 3:
                step["done"] = total(down_pair)
            (step,) = together(step)
            if hops:
                gains, hops = gains + step["gains"], hops[1:]
            if k == 1:
                gate_sum = step["done"]
            if k == 2:
                up_sum = step["done"]
            if k == 3:
                down_sum = step["done"]
            dense, held = step["dense"], step.get("next")
            lines.append(step["line"])
        for j, pieces in enumerate(lines[-1]):
            dense = place(pieces, [(outer - 1, j, turn) for turn in others], dense)
    else:
        for hop in hops:
            gains = gains + exchange(gains, hop)
        gate_sum, up_sum, down_sum = (
            total(pair) for pair in (gate_pair, up_pair, sum_dp(down_half))
        )
        gathered = lax.all_gather(reduced, ("dp", "expert"), axis=0, tiled=True)
        gathered = gathered.reshape(dp_count, width, -1).astype(F32)
        starts = [sum(sizes[:i]) for i in range(len(sizes))]
        dense = [gathered[:, :, at : at + size] for at, size in zip(starts, sizes)]
        dense[:-1] = [t.transpose(1, 0, 2).reshape(width, -1) for t in dense[:-1]]
        mix_w = dense[-1].reshape(dp_count, parts, width // parts, -1)
        dense[-1] = mix_w.transpose(2, 0, 1, 3).reshape(width // parts, width)
    return (
        block_out,
        grad_input,
        gains[0],
        gains[1],
        *dense,
        gate_sum,
        up_sum,
        down_sum,
    )


def solution(mesh):
    tokens = P(("dp", "expert", "tensor"), None)
    whole = P()
    columns = P(None, "tensor")
    hidden_last = P("expert", None, "tensor")
    hidden_mid = P("expert", "tensor", None)
    mixer = P("tensor", None)
    return jax.shard_map(
        body,
        mesh=mesh,
        in_specs=(
            tokens,
            P(("dp", "expert"), None),
            tokens,
            tokens,
            whole,
            whole,
            columns,
            columns,
            columns,
            mixer,
            hidden_last,
            hidden_last,
            hidden_mid,
            tokens,
        ),
        out_specs=(
            tokens,
            tokens,
            whole,
            whole,
            columns,
            columns,
            columns,
            mixer,
            hidden_last,
            hidden_last,
            hidden_mid,
        ),
        check_vma=False,
    )
```

```python
import functools

import jax
import jax.numpy as jnp
import numpy as np
from jax import lax
from jax.experimental import pallas as pl
from jax.experimental.pallas import tpu as pltpu
from jax.sharding import PartitionSpec as P

HEAD_DIM = 64
EPS = 1e-05
ATTN_SCALE = 0.015625
THETA = 10000.0
NEG_FILL = -1e30
F32 = jnp.float32
BF16 = jnp.bfloat16
NO_COST = pl.CostEstimate(flops=1, bytes_accessed=1, transcendentals=0)


def after(values, token):
    return lax.optimization_barrier((values, token))[0]


def swap(values):
    return lax.ppermute(values, "tensor", [(0, 1), (1, 0)])


def shift_dp(values, step):
    count = lax.axis_size("dp")
    return lax.ppermute(values, "dp", [(i, (i + step) % count) for i in range(count)])


def grid_sizes():
    count = lax.axis_size("expert")
    return 4, count // 4


def shift_outer(values, step=1):
    outer, inner = grid_sizes()
    pairs = [(((o + step) % outer) * inner + i, o * inner + i) for o in range(outer) for i in range(inner)]
    return lax.ppermute(values, "expert", pairs)


def shift_inner(values):
    outer, inner = grid_sizes()
    pairs = [(o * inner + (i + 1) % inner, o * inner + i) for o in range(outer) for i in range(inner)]
    return lax.ppermute(values, "expert", pairs)


def inner_line(block):
    line = [block]
    for _ in range(1, grid_sizes()[1]):
        line.append(shift_inner(line[-1]))
    return line


def inner_sum(parts):
    inner, total = len(parts), parts[1 % len(parts)]
    for j in range(2, inner + 1):
        total = shift_inner(total.astype(BF16)).astype(F32) + parts[j % inner].astype(F32)
    return total


def together(*values):
    return lax.optimization_barrier(values)


def hops_of_all():
    bits = {}
    for axis in ("tensor", "expert", "dp"):
        count = lax.axis_size(axis)
        bits[axis] = [(axis, 1 << i) for i in range(count.bit_length() - 1)]
    return bits["tensor"] + bits["dp"] + bits["expert"]


def exchange(values, hop):
    axis, bit = hop
    return lax.ppermute(values, axis, [(i, i ^ bit) for i in range(lax.axis_size(axis))])


def norm_forward(values, gain_vector):
    inv_scale = lax.rsqrt(jnp.mean(values * values, axis=-1, keepdims=True) + EPS)
    return (values * inv_scale * gain_vector, inv_scale)


def norm_backward(values, inv_scale, gain_vector, upstream):
    weighted = upstream * gain_vector
    inner = jnp.mean(weighted * values, axis=-1, keepdims=True)
    value_gradient = inv_scale * weighted - values * (inv_scale * inv_scale * inv_scale) * inner
    grad_gain = jnp.sum(upstream * values * inv_scale, axis=0)
    return (value_gradient, grad_gain)


def dot(spec, left, right, kind=F32):
    return jnp.einsum(spec, left, right, preferred_element_type=kind)

def dot_t(left, right):
    return lax.dot_general(left, right, (((1,), (1,)), ((), ())), preferred_element_type=F32)


def full_spec(*shape):
    return pl.BlockSpec(shape, lambda *_: (0,) * len(shape))


def rope_tables(length, width):
    half = HEAD_DIM // 2
    frequency = (THETA ** (-np.arange(half, dtype=np.float32) * 2.0 / HEAD_DIM)).astype(np.float32)
    angle = np.arange(length, dtype=np.float32)[:, None] * frequency[None, :]
    cosine, sine = np.cos(angle.astype(np.float64)), np.sin(angle.astype(np.float64))
    cosine = np.concatenate([cosine, cosine], axis=1)
    sine = np.concatenate([-sine, sine], axis=1)
    copies = width // HEAD_DIM
    return np.tile(cosine, (1, copies)).astype(np.float32), np.tile(sine, (1, copies)).astype(np.float32)


def turn(values, cosine, sine):
    width, half = values.shape[1], HEAD_DIM // 2
    copies = width // cosine.shape[1]
    lane = lax.broadcasted_iota(jnp.int32, values.shape, 1)
    first = lax.rem(lane, HEAD_DIM) < half
    other = jnp.where(first, pltpu.roll(values, width - half, 1), pltpu.roll(values, half, 1))
    return values * jnp.concatenate([cosine] * copies, 1) + other * jnp.concatenate([sine] * copies, 1)


def masked_scores(query, key, allowed):
    return jnp.where(allowed, dot_t(query, key) * ATTN_SCALE, NEG_FILL)


def allowed_pairs(segs):
    length = segs.shape[1]
    row = lax.broadcasted_iota(jnp.int32, (length, length), 0)
    column = lax.broadcasted_iota(jnp.int32, (length, length), 1)
    seg_row = segs.astype(F32)
    seg_column = jnp.sum(jnp.where(row == column, seg_row, 0.0), axis=1, keepdims=True)
    return (column <= row) & (seg_row == seg_column)


def row_places(meta, rows):
    own = pl.ds(pl.multiple_of(meta[0] * rows, rows), rows)
    other = pl.ds(pl.multiple_of((1 - meta[0]) * rows, rows), rows)
    return own, other


def attend_kernel(
    meta, own_ref, other_ref, gain_ref, segs, cos_ref, sin_ref, wq, wk, wv, wo,
    hidden_out, q_out, k_out, v_out, mixed_out, log_out, own_out, other_out, x_s, part_s,
):
    rows = own_ref.shape[0]
    own, other = row_places(meta, rows)
    x_s[own, :] = own_ref[...].astype(F32)
    x_s[other, :] = other_ref[...].astype(F32)
    x = x_s[...]
    scale = lax.rsqrt(jnp.mean(x * x, axis=-1, keepdims=True) + EPS)
    hidden = (x * scale * gain_ref[...]).astype(BF16)
    hidden_out[...] = hidden
    cosine, sine = cos_ref[...], sin_ref[...]
    q_out[...] = turn(jnp.dot(hidden, wq[...], preferred_element_type=F32), cosine, sine).astype(BF16)
    k_out[...] = turn(jnp.dot(hidden, wk[...], preferred_element_type=F32), cosine, sine).astype(BF16)
    v_out[...] = jnp.dot(hidden, wv[...], preferred_element_type=F32).astype(BF16)
    allowed = allowed_pairs(segs[...])
    heads, heads_kv = wq.shape[1] // HEAD_DIM, wk.shape[1] // HEAD_DIM
    group = heads // heads_kv
    for g in range(heads_kv):
        key = k_out[:, g * HEAD_DIM : (g + 1) * HEAD_DIM]
        value = v_out[:, g * HEAD_DIM : (g + 1) * HEAD_DIM]
        for h in range(g * group, (g + 1) * group):
            at = slice(h * HEAD_DIM, (h + 1) * HEAD_DIM)
            scores = masked_scores(q_out[:, at], key, allowed)
            top = jnp.max(scores, axis=-1, keepdims=True)
            log_total = top + jnp.log(jnp.sum(jnp.exp(scores - top), axis=-1, keepdims=True))
            log_out[:, h : h + 1] = log_total
            prob = jnp.exp(scores - log_total).astype(BF16)
            mixed_out[:, at] = jnp.dot(prob, value, preferred_element_type=F32).astype(BF16)
    part_s[...] = jnp.dot(mixed_out[...], wo[...], preferred_element_type=F32)
    own_out[...] = part_s[own, :]
    other_out[...] = part_s[other, :]


def attend(meta, own, other, gain, segs, wq, wk, wv, wo):
    rows, width = own.shape
    length = segs.shape[1]
    cosine, sine = rope_tables(length, 128)
    operands = (own, other, gain[None, :], segs, cosine, sine, wq, wk, wv, wo)
    shapes = [
        ((length, width), BF16),
        ((length, wq.shape[1]), BF16),
        ((length, wk.shape[1]), BF16),
        ((length, wv.shape[1]), BF16),
        ((length, wq.shape[1]), BF16),
        ((length, 128), F32),
        ((rows, width), F32),
        ((rows, width), F32),
    ]
    return pl.pallas_call(
        attend_kernel,
        out_shape=[jax.ShapeDtypeStruct(*shape) for shape in shapes],
        grid_spec=pltpu.PrefetchScalarGridSpec(
            num_scalar_prefetch=1,
            grid=(1,),
            in_specs=[full_spec(*t.shape) for t in operands],
            out_specs=[full_spec(*shape) for shape, _ in shapes],
            scratch_shapes=[pltpu.VMEM((length, width), F32)] * 2,
        ),
        compiler_params=pltpu.CompilerParams(vmem_limit_bytes=56 * 1024 * 1024),
        cost_estimate=NO_COST,
    )(meta, *operands)


def attend_back_kernel(
    shares, meta, b_ref, segs, cos_ref, sin_ref, wq, wk, wv, wo,
    q_ref, k_ref, v_ref, mixed_ref, log_ref, *refs,
):
    share_outs, (own_out, other_out, grad_s, dq_s, part_s) = refs[:shares], refs[shares:]
    own, other = row_places(meta, own_out.shape[0])
    grad_s[...] = dot_t(b_ref[...], wo[...]).astype(BF16)
    cosine, sine = cos_ref[...], -sin_ref[...]
    allowed = allowed_pairs(segs[...])
    wide, narrow = wq.shape[1], wk.shape[1]
    heads, heads_kv = wide // HEAD_DIM, narrow // HEAD_DIM
    group = heads // heads_kv

    def transposed_dot(left, right):
        return lax.dot_general(left, right, (((0,), (0,)), ((), ())), preferred_element_type=F32)

    for g in range(heads_kv):
        there = slice(g * HEAD_DIM, (g + 1) * HEAD_DIM)
        key, value = k_ref[:, there], v_ref[:, there]
        grad_key = grad_value = 0.0
        for h in range(g * group, (g + 1) * group):
            at = slice(h * HEAD_DIM, (h + 1) * HEAD_DIM)
            query, grad = q_ref[:, at], grad_s[:, at]
            prob = jnp.exp(masked_scores(query, key, allowed) - log_ref[:, h : h + 1])
            delta = jnp.sum(grad.astype(F32) * mixed_ref[:, at].astype(F32), axis=-1, keepdims=True)
            grad_scores = (prob * (dot_t(grad, value) - delta) * ATTN_SCALE).astype(BF16)
            dq_s[:, at] = jnp.dot(grad_scores, key, preferred_element_type=F32)
            grad_key = grad_key + transposed_dot(grad_scores, query)
            grad_value = grad_value + transposed_dot(prob.astype(BF16), grad)
        dq_s[:, wide + g * HEAD_DIM : wide + (g + 1) * HEAD_DIM] = grad_key
        at = wide + narrow + g * HEAD_DIM
        dq_s[:, at : at + HEAD_DIM] = grad_value
    dq = turn(dq_s[:, :wide], cosine, sine).astype(BF16)
    dk = turn(dq_s[:, wide : wide + narrow], cosine, sine).astype(BF16)
    dv = dq_s[:, wide + narrow :].astype(BF16)
    part_s[...] = dot_t(dq, wq[...]) + dot_t(dk, wk[...]) + dot_t(dv, wv[...])
    own_out[...] = part_s[own, :]
    other_out[...] = part_s[other, :]
    for r in range(shares):

        @pl.when(meta[1] == r)
        def _():
            for step in range(shares):
                at = 0
                for part in (dq, dk, dv):
                    size = part.shape[1] // shares
                    index = (r + step) % shares
                    share_outs[step][:, at : at + size] = part[:, index * size : (index + 1) * size]
                    at += size


def attend_back(meta, shares, resid, segs, wq, wk, wv, wo, q, k, v, mixed, log_total):
    length, width = resid.shape
    cosine, sine = rope_tables(length, 128)
    operands = (resid, segs, cosine, sine, wq, wk, wv, wo, q, k, v, mixed, log_total)
    columns = wq.shape[1] + wk.shape[1] + wv.shape[1]
    shapes = [((length, columns // shares), BF16)] * shares
    shapes += [((length // 2, width), F32)] * 2
    return pl.pallas_call(
        functools.partial(attend_back_kernel, shares),
        out_shape=[jax.ShapeDtypeStruct(*shape) for shape in shapes],
        grid_spec=pltpu.PrefetchScalarGridSpec(
            num_scalar_prefetch=1,
            grid=(1,),
            in_specs=[full_spec(*t.shape) for t in operands],
            out_specs=[full_spec(*shape) for shape, _ in shapes],
            scratch_shapes=[
                pltpu.VMEM((length, wq.shape[1]), BF16),
                pltpu.VMEM((length, columns), F32),
                pltpu.VMEM((length, width), F32),
            ],
        ),
        compiler_params=pltpu.CompilerParams(vmem_limit_bytes=56 * 1024 * 1024),
        cost_estimate=NO_COST,
    )(meta, *operands)


def expert_kernel(inner, aliased, experts, meta, *refs):
    blocks, ups, tables = (refs[i * inner : (i + 1) * inner] for i in range(3))
    refs = refs[3 * inner :]
    weight_refs, refs = refs[:6], refs[6 + aliased :]
    tokens_out, upstream_out = refs[:2]
    used_out, gate_out, up_out = refs[2:4], refs[4:6], refs[6:8]
    mix_out, in_out = refs[8 : 8 + inner], refs[8 + inner : 8 + 2 * inner]
    table, mix_total, in_total = refs[8 + 2 * inner :]
    rows, width = blocks[0].shape
    expert = pl.program_id(0)

    def place(j):
        return pl.ds(pl.multiple_of(lax.rem(meta[1] + j, inner) * rows, rows), rows)

    @pl.when(expert == 0)
    def _():
        for j in range(inner):
            tokens_out[place(j), :] = blocks[j][...]
            upstream_out[place(j), :] = ups[j][...]
            table[place(j), :] = tables[j][...].astype(F32)
        mix_total[...] = jnp.zeros_like(mix_total)
        in_total[...] = jnp.zeros_like(in_total)

    lane = lax.broadcasted_iota(jnp.int32, table.shape, 1)
    wanted = (lax.rem(lane, experts) == meta[2] + expert) & (lane < 3 * experts)
    weight = jnp.sum(jnp.where(wanted, table[...], 0.0), axis=1, keepdims=True)
    for half in range(2):
        gate, up, down = (weight_refs[2 * i + half][0] for i in range(3))
        pre_gate = jnp.dot(tokens_out[...], gate, preferred_element_type=F32)
        pre_up = jnp.dot(tokens_out[...], up, preferred_element_type=F32)
        grad_act = dot_t(upstream_out[...], down) * weight
        gate_sigmoid = 1.0 / (1.0 + jnp.exp(-pre_gate))
        silu = pre_gate * gate_sigmoid
        used = (silu * pre_up * weight).astype(BF16)
        grad_gate = grad_act * pre_up * gate_sigmoid * (1.0 + pre_gate * (1.0 - gate_sigmoid))
        grad_up = grad_act * silu
        used_out[half][0] = used
        gate_out[half][0] = grad_gate.astype(BF16)
        up_out[half][0] = grad_up.astype(BF16)
        mix_total[...] += jnp.dot(used, down, preferred_element_type=F32)
        in_total[...] += dot_t((grad_gate * weight).astype(BF16), gate) + dot_t(
            (grad_up * weight).astype(BF16), up
        )

    @pl.when(expert == pl.num_programs(0) - 1)
    def _():
        for j in range(inner):
            mix_out[j][...] = mix_total[place(j), :].astype(BF16)
            in_out[j][...] = in_total[place(j), :].astype(BF16)


def run_experts(meta, chunk_index, blocks, payloads, expert_weights, buffers, total, expert_count):
    inner, rows, width = len(blocks), blocks[0].shape[0], expert_weights[0].shape[1]
    firsts = [t.shape[1] // width - 1 for t in payloads]
    experts, half = expert_weights[0].shape[0], expert_weights[0].shape[2]
    chunk = inner * rows
    extra = 128
    by_chunk = pl.BlockSpec((chunk, width), lambda e, m: (m[0], 0))
    per_expert = pl.BlockSpec((1, chunk, half), lambda e, m: (e, m[0], 0))
    spread = pl.BlockSpec((1, width, half), lambda e, m: (e, 0, 0))
    tall = pl.BlockSpec((1, half, width), lambda e, m: (e, 0, 0))
    line = pl.BlockSpec((rows, width), lambda e, m: (chunk_index, 0))
    shapes = [jax.ShapeDtypeStruct((total, width), BF16)] * 2
    shapes += [jax.ShapeDtypeStruct((experts, total, half), BF16)] * 6
    shapes += [jax.ShapeDtypeStruct((total // inner, width), BF16)] * inner
    first = 1 + 3 * inner + 6
    return pl.pallas_call(
        functools.partial(expert_kernel, inner, len(buffers), expert_count),
        out_shape=shapes + [jax.ShapeDtypeStruct((rows, width), BF16)] * inner,
        grid_spec=pltpu.PrefetchScalarGridSpec(
            num_scalar_prefetch=1,
            grid=(experts,),
            in_specs=[full_spec(rows, width)] * inner
            + [pl.BlockSpec((rows, width), lambda e, m, at=at: (0, at)) for at in firsts]
            + [
                pl.BlockSpec((rows, extra), lambda e, m, at=at: (0, (at + 1) * (width // extra)))
                for at in firsts
            ]
            + [spread] * 4
            + [tall] * 2
            + [pl.BlockSpec(memory_space=pl.ANY)] * len(buffers),
            out_specs=[by_chunk] * 2
            + [per_expert] * 6
            + [line] * inner
            + [full_spec(rows, width)] * inner,
            scratch_shapes=[
                pltpu.VMEM((chunk, extra), F32),
                pltpu.VMEM((chunk, width), F32),
                pltpu.VMEM((chunk, width), F32),
            ],
        ),
        input_output_aliases={first + i: i for i in range(len(buffers))},
        compiler_params=pltpu.CompilerParams(vmem_limit_bytes=56 * 1024 * 1024),
        cost_estimate=NO_COST,
    )(meta, *blocks, *payloads, *payloads, *expert_weights, *buffers)


def weight_grads_kernel(summed, tokens, gate, up, upstream, used, *refs):
    added, outs = refs[: 3 if summed else 0], refs[3 if summed else 0 :]

    def store(index, at, value):
        if summed:
            value = value + added[index][at].astype(F32)
        outs[index][at] = value.astype(BF16)

    def product(left, right):
        return lax.dot_general(left, right, (((0,), (0,)), ((), ())), preferred_element_type=F32)

    for e in range(gate.shape[0]):
        store(0, e, product(tokens[...], gate[e]))
        store(1, e, product(tokens[...], up[e]))
    store(2, 0, product(used[0], upstream[...]))


def weight_grads(tokens, upstream, used, gate, up, added):
    (experts, total, half), width = gate.shape, tokens.shape[1]
    steps = 2 * experts
    high, low = width // steps, half // 2
    spread = pl.BlockSpec((experts, high, half), lambda r: (0, r, 0))
    tall = pl.BlockSpec((1, low, width), lambda r: (lax.div(r, 2), lax.rem(r, 2), 0))
    shapes = [(experts, width, half)] * 2 + [(experts, half, width)]
    return pl.pallas_call(
        functools.partial(weight_grads_kernel, bool(added)),
        out_shape=[jax.ShapeDtypeStruct(shape, BF16) for shape in shapes],
        grid=(steps,),
        in_specs=[
            pl.BlockSpec((total, high), lambda r: (0, r)),
            full_spec(experts, total, half),
            full_spec(experts, total, half),
            full_spec(total, width),
            pl.BlockSpec((1, total, low), lambda r: (lax.div(r, 2), 0, lax.rem(r, 2))),
        ]
        + ([spread, spread, tall] if added else []),
        out_specs=[spread, spread, tall],
        compiler_params=pltpu.CompilerParams(vmem_limit_bytes=56 * 1024 * 1024),
        cost_estimate=NO_COST,
    )(tokens, gate, up, upstream, used, *added)


def place_kernel(sizes, aliased, meta, block_ref, *refs):
    at = 0
    for size, out in zip(sizes, refs[aliased:]):
        out[...] = block_ref[0, :, at : at + size].astype(F32)
        at += size


def place_line(meta, pieces, sizes, shapes, buffers):
    count, rows, width = pieces.shape
    low = [pl.BlockSpec((rows, size), lambda i, m: (m[4 * i], m[4 * i + 1])) for size in sizes[:-1]]
    low.append(pl.BlockSpec((rows, sizes[-1]), lambda i, m: (m[4 * i + 2], m[4 * i + 3])))
    return pl.pallas_call(
        functools.partial(place_kernel, sizes, len(buffers)),
        out_shape=[jax.ShapeDtypeStruct(shape, F32) for shape in shapes],
        grid_spec=pltpu.PrefetchScalarGridSpec(
            num_scalar_prefetch=1,
            grid=(count,),
            in_specs=[pl.BlockSpec((1, rows, width), lambda i, m: (i, 0, 0))]
            + [pl.BlockSpec(memory_space=pl.ANY)] * len(buffers),
            out_specs=low,
        ),
        input_output_aliases={2 + i: i for i in range(len(buffers))},
        cost_estimate=NO_COST,
    )(meta, pieces, *buffers)


def dense_kernel(count, inner, meta, *refs):
    hidden, mixed, shares, resids = (refs[i * count : (i + 1) * count] for i in range(4))
    outs, scratch = refs[4 * count : -1], refs[-1]
    size, step = shares[0].shape[1], pl.program_id(0)

    def summed(lefts, rights):
        return sum(
            lax.dot_general(
                left[...], right[...], (((0,), (0,)), ((), ())), preferred_element_type=F32
            )
            for left, right in zip(lefts, rights)
        )

    scratch[:, :size] = summed(hidden, shares).astype(BF16)
    scratch[:, size:] = summed(mixed, resids).astype(BF16)
    rows = outs[0].shape[0]
    for k in range(len(outs) // inner):

        @pl.when(lax.rem(meta[0] + k, len(outs) // inner) == step)
        def _():
            for j in range(inner):
                start = pl.multiple_of(lax.rem(meta[1] + j, inner) * rows, rows)
                outs[k * inner + j][...] = scratch[pl.ds(start, rows), :]


def dense_blocks(meta, hidden, mixed, shares, resids, outer, inner):
    count, (length, width), size = len(hidden), hidden[0].shape, shares[0].shape[1]
    high, wide = width // outer, mixed[0].shape[1]
    part = resids[0].shape[1] * wide // width
    per = wide // high
    block = (high // inner, size + part)
    return pl.pallas_call(
        functools.partial(dense_kernel, count, inner),
        out_shape=[jax.ShapeDtypeStruct(block, BF16)] * (outer * inner),
        grid_spec=pltpu.PrefetchScalarGridSpec(
            num_scalar_prefetch=1,
            grid=(outer,),
            in_specs=[pl.BlockSpec((length, high), lambda r, m: (0, r))] * count
            + [pl.BlockSpec((length, high), lambda r, m: (0, lax.rem(r, per)))] * count
            + [full_spec(length, size)] * count
            + [pl.BlockSpec((length, part), lambda r, m: (0, lax.div(r, per)))] * count,
            out_specs=[full_spec(*block)] * (outer * inner),
            scratch_shapes=[pltpu.VMEM((high, size + part), BF16)],
        ),
        compiler_params=pltpu.CompilerParams(vmem_limit_bytes=56 * 1024 * 1024),
        cost_estimate=NO_COST,
    )(meta, *hidden, *mixed, *shares, *resids)


def body(
    activations,
    segments,
    routes,
    route_weights,
    norm_attn_gain,
    norm_ffn_gain,
    query_weight,
    key_matrix,
    value_matrix,
    output_projection_weight,
    expert_gate,
    expert_up,
    expert_down,
    grad_output,
):
    tensor_rank = lax.axis_index("tensor")
    dp_rank = lax.axis_index("dp")
    dp_count = lax.axis_size("dp")
    outer, inner = grid_sizes()
    outer_rank = lax.axis_index("expert") // inner
    inner_rank = lax.axis_index("expert") % inner
    rows, width = activations.shape
    experts_here = expert_gate.shape[0]
    expert_count = experts_here * lax.axis_size("expert")

    named = routes[:, :, None] == jnp.arange(expert_count, dtype=jnp.int32)
    weight_table = jnp.sum(jnp.where(named, route_weights[:, :, None], 0.0), axis=1)
    high = lax.reduce_precision(weight_table, 8, 7)
    middle = lax.reduce_precision(weight_table - high, 8, 7)
    low = weight_table - high - middle
    table = jnp.concatenate([high, middle, low], axis=1).astype(BF16)
    table = jnp.pad(table, ((0, 0), (0, -table.shape[1] % 128)))
    payload = jnp.concatenate([grad_output, table], axis=1)
    up_one, up_three, up_line = shift_outer(payload, 1), shift_outer(payload, -1), inner_line(payload)
    heads_meta = jnp.stack([tensor_rank, dp_rank]).astype(jnp.int32)
    attn_weights = (query_weight, key_matrix, value_matrix, output_projection_weight)
    hidden, q, k, v, mixed, log_total, attn_own, attn_other = attend(
        heads_meta, activations, swap(activations), norm_attn_gain, segments, *attn_weights
    )
    x_own = activations.astype(F32)
    attn_own, attn_other, up_one, up_three, up_line = together(
        attn_own, attn_other, up_one, up_three, up_line
    )
    up_three = inner_line(up_three)
    residual = x_own + attn_own + swap(attn_other)
    normed_two, scale_two = norm_forward(residual, norm_ffn_gain)

    expert_weights = []
    for weights_own in (expert_gate, expert_up, expert_down):
        expert_weights += [weights_own, swap(weights_own)]
    first_expert = lax.axis_index("expert") * experts_here

    h_own = normed_two.astype(BF16)
    h_one, h_line = shift_outer(h_own, 1), inner_line(h_own)
    h_one, h_line, up_one, up_three = together(h_one, h_line, up_one, up_three)
    both = jnp.concatenate([h_one, up_one], axis=1)

    def experts_on(chunk, buffers, blocks, payloads):
        meta = jnp.stack([(outer_rank + chunk) % outer, inner_rank, first_expert])
        made = run_experts(
            meta.astype(jnp.int32), chunk, blocks, payloads, expert_weights, buffers,
            outer * inner * rows, expert_count,
        )
        return list(made[: 8 + inner]), made[8 + inner :]

    def line_sum(parts):
        return inner_sum(parts).astype(BF16)

    others_rows = [shift_dp(activations, step) for step in range(1, dp_count)]
    line, both = inner_line(both), shift_outer(both, 1)
    made = experts_on(0, [], h_line, up_line)
    made, line, both = together(made, line, both)
    buffers, in_zero = made
    made = experts_on(1, buffers, line, line)
    line, both = inner_line(both), shift_outer(both, 1)
    made, line, both = together(made, line, both)
    buffers, parts = made
    made = experts_on(2, buffers, line, line)
    line, sum_one = inner_line(both[:, :width]), line_sum(parts)
    made, line, sum_one = together(made, line, sum_one)
    buffers, parts = made
    sum_one, sum_two = shift_outer(sum_one, -1), line_sum(parts)
    made = experts_on(3, buffers, line, up_three)
    made, sum_one, sum_two, in_zero = together(made, sum_one, sum_two, in_zero)
    buffers, parts = made
    tokens_all, upstream_all, *pairs = buffers
    pairs, mix_lines = pairs[:6], pairs[6:]
    sides = [[pairs[at + half] for at in (0, 2, 4)] for half in range(2)]
    peers = weight_grads(tokens_all, upstream_all, *sides[1], [])
    sum_two, sum_three, sum_zero = shift_outer(sum_two, -2), line_sum(parts), inner_sum(in_zero)
    sum_two, sum_three, sum_zero, peers = together(sum_two, sum_three, sum_zero, peers)
    hidden_all = [hidden]
    for step in range(1, dp_count):
        other = jnp.concatenate([others_rows[step - 1], swap(others_rows[step - 1])], axis=0)
        other = jnp.where(tensor_rank == 0, other, jnp.roll(other, rows, 0)).astype(F32)
        hidden_all.append(norm_forward(other, norm_attn_gain)[0].astype(BF16))
    mix_lines = after(mix_lines, sum_three)
    mix_line = inner_sum(mix_lines)
    sum_three, arrived, hidden_all = together(
        shift_outer(sum_three, -3), [swap(peer) for peer in peers], hidden_all
    )
    grad_h_own = sum_zero.astype(F32)
    for term in (sum_one, sum_two, sum_three):
        grad_h_own = grad_h_own + term.astype(F32)

    def sum_dp(half):
        bit, found = 1, []
        while bit < dp_count:
            found.append(lax.ppermute(half, "dp", [(i, i ^ bit) for i in range(dp_count)]))
            bit *= 2
            if bit < dp_count:
                half = (half.astype(F32) + found.pop().astype(F32)).astype(BF16)
        return half, *found

    def total(pair):
        return sum(t.astype(F32) for t in pair)

    grad_norm_part, _ = norm_backward(residual, scale_two, norm_ffn_gain, grad_h_own)
    grad_resid = grad_output.astype(F32) + grad_norm_part
    resid_own = grad_resid.astype(BF16)
    resid_other = swap(resid_own)
    resid_full = jnp.where(
        tensor_rank == 0,
        jnp.concatenate([resid_own, resid_other], axis=0),
        jnp.concatenate([resid_other, resid_own], axis=0),
    )
    *shares, dh_own, dh_other = attend_back(
        heads_meta, dp_count, resid_full, segments, *attn_weights, q, k, v, mixed, log_total,
    )

    mixed_all = [mixed] + [shift_dp(mixed, step) for step in range(1, dp_count)]
    length, share_width = resid_full.shape[0], width // dp_count

    def columns(index):
        return lax.dynamic_slice_in_dim(resid_full, index * share_width, share_width, 1)

    resid_shares = [columns(dp_rank)]
    for step in range(1, dp_count):
        resid_shares.append(shift_dp(columns((dp_rank + step) % dp_count), step))
    shares, resid_shares = together(shares, resid_shares)
    all_shares = [shares[0]] + [shift_dp(shares[step], step) for step in range(1, dp_count)]
    (all_shares,) = together(all_shares)
    parts = width // mixed.shape[1]
    sizes = [t.shape[1] // dp_count for t in (query_weight, key_matrix, value_matrix)]
    sizes.append(share_width // parts)
    aligned = all(size % 128 == 0 for size in sizes)
    block = width // (outer * inner)
    def row_terms(part, step):
        start = (outer_rank + step) % outer * inner
        return [
            lax.dynamic_slice_in_dim(part, (start + (inner_rank + j) % inner) * block, block, 0)
            for j in range(inner)
        ]

    if aligned:
        meta = jnp.stack([outer_rank, inner_rank]).astype(jnp.int32)
        made = dense_blocks(meta, hidden_all, mixed_all, all_shares, resid_shares, outer, inner)
        terms = [made[k * inner : (k + 1) * inner] for k in range(outer)]
    else:
        qkv_part = dot(
            "sd,sa->da", jnp.concatenate(hidden_all, 0), jnp.concatenate(all_shares, 0), BF16
        )
        mix_part = dot(
            "sa,shb->hab",
            jnp.concatenate(mixed_all, 0),
            jnp.concatenate(resid_shares, 0).reshape(length * dp_count, parts, share_width // parts),
            BF16,
        )
        dense_part = jnp.concatenate([qkv_part, mix_part.reshape(width, -1)], axis=1)
        terms = [row_terms(dense_part, k) for k in range(outer)]
    terms, mix_line, arrived = together(terms, mix_line, arrived)
    mix_line = [mix_line[k * rows : (k + 1) * rows] for k in range(outer)]
    two, dh_other = line_sum(terms[2]), swap(dh_other)
    carried = shift_outer(mix_line[2].astype(BF16), -1)
    halves = weight_grads(tokens_all, upstream_all, *sides[0], arrived)
    two, dh_other, carried, terms, halves, mix_line = together(
        two, dh_other, carried, terms, halves, mix_line
    )
    mix_line[1] = mix_line[1].astype(F32) + carried.astype(F32)
    gate_half, up_half, down_half = halves
    gate_pair = sum_dp(gate_half)
    scale_one = lax.rsqrt(jnp.mean(x_own * x_own, axis=-1, keepdims=True) + EPS)
    grad_x_part, grad_attn_gain = norm_backward(
        x_own, scale_one, norm_attn_gain, dh_own + dh_other
    )
    grad_input = grad_resid + grad_x_part
    late = after((grad_h_own, residual, scale_two), terms)
    grad_ffn_gain = jnp.sum(late[0] * late[1] * late[2], axis=0)
    gains, hops = jnp.stack([grad_attn_gain, grad_ffn_gain]), hops_of_all()
    two, one, three = shift_outer(two, -2), line_sum(terms[1]), line_sum(terms[3])
    two, one, three, terms, gains = together(two, one, three, terms, gains)
    one, three, zero = shift_outer(one, -1), shift_outer(three, -3), inner_sum(terms[0])
    one, three, zero, other, grad_input, gate_pair = together(
        one, three, zero, exchange(gains, hops[0]), grad_input, gate_pair
    )
    gains, hops = gains + other, hops[1:]
    reduced = zero.astype(F32)
    for term in (one, two, three):
        reduced = reduced + term.astype(F32)
    reduced = reduced.astype(BF16)
    shapes = [t.shape for t in (query_weight, key_matrix, value_matrix)] + [(width // parts, width)]

    def block_of(from_one, from_three):
        mix = mix_line[0].astype(F32) + from_one.astype(F32) + from_three.astype(F32)
        return (after(residual, reduced) + mix).astype(BF16)

    mix_one, mix_three = mix_line[1].astype(BF16), mix_line[3].astype(BF16)
    if aligned:
        per, dense = outer * inner // parts, []

        def place(pieces, found, dense):
            meta = []
            for k, j, turn in found:
                index = (outer_rank + k) % outer * inner + (inner_rank + j) % inner
                share = (dp_rank - turn) % dp_count
                meta += [index, share, index % per, share * parts + index // per]
            return place_line(jnp.stack(meta).astype(jnp.int32), pieces, sizes, shapes, dense)

        others = range(1, dp_count)
        step = {
            "line": inner_line(reduced[None]),
            "next": shift_outer(reduced[None]),
            "others": [shift_dp(reduced, turn)[None] for turn in others],
            "gains": exchange(gains, hops[0]),
        }
        (step,) = together(step)
        gains, hops = gains + step["gains"], hops[1:]
        lines = [step["line"]]
        held = jnp.concatenate([step["next"], *step["others"]], axis=0)
        up_pair, down_pair = (sum_dp(after(t, step["others"])) for t in (up_half, down_half))
        for k in range(1, outer + 1):
            step = {"line": inner_line(held), "gains": exchange(gains, hops[0]) if hops else gains}
            if k < outer:
                step["next"] = shift_outer(held if k + 1 < outer else held[1:])
            before = [(k - 1, turn) for turn in ([0] if k == 1 else [0, *others])]
            before = [(at - 1 if turn else at, turn) for at, turn in before]
            made = dense
            for j, pieces in enumerate(lines[-1]):
                made = place(pieces, [(at, j, turn) for at, turn in before], made)
            step["dense"] = made
            if k == 1:
                step["done"] = total(gate_pair)
            if k == 2:
                step["pair"] = up_pair
            if k == 3:
                step["done"] = total(up_pair)
                step["mix"] = shift_outer(after(mix_one, held), -1)
            if k == 4:
                step["pair"], step["mix"] = down_pair, shift_outer(after(mix_three, held), -3)
            (step,) = together(step)
            if hops:
                gains, hops = gains + step["gains"], hops[1:]
            if k == 1:
                gate_sum = step["done"]
            if k == 2:
                up_pair = step["pair"]
            if k == 3:
                up_sum, mix_one = step["done"], step["mix"]
            if k == 4:
                down_sum, block_out = total(step["pair"]), block_of(mix_one, step["mix"])
            dense, held = step["dense"], step.get("next")
            lines.append(step["line"])
        for j, pieces in enumerate(lines[-1]):
            dense = place(pieces, [(outer - 1, j, turn) for turn in others], dense)
    else:
        for hop in hops:
            gains = gains + exchange(gains, hop)
        gate_sum, up_sum, down_sum = (
            total(pair) for pair in (gate_pair, sum_dp(up_half), sum_dp(down_half))
        )
        block_out = block_of(shift_outer(mix_one, -1), shift_outer(mix_three, -3))
        gathered = lax.all_gather(reduced, ("dp", "expert"), axis=0, tiled=True)
        gathered = gathered.reshape(dp_count, width, -1).astype(F32)
        starts = [sum(sizes[:i]) for i in range(len(sizes))]
        dense = [gathered[:, :, at : at + size] for at, size in zip(starts, sizes)]
        dense[:-1] = [t.transpose(1, 0, 2).reshape(width, -1) for t in dense[:-1]]
        mix_w = dense[-1].reshape(dp_count, parts, width // parts, -1)
        dense[-1] = mix_w.transpose(2, 0, 1, 3).reshape(width // parts, width)
    return (
        block_out,
        grad_input,
        gains[0],
        gains[1],
        *dense,
        gate_sum,
        up_sum,
        down_sum,
    )


def solution(mesh):
    tokens = P(("dp", "expert", "tensor"), None)
    whole = P()
    columns = P(None, "tensor")
    hidden_last = P("expert", None, "tensor")
    hidden_mid = P("expert", "tensor", None)
    mixer = P("tensor", None)
    return jax.shard_map(
        body,
        mesh=mesh,
        in_specs=(
            tokens,
            P(("dp", "expert"), None),
            tokens,
            tokens,
            whole,
            whole,
            columns,
            columns,
            columns,
            mixer,
            hidden_last,
            hidden_last,
            hidden_mid,
            tokens,
        ),
        out_specs=(
            tokens,
            tokens,
            whole,
            whole,
            columns,
            columns,
            columns,
            mixer,
            hidden_last,
            hidden_last,
            hidden_mid,
        ),
        check_vma=False,
    )
```

```python
import functools

import jax
import jax.numpy as jnp
import numpy as np
from jax import lax
from jax.experimental import pallas as pl
from jax.experimental.pallas import tpu as pltpu
from jax.sharding import PartitionSpec as P

HEAD_DIM = 64
EPS = 1e-05
ATTN_SCALE = 0.015625
THETA = 10000.0
NEG_FILL = -1e30
F32 = jnp.float32
BF16 = jnp.bfloat16
NO_COST = pl.CostEstimate(flops=1, bytes_accessed=1, transcendentals=0)


def after(values, token):
    return lax.optimization_barrier((values, token))[0]


def swap(values):
    return lax.ppermute(values, "tensor", [(0, 1), (1, 0)])


def shift_dp(values, step):
    count = lax.axis_size("dp")
    return lax.ppermute(values, "dp", [(i, (i + step) % count) for i in range(count)])


def grid_sizes():
    count = lax.axis_size("expert")
    return 4, count // 4


def shift_outer(values, step=1):
    outer, inner = grid_sizes()
    pairs = [(((o + step) % outer) * inner + i, o * inner + i) for o in range(outer) for i in range(inner)]
    return lax.ppermute(values, "expert", pairs)


def shift_inner(values):
    outer, inner = grid_sizes()
    pairs = [(o * inner + (i + 1) % inner, o * inner + i) for o in range(outer) for i in range(inner)]
    return lax.ppermute(values, "expert", pairs)


def inner_line(block):
    line = [block]
    for _ in range(1, grid_sizes()[1]):
        line.append(shift_inner(line[-1]))
    return line


def inner_sum(parts):
    inner, total = len(parts), parts[1 % len(parts)]
    for j in range(2, inner + 1):
        total = shift_inner(total.astype(BF16)).astype(F32) + parts[j % inner].astype(F32)
    return total


def inner_line_of(parts):
    inner, total = len(parts), parts[1 % len(parts)]
    for j in range(2, inner):
        total = shift_inner(total.astype(BF16)).astype(F32) + parts[j].astype(F32)
    return [parts[0]] if inner == 1 else [shift_inner(total.astype(BF16)), parts[0]]


def together(*values):
    return lax.optimization_barrier(values)


def hops_of_all():
    bits = {}
    for axis in ("tensor", "expert", "dp"):
        count = lax.axis_size(axis)
        bits[axis] = [(axis, 1 << i) for i in range(count.bit_length() - 1)]
    return bits["tensor"] + bits["dp"] + bits["expert"]


def exchange(values, hop):
    axis, bit = hop
    return lax.ppermute(values, axis, [(i, i ^ bit) for i in range(lax.axis_size(axis))])


def norm_forward(values, gain_vector):
    inv_scale = lax.rsqrt(jnp.mean(values * values, axis=-1, keepdims=True) + EPS)
    return (values * inv_scale * gain_vector, inv_scale)


def norm_backward(values, inv_scale, gain_vector, upstream):
    weighted = upstream * gain_vector
    inner = jnp.mean(weighted * values, axis=-1, keepdims=True)
    value_gradient = inv_scale * weighted - values * (inv_scale * inv_scale * inv_scale) * inner
    grad_gain = jnp.sum(upstream * values * inv_scale, axis=0)
    return (value_gradient, grad_gain)


def dot(spec, left, right, kind=F32):
    return jnp.einsum(spec, left, right, preferred_element_type=kind)

def dot_t(left, right):
    return lax.dot_general(left, right, (((1,), (1,)), ((), ())), preferred_element_type=F32)


def full_spec(*shape):
    return pl.BlockSpec(shape, lambda *_: (0,) * len(shape))


def rope_tables(length, width):
    half = HEAD_DIM // 2
    frequency = (THETA ** (-np.arange(half, dtype=np.float32) * 2.0 / HEAD_DIM)).astype(np.float32)
    angle = np.arange(length, dtype=np.float32)[:, None] * frequency[None, :]
    cosine, sine = np.cos(angle.astype(np.float64)), np.sin(angle.astype(np.float64))
    cosine = np.concatenate([cosine, cosine], axis=1)
    sine = np.concatenate([-sine, sine], axis=1)
    copies = width // HEAD_DIM
    return np.tile(cosine, (1, copies)).astype(np.float32), np.tile(sine, (1, copies)).astype(np.float32)


def turn(values, cosine, sine):
    width, half = values.shape[1], HEAD_DIM // 2
    copies = width // cosine.shape[1]
    lane = lax.broadcasted_iota(jnp.int32, values.shape, 1)
    first = lax.rem(lane, HEAD_DIM) < half
    other = jnp.where(first, pltpu.roll(values, width - half, 1), pltpu.roll(values, half, 1))
    return values * jnp.concatenate([cosine] * copies, 1) + other * jnp.concatenate([sine] * copies, 1)


def masked_scores(query, key, allowed):
    return jnp.where(allowed, dot_t(query, key) * ATTN_SCALE, NEG_FILL)


def allowed_pairs(segs):
    length = segs.shape[1]
    row = lax.broadcasted_iota(jnp.int32, (length, length), 0)
    column = lax.broadcasted_iota(jnp.int32, (length, length), 1)
    seg_row = segs.astype(F32)
    seg_column = jnp.sum(jnp.where(row == column, seg_row, 0.0), axis=1, keepdims=True)
    return (column <= row) & (seg_row == seg_column)


def row_places(meta, rows):
    own = pl.ds(pl.multiple_of(meta[0] * rows, rows), rows)
    other = pl.ds(pl.multiple_of((1 - meta[0]) * rows, rows), rows)
    return own, other


def attend_kernel(
    meta, own_ref, other_ref, gain_ref, segs, cos_ref, sin_ref, wq, wk, wv, wo,
    hidden_out, q_out, k_out, v_out, mixed_out, log_out, own_out, other_out, x_s, part_s, wo_s, sem,
):
    rows = own_ref.shape[0]
    late = pltpu.make_async_copy(wo, wo_s, sem)
    late.start()
    own, other = row_places(meta, rows)
    x_s[own, :] = own_ref[...].astype(F32)
    x_s[other, :] = other_ref[...].astype(F32)
    x = x_s[...]
    scale = lax.rsqrt(jnp.mean(x * x, axis=-1, keepdims=True) + EPS)
    hidden = (x * scale * gain_ref[...]).astype(BF16)
    hidden_out[...] = hidden
    cosine, sine = cos_ref[...], sin_ref[...]
    q_out[...] = turn(jnp.dot(hidden, wq[...], preferred_element_type=F32), cosine, sine).astype(BF16)
    k_out[...] = turn(jnp.dot(hidden, wk[...], preferred_element_type=F32), cosine, sine).astype(BF16)
    v_out[...] = jnp.dot(hidden, wv[...], preferred_element_type=F32).astype(BF16)
    allowed = allowed_pairs(segs[...])
    heads, heads_kv = wq.shape[1] // HEAD_DIM, wk.shape[1] // HEAD_DIM
    group = heads // heads_kv
    for g in range(heads_kv):
        key = k_out[:, g * HEAD_DIM : (g + 1) * HEAD_DIM]
        value = v_out[:, g * HEAD_DIM : (g + 1) * HEAD_DIM]
        for h in range(g * group, (g + 1) * group):
            at = slice(h * HEAD_DIM, (h + 1) * HEAD_DIM)
            scores = masked_scores(q_out[:, at], key, allowed)
            top = jnp.max(scores, axis=-1, keepdims=True)
            log_total = top + jnp.log(jnp.sum(jnp.exp(scores - top), axis=-1, keepdims=True))
            log_out[:, h : h + 1] = log_total
            prob = jnp.exp(scores - log_total).astype(BF16)
            mixed_out[:, at] = jnp.dot(prob, value, preferred_element_type=F32).astype(BF16)
    late.wait()
    part_s[...] = jnp.dot(mixed_out[...], wo_s[...], preferred_element_type=F32)
    own_out[...] = part_s[own, :]
    other_out[...] = part_s[other, :]


def attend(meta, own, other, gain, segs, wq, wk, wv, wo):
    rows, width = own.shape
    length = segs.shape[1]
    cosine, sine = rope_tables(length, 128)
    operands = (own, other, gain[None, :], segs, cosine, sine, wq, wk, wv, wo)
    shapes = [
        ((length, width), BF16),
        ((length, wq.shape[1]), BF16),
        ((length, wk.shape[1]), BF16),
        ((length, wv.shape[1]), BF16),
        ((length, wq.shape[1]), BF16),
        ((length, 128), F32),
        ((rows, width), F32),
        ((rows, width), F32),
    ]
    return pl.pallas_call(
        attend_kernel,
        out_shape=[jax.ShapeDtypeStruct(*shape) for shape in shapes],
        grid_spec=pltpu.PrefetchScalarGridSpec(
            num_scalar_prefetch=1,
            grid=(1,),
            in_specs=[full_spec(*t.shape) for t in operands[:-1]]
            + [pl.BlockSpec(memory_space=pl.ANY)],
            out_specs=[full_spec(*shape) for shape, _ in shapes],
            scratch_shapes=[pltpu.VMEM((length, width), F32)] * 2
            + [pltpu.VMEM(wo.shape, BF16), pltpu.SemaphoreType.DMA],
        ),
        compiler_params=pltpu.CompilerParams(vmem_limit_bytes=56 * 1024 * 1024),
        cost_estimate=NO_COST,
    )(meta, *operands)


def attend_back_kernel(
    shares, meta, b_ref, segs, cos_ref, sin_ref, wq, wk, wv, wo,
    q_ref, k_ref, v_ref, mixed_ref, log_ref, *refs,
):
    share_outs, (own_out, other_out, grad_s, dq_s, part_s, *late_s, sems) = refs[:shares], refs[shares:]
    late = [
        pltpu.make_async_copy(source, target, sems.at[i])
        for i, (source, target) in enumerate(zip((wq, wk, wv), late_s))
    ]
    for copy in late:
        copy.start()
    own, other = row_places(meta, own_out.shape[0])
    grad_s[...] = dot_t(b_ref[...], wo[...]).astype(BF16)
    cosine, sine = cos_ref[...], -sin_ref[...]
    allowed = allowed_pairs(segs[...])
    wide, narrow = wq.shape[1], wk.shape[1]
    heads, heads_kv = wide // HEAD_DIM, narrow // HEAD_DIM
    group = heads // heads_kv

    def transposed_dot(left, right):
        return lax.dot_general(left, right, (((0,), (0,)), ((), ())), preferred_element_type=F32)

    for g in range(heads_kv):
        there = slice(g * HEAD_DIM, (g + 1) * HEAD_DIM)
        key, value = k_ref[:, there], v_ref[:, there]
        grad_key = grad_value = 0.0
        for h in range(g * group, (g + 1) * group):
            at = slice(h * HEAD_DIM, (h + 1) * HEAD_DIM)
            query, grad = q_ref[:, at], grad_s[:, at]
            prob = jnp.exp(masked_scores(query, key, allowed) - log_ref[:, h : h + 1])
            delta = jnp.sum(grad.astype(F32) * mixed_ref[:, at].astype(F32), axis=-1, keepdims=True)
            grad_scores = (prob * (dot_t(grad, value) - delta) * ATTN_SCALE).astype(BF16)
            dq_s[:, at] = jnp.dot(grad_scores, key, preferred_element_type=F32)
            grad_key = grad_key + transposed_dot(grad_scores, query)
            grad_value = grad_value + transposed_dot(prob.astype(BF16), grad)
        dq_s[:, wide + g * HEAD_DIM : wide + (g + 1) * HEAD_DIM] = grad_key
        at = wide + narrow + g * HEAD_DIM
        dq_s[:, at : at + HEAD_DIM] = grad_value
    dq = turn(dq_s[:, :wide], cosine, sine).astype(BF16)
    dk = turn(dq_s[:, wide : wide + narrow], cosine, sine).astype(BF16)
    dv = dq_s[:, wide + narrow :].astype(BF16)
    for copy in late:
        copy.wait()
    part_s[...] = sum(dot_t(part, held[...]) for part, held in zip((dq, dk, dv), late_s))
    own_out[...] = part_s[own, :]
    other_out[...] = part_s[other, :]
    for r in range(shares):

        @pl.when(meta[1] == r)
        def _():
            for step in range(shares):
                at = 0
                for part in (dq, dk, dv):
                    size = part.shape[1] // shares
                    index = (r + step) % shares
                    share_outs[step][:, at : at + size] = part[:, index * size : (index + 1) * size]
                    at += size


def attend_back(meta, shares, resid, segs, wq, wk, wv, wo, q, k, v, mixed, log_total):
    length, width = resid.shape
    cosine, sine = rope_tables(length, 128)
    operands = (resid, segs, cosine, sine, wq, wk, wv, wo, q, k, v, mixed, log_total)
    columns = wq.shape[1] + wk.shape[1] + wv.shape[1]
    shapes = [((length, columns // shares), BF16)] * shares
    shapes += [((length // 2, width), F32)] * 2
    return pl.pallas_call(
        functools.partial(attend_back_kernel, shares),
        out_shape=[jax.ShapeDtypeStruct(*shape) for shape in shapes],
        grid_spec=pltpu.PrefetchScalarGridSpec(
            num_scalar_prefetch=1,
            grid=(1,),
            in_specs=[
                pl.BlockSpec(memory_space=pl.ANY) if 4 <= i < 7 else full_spec(*t.shape)
                for i, t in enumerate(operands)
            ],
            out_specs=[full_spec(*shape) for shape, _ in shapes],
            scratch_shapes=[
                pltpu.VMEM((length, wq.shape[1]), BF16),
                pltpu.VMEM((length, columns), F32),
                pltpu.VMEM((length, width), F32),
            ]
            + [pltpu.VMEM(t.shape, BF16) for t in (wq, wk, wv)]
            + [pltpu.SemaphoreType.DMA((3,))],
        ),
        compiler_params=pltpu.CompilerParams(vmem_limit_bytes=56 * 1024 * 1024),
        cost_estimate=NO_COST,
    )(meta, *operands)


def expert_kernel(inner, aliased, experts, meta, *refs):
    blocks, ups, tables = (refs[i * inner : (i + 1) * inner] for i in range(3))
    refs = refs[3 * inner :]
    weight_refs, refs = refs[:6], refs[6 + aliased :]
    tokens_out, upstream_out = refs[:2]
    used_out, gate_out, up_out = refs[2:4], refs[4:6], refs[6:8]
    mix_out, in_out = refs[8 : 8 + inner], refs[8 + inner : 8 + 2 * inner]
    table, mix_total, in_total = refs[8 + 2 * inner :]
    rows, width = blocks[0].shape
    expert = pl.program_id(0)

    def place(j):
        return pl.ds(pl.multiple_of(lax.rem(meta[1] + j, inner) * rows, rows), rows)

    @pl.when(expert == 0)
    def _():
        for j in range(inner):
            tokens_out[place(j), :] = blocks[j][...]
            upstream_out[place(j), :] = ups[j][...]
            table[place(j), :] = tables[j][...].astype(F32)
        mix_total[...] = jnp.zeros_like(mix_total)
        in_total[...] = jnp.zeros_like(in_total)

    lane = lax.broadcasted_iota(jnp.int32, table.shape, 1)
    wanted = (lax.rem(lane, experts) == meta[2] + expert) & (lane < 3 * experts)
    weight = jnp.sum(jnp.where(wanted, table[...], 0.0), axis=1, keepdims=True)
    for half in range(2):
        gate, up, down = (weight_refs[2 * i + half][0] for i in range(3))
        pre_gate = jnp.dot(tokens_out[...], gate, preferred_element_type=F32)
        pre_up = jnp.dot(tokens_out[...], up, preferred_element_type=F32)
        grad_act = dot_t(upstream_out[...], down) * weight
        gate_sigmoid = 1.0 / (1.0 + jnp.exp(-pre_gate))
        silu = pre_gate * gate_sigmoid
        used = (silu * pre_up * weight).astype(BF16)
        grad_gate = grad_act * pre_up * gate_sigmoid * (1.0 + pre_gate * (1.0 - gate_sigmoid))
        grad_up = grad_act * silu
        used_out[half][0] = used
        gate_out[half][0] = grad_gate.astype(BF16)
        up_out[half][0] = grad_up.astype(BF16)
        mix_total[...] += jnp.dot(used, down, preferred_element_type=F32)
        in_total[...] += dot_t((grad_gate * weight).astype(BF16), gate) + dot_t(
            (grad_up * weight).astype(BF16), up
        )

    @pl.when(expert == pl.num_programs(0) - 1)
    def _():
        for j in range(inner):
            mix_out[j][...] = mix_total[place(j), :].astype(BF16)
            in_out[j][...] = in_total[place(j), :].astype(BF16)


def run_experts(meta, chunk_index, blocks, payloads, expert_weights, buffers, total, expert_count):
    inner, rows, width = len(blocks), blocks[0].shape[0], expert_weights[0].shape[1]
    firsts = [t.shape[1] // width - 1 for t in payloads]
    experts, half = expert_weights[0].shape[0], expert_weights[0].shape[2]
    chunk = inner * rows
    extra = 128
    by_chunk = pl.BlockSpec((chunk, width), lambda e, m: (m[0], 0))
    per_expert = pl.BlockSpec((1, chunk, half), lambda e, m: (e, m[0], 0))
    spread = pl.BlockSpec((1, width, half), lambda e, m: (e, 0, 0))
    tall = pl.BlockSpec((1, half, width), lambda e, m: (e, 0, 0))
    line = pl.BlockSpec((rows, width), lambda e, m: (chunk_index, 0))
    shapes = [jax.ShapeDtypeStruct((total, width), BF16)] * 2
    shapes += [jax.ShapeDtypeStruct((experts, total, half), BF16)] * 6
    shapes += [jax.ShapeDtypeStruct((total // inner, width), BF16)] * inner
    first = 1 + 3 * inner + 6
    return pl.pallas_call(
        functools.partial(expert_kernel, inner, len(buffers), expert_count),
        out_shape=shapes + [jax.ShapeDtypeStruct((rows, width), BF16)] * inner,
        grid_spec=pltpu.PrefetchScalarGridSpec(
            num_scalar_prefetch=1,
            grid=(experts,),
            in_specs=[full_spec(rows, width)] * inner
            + [pl.BlockSpec((rows, width), lambda e, m, at=at: (0, at)) for at in firsts]
            + [
                pl.BlockSpec((rows, extra), lambda e, m, at=at: (0, (at + 1) * (width // extra)))
                for at in firsts
            ]
            + [spread] * 4
            + [tall] * 2
            + [pl.BlockSpec(memory_space=pl.ANY)] * len(buffers),
            out_specs=[by_chunk] * 2
            + [per_expert] * 6
            + [line] * inner
            + [full_spec(rows, width)] * inner,
            scratch_shapes=[
                pltpu.VMEM((chunk, extra), F32),
                pltpu.VMEM((chunk, width), F32),
                pltpu.VMEM((chunk, width), F32),
            ],
        ),
        input_output_aliases={first + i: i for i in range(len(buffers))},
        compiler_params=pltpu.CompilerParams(vmem_limit_bytes=56 * 1024 * 1024),
        cost_estimate=NO_COST,
    )(meta, *blocks, *payloads, *payloads, *expert_weights, *buffers)


def weight_grads_kernel(count, downs, summed, tokens, *refs):
    sides, down, refs = refs[:count], refs[count : count + downs], refs[count + downs :]
    made = count + (downs > 0)
    added, outs = refs[: made * summed], refs[made * summed :]

    def store(index, at, value):
        if summed:
            value = value + added[index][at].astype(F32)
        outs[index][at] = value.astype(BF16)

    def product(left, right):
        return lax.dot_general(left, right, (((0,), (0,)), ((), ())), preferred_element_type=F32)

    for index, side in enumerate(sides):
        for e in range(side.shape[0]):
            store(index, e, product(tokens[...], side[e]))
    if downs:
        upstream, used = down
        store(count, 0, product(used[0], upstream[...]))


def weight_grads(tokens, sides, down, added):
    (experts, total, half), width = sides[0].shape, tokens.shape[1]
    steps = 2 * experts
    high, low = width // steps, half // 2
    spread = pl.BlockSpec((experts, high, half), lambda r: (0, r, 0))
    tall = pl.BlockSpec((1, low, width), lambda r: (lax.div(r, 2), lax.rem(r, 2), 0))
    specs = [spread] * len(sides) + [tall] * (len(down) > 0)
    shapes = [(experts, width, half)] * len(sides) + [(experts, half, width)] * (len(down) > 0)
    down_specs = [
        full_spec(total, width),
        pl.BlockSpec((1, total, low), lambda r: (lax.div(r, 2), 0, lax.rem(r, 2))),
    ]
    return pl.pallas_call(
        functools.partial(weight_grads_kernel, len(sides), len(down), len(added) > 0),
        out_shape=[jax.ShapeDtypeStruct(shape, BF16) for shape in shapes],
        grid=(steps,),
        in_specs=[pl.BlockSpec((total, high), lambda r: (0, r))]
        + [full_spec(experts, total, half)] * len(sides)
        + down_specs[: len(down)]
        + specs * (len(added) > 0),
        out_specs=specs,
        compiler_params=pltpu.CompilerParams(vmem_limit_bytes=56 * 1024 * 1024),
        cost_estimate=NO_COST,
    )(tokens, *sides, *down, *added)


def place_kernel(sizes, aliased, meta, block_ref, *refs):
    at = 0
    for size, out in zip(sizes, refs[aliased:]):
        out[...] = block_ref[0, :, at : at + size].astype(F32)
        at += size


def place_line(meta, pieces, sizes, shapes, buffers):
    count, rows, width = pieces.shape
    low = [pl.BlockSpec((rows, size), lambda i, m: (m[4 * i], m[4 * i + 1])) for size in sizes[:-1]]
    low.append(pl.BlockSpec((rows, sizes[-1]), lambda i, m: (m[4 * i + 2], m[4 * i + 3])))
    return pl.pallas_call(
        functools.partial(place_kernel, sizes, len(buffers)),
        out_shape=[jax.ShapeDtypeStruct(shape, F32) for shape in shapes],
        grid_spec=pltpu.PrefetchScalarGridSpec(
            num_scalar_prefetch=1,
            grid=(count,),
            in_specs=[pl.BlockSpec((1, rows, width), lambda i, m: (i, 0, 0))]
            + [pl.BlockSpec(memory_space=pl.ANY)] * len(buffers),
            out_specs=low,
        ),
        input_output_aliases={2 + i: i for i in range(len(buffers))},
        cost_estimate=NO_COST,
    )(meta, pieces, *buffers)


def dense_kernel(count, inner, meta, *refs):
    hidden, mixed, shares, resids = (refs[i * count : (i + 1) * count] for i in range(4))
    outs, scratch = refs[4 * count : -1], refs[-1]
    size, step = shares[0].shape[1], pl.program_id(0)

    def summed(lefts, rights):
        return sum(
            lax.dot_general(
                left[...], right[...], (((0,), (0,)), ((), ())), preferred_element_type=F32
            )
            for left, right in zip(lefts, rights)
        )

    scratch[:, :size] = summed(hidden, shares).astype(BF16)
    scratch[:, size:] = summed(mixed, resids).astype(BF16)
    rows = outs[0].shape[0]
    for k in range(len(outs) // inner):

        @pl.when(step == k)
        def _():
            for j in range(inner):
                start = pl.multiple_of(lax.rem(meta[0] + j, inner) * rows, rows)
                outs[k * inner + j][...] = scratch[pl.ds(start, rows), :]


def dense_blocks(meta, hidden, mixed, shares, resids, outer, inner):
    count, (length, width), size = len(hidden), hidden[0].shape, shares[0].shape[1]
    high, wide, steps = width // outer, mixed[0].shape[1], meta.shape[0] - 1
    part = resids[0].shape[1] * wide // width
    per = wide // high
    block = (high // inner, size + part)
    made = pl.pallas_call(
        functools.partial(dense_kernel, count, inner),
        out_shape=[jax.ShapeDtypeStruct(block, BF16)] * (steps * inner),
        grid_spec=pltpu.PrefetchScalarGridSpec(
            num_scalar_prefetch=1,
            grid=(steps,),
            in_specs=[pl.BlockSpec((length, high), lambda i, m: (0, m[1 + i]))] * count
            + [pl.BlockSpec((length, high), lambda i, m: (0, lax.rem(m[1 + i], per)))] * count
            + [full_spec(length, size)] * count
            + [pl.BlockSpec((length, part), lambda i, m: (0, lax.div(m[1 + i], per)))] * count,
            out_specs=[full_spec(*block)] * (steps * inner),
            scratch_shapes=[pltpu.VMEM((high, size + part), BF16)],
        ),
        compiler_params=pltpu.CompilerParams(vmem_limit_bytes=56 * 1024 * 1024),
        cost_estimate=NO_COST,
    )(meta, *hidden, *mixed, *shares, *resids)
    return [made[i * inner : (i + 1) * inner] for i in range(steps)]


def body(
    activations,
    segments,
    routes,
    route_weights,
    norm_attn_gain,
    norm_ffn_gain,
    query_weight,
    key_matrix,
    value_matrix,
    output_projection_weight,
    expert_gate,
    expert_up,
    expert_down,
    grad_output,
):
    tensor_rank = lax.axis_index("tensor")
    dp_rank = lax.axis_index("dp")
    dp_count = lax.axis_size("dp")
    outer, inner = grid_sizes()
    outer_rank = lax.axis_index("expert") // inner
    inner_rank = lax.axis_index("expert") % inner
    rows, width = activations.shape
    experts_here = expert_gate.shape[0]
    expert_count = experts_here * lax.axis_size("expert")

    named = routes[:, :, None] == jnp.arange(expert_count, dtype=jnp.int32)
    weight_table = jnp.sum(jnp.where(named, route_weights[:, :, None], 0.0), axis=1)
    high = lax.reduce_precision(weight_table, 8, 7)
    middle = lax.reduce_precision(weight_table - high, 8, 7)
    low = weight_table - high - middle
    table = jnp.concatenate([high, middle, low], axis=1).astype(BF16)
    table = jnp.pad(table, ((0, 0), (0, -table.shape[1] % 128)))
    payload = jnp.concatenate([grad_output, table], axis=1)
    up_one, up_three, up_line = shift_outer(payload, 1), shift_outer(payload, -1), inner_line(payload)
    heads_meta = jnp.stack([tensor_rank, dp_rank]).astype(jnp.int32)
    attn_weights = (query_weight, key_matrix, value_matrix, output_projection_weight)
    hidden, q, k, v, mixed, log_total, attn_own, attn_other = attend(
        heads_meta, activations, swap(activations), norm_attn_gain, segments, *attn_weights
    )
    x_own = activations.astype(F32)
    attn_own, attn_other, up_one, up_three, up_line = together(
        attn_own, attn_other, up_one, up_three, up_line
    )
    up_three = inner_line(up_three)
    residual = x_own + attn_own + swap(attn_other)
    normed_two, scale_two = norm_forward(residual, norm_ffn_gain)

    expert_weights = []
    for weights_own in (expert_gate, expert_up, expert_down):
        expert_weights += [weights_own, swap(weights_own)]
    first_expert = lax.axis_index("expert") * experts_here

    h_own = normed_two.astype(BF16)
    h_one, h_line = shift_outer(h_own, 1), inner_line(h_own)
    h_one, h_line, up_one, up_three = together(h_one, h_line, up_one, up_three)
    both = jnp.concatenate([h_one, up_one], axis=1)

    def experts_on(chunk, buffers, blocks, payloads):
        meta = jnp.stack([(outer_rank + chunk) % outer, inner_rank, first_expert])
        made = run_experts(
            meta.astype(jnp.int32), chunk, blocks, payloads, expert_weights, buffers,
            outer * inner * rows, expert_count,
        )
        return list(made[: 8 + inner]), made[8 + inner :]

    def line_sum(parts):
        return inner_sum(parts).astype(BF16)

    others_rows = [shift_dp(activations, step) for step in range(1, dp_count)]
    line, both = inner_line(both), shift_outer(both, 1)
    made = experts_on(0, [], h_line, up_line)
    made, line, both, others_rows = together(made, line, both, others_rows)
    buffers, in_zero = made
    others_swapped = [swap(t) for t in others_rows]
    made = experts_on(1, buffers, line, line)
    line, both = inner_line(both), shift_outer(both, 1)
    mixed_all = [mixed] + [shift_dp(mixed, step) for step in range(1, dp_count)]
    made, line, both, mixed_all, others_swapped = together(
        made, line, both, mixed_all, others_swapped
    )
    buffers, parts = made
    made = experts_on(2, buffers, line, line)
    line, sum_one = inner_line(both[:, :width]), line_sum(parts)
    hidden_all = [hidden]
    for step in range(1, dp_count):
        other = jnp.concatenate([others_rows[step - 1], others_swapped[step - 1]], axis=0)
        other = jnp.where(tensor_rank == 0, other, jnp.roll(other, rows, 0)).astype(F32)
        hidden_all.append(norm_forward(other, norm_attn_gain)[0].astype(BF16))
    made, line, sum_one, hidden_all = together(made, line, sum_one, hidden_all)
    buffers, parts = made
    sum_one, sum_two = shift_outer(sum_one, -1), line_sum(parts)
    made = experts_on(3, buffers, line, up_three)
    made, sum_one, sum_two, in_zero = together(made, sum_one, sum_two, in_zero)
    buffers, parts = made
    tokens_all, upstream_all, *pairs = buffers
    pairs, mix_lines = pairs[:6], pairs[6:]
    sides = [[pairs[at + half] for at in (0, 2, 4)] for half in range(2)]
    peers = weight_grads(tokens_all, sides[1][1:], (upstream_all, sides[1][0]), [])
    sum_two, sum_three, sum_zero = shift_outer(sum_two, -2), line_sum(parts), inner_sum(in_zero)
    sum_two, sum_three, sum_zero, peers = together(sum_two, sum_three, sum_zero, peers)
    mix_lines = after(mix_lines, sum_three)
    mix_found = inner_line_of(mix_lines)
    sum_three, arrived = together(shift_outer(sum_three, -3), [swap(peer) for peer in peers])
    grad_h_own = sum_zero.astype(F32)
    for term in (sum_one, sum_two, sum_three):
        grad_h_own = grad_h_own + term.astype(F32)

    def sum_dp(half):
        bit, found = 1, []
        while bit < dp_count:
            found.append(lax.ppermute(half, "dp", [(i, i ^ bit) for i in range(dp_count)]))
            bit *= 2
            if bit < dp_count:
                half = (half.astype(F32) + found.pop().astype(F32)).astype(BF16)
        return half, *found

    def total(pair):
        return sum(t.astype(F32) for t in pair)

    grad_norm_part, _ = norm_backward(residual, scale_two, norm_ffn_gain, grad_h_own)
    grad_resid = grad_output.astype(F32) + grad_norm_part
    resid_own = grad_resid.astype(BF16)
    resid_other = swap(resid_own)
    resid_full = jnp.where(
        tensor_rank == 0,
        jnp.concatenate([resid_own, resid_other], axis=0),
        jnp.concatenate([resid_other, resid_own], axis=0),
    )
    *shares, dh_own, dh_other = attend_back(
        heads_meta, dp_count, resid_full, segments, *attn_weights, q, k, v, mixed, log_total,
    )

    length, share_width = resid_full.shape[0], width // dp_count

    def columns(index):
        return lax.dynamic_slice_in_dim(resid_full, index * share_width, share_width, 1)

    resid_shares = [columns(dp_rank)]
    for step in range(1, dp_count):
        resid_shares.append(shift_dp(columns((dp_rank + step) % dp_count), step))
    shares, resid_shares = together(shares, resid_shares)
    all_shares = [shares[0]] + [shift_dp(shares[step], step) for step in range(1, dp_count)]
    parts = width // mixed.shape[1]
    sizes = [t.shape[1] // dp_count for t in (query_weight, key_matrix, value_matrix)]
    sizes.append(share_width // parts)
    aligned = all(size % 128 == 0 for size in sizes)
    (gate_half,) = weight_grads(tokens_all, sides[0][1:2], [], arrived[:1])
    all_shares, gate_half = together(all_shares, gate_half)
    block = width // (outer * inner)
    def row_terms(part, step):
        start = (outer_rank + step) % outer * inner
        return [
            lax.dynamic_slice_in_dim(part, (start + (inner_rank + j) % inner) * block, block, 0)
            for j in range(inner)
        ]

    if aligned:

        def blocks_of(steps, all_shares):
            meta = jnp.stack([inner_rank] + [(outer_rank + k) % outer for k in steps])
            return dense_blocks(
                meta.astype(jnp.int32), hidden_all, mixed_all, all_shares, resid_shares, outer, inner
            )

        terms = [None, None, *blocks_of([2], all_shares), None]
    else:
        qkv_part = dot(
            "sd,sa->da", jnp.concatenate(hidden_all, 0), jnp.concatenate(all_shares, 0), BF16
        )
        mix_part = dot(
            "sa,shb->hab",
            jnp.concatenate(mixed_all, 0),
            jnp.concatenate(resid_shares, 0).reshape(length * dp_count, parts, share_width // parts),
            BF16,
        )
        dense_part = jnp.concatenate([qkv_part, mix_part.reshape(width, -1)], axis=1)
        terms = [row_terms(dense_part, k) for k in range(outer)]
    terms[2], mix_found, arrived = together(terms[2], mix_found, arrived)
    mix_line = [
        sum(t[k * rows : (k + 1) * rows].astype(F32) for t in mix_found) for k in range(outer)
    ]
    two, dh_other = line_sum(terms[2]), swap(dh_other)
    carried = shift_outer(mix_line[2].astype(BF16), -1)
    if aligned:
        terms[1], terms[3], terms[0] = blocks_of([1, 3, 0], after(all_shares, terms[2]))
    two, dh_other, terms, arrived = together(two, dh_other, terms, arrived)
    gate_pair = sum_dp(after(gate_half, two))
    scale_one = lax.rsqrt(jnp.mean(x_own * x_own, axis=-1, keepdims=True) + EPS)
    grad_x_part, grad_attn_gain = norm_backward(
        x_own, scale_one, norm_attn_gain, dh_own + dh_other
    )
    grad_input = grad_resid + grad_x_part
    late = after((grad_h_own, residual, scale_two), terms)
    grad_ffn_gain = jnp.sum(late[0] * late[1] * late[2], axis=0)
    gains, hops = jnp.stack([grad_attn_gain, grad_ffn_gain]), hops_of_all()
    two, one, three = shift_outer(two, -2), line_sum(terms[1]), line_sum(terms[3])
    halves = weight_grads(tokens_all, sides[0][2:], (upstream_all, sides[0][0]), arrived[1:])
    two, one, three, terms, gains, carried, halves = together(
        two, one, three, terms, gains, carried, halves
    )
    mix_line[1] = mix_line[1].astype(F32) + carried.astype(F32)
    up_half, down_half = halves
    one, three, zero = shift_outer(one, -1), shift_outer(three, -3), inner_sum(terms[0])
    one, three, zero, other, grad_input, gate_pair = together(
        one, three, zero, exchange(gains, hops[0]), grad_input, gate_pair
    )
    gains, hops = gains + other, hops[1:]
    reduced = zero.astype(F32)
    for term in (one, two, three):
        reduced = reduced + term.astype(F32)
    reduced = reduced.astype(BF16)
    shapes = [t.shape for t in (query_weight, key_matrix, value_matrix)] + [(width // parts, width)]

    def block_of(from_one, from_three):
        mix = mix_line[0].astype(F32) + from_one.astype(F32) + from_three.astype(F32)
        return (after(residual, reduced) + mix).astype(BF16)

    mix_one, mix_three = mix_line[1].astype(BF16), mix_line[3].astype(BF16)
    if aligned:
        per, dense = outer * inner // parts, []

        def place(pieces, found, dense):
            meta = []
            for k, j, turn in found:
                index = (outer_rank + k) % outer * inner + (inner_rank + j) % inner
                share = (dp_rank - turn) % dp_count
                meta += [index, share, index % per, share * parts + index // per]
            return place_line(jnp.stack(meta).astype(jnp.int32), pieces, sizes, shapes, dense)

        others = range(1, dp_count)
        step = {
            "line": inner_line(reduced[None]),
            "next": shift_outer(reduced[None]),
            "others": [shift_dp(reduced, turn)[None] for turn in others],
            "gains": exchange(gains, hops[0]),
        }
        (step,) = together(step)
        gains, hops = gains + step["gains"], hops[1:]
        lines = [step["line"]]
        held = jnp.concatenate([step["next"], *step["others"]], axis=0)
        up_pair, down_pair = (sum_dp(after(t, step["others"])) for t in (up_half, down_half))
        for k in range(1, outer + 1):
            step = {"line": inner_line(held), "gains": exchange(gains, hops[0]) if hops else gains}
            if k < outer:
                step["next"] = shift_outer(held if k + 1 < outer else held[1:])
            before = [(k - 1, turn) for turn in ([0] if k == 1 else [0, *others])]
            before = [(at - 1 if turn else at, turn) for at, turn in before]
            made = dense
            for j, pieces in enumerate(lines[-1]):
                made = place(pieces, [(at, j, turn) for at, turn in before], made)
            if k == outer:
                made = place(held, [(outer - 1, 0, turn) for turn in others], made)
            step["dense"] = made
            if k == 1:
                step["done"] = total(gate_pair)
            if k == 2:
                step["pair"] = up_pair
            if k == 3:
                step["done"] = total(up_pair)
                step["mix"] = shift_outer(after(mix_one, held), -1)
            if k == 4:
                step["done"] = total(after(down_pair, made))
                step["mix"] = shift_outer(after(mix_three, held), -3)
            (step,) = together(step)
            if hops:
                gains, hops = gains + step["gains"], hops[1:]
            if k == 1:
                gate_sum = step["done"]
            if k == 2:
                up_pair = step["pair"]
            if k == 3:
                up_sum, mix_one = step["done"], step["mix"]
            if k == 4:
                down_sum, block_out = step["done"], block_of(mix_one, step["mix"])
            dense, held = step["dense"], step.get("next")
            lines.append(step["line"])
        for j in range(1, inner):
            dense = place(lines[-1][j], [(outer - 1, j, turn) for turn in others], dense)
    else:
        for hop in hops:
            gains = gains + exchange(gains, hop)
        gate_sum, up_sum, down_sum = (
            total(pair) for pair in (gate_pair, sum_dp(up_half), sum_dp(down_half))
        )
        block_out = block_of(shift_outer(mix_one, -1), shift_outer(mix_three, -3))
        gathered = lax.all_gather(reduced, ("dp", "expert"), axis=0, tiled=True)
        gathered = gathered.reshape(dp_count, width, -1).astype(F32)
        starts = [sum(sizes[:i]) for i in range(len(sizes))]
        dense = [gathered[:, :, at : at + size] for at, size in zip(starts, sizes)]
        dense[:-1] = [t.transpose(1, 0, 2).reshape(width, -1) for t in dense[:-1]]
        mix_w = dense[-1].reshape(dp_count, parts, width // parts, -1)
        dense[-1] = mix_w.transpose(2, 0, 1, 3).reshape(width // parts, width)
    return (
        block_out,
        grad_input,
        gains[0],
        gains[1],
        *dense,
        gate_sum,
        up_sum,
        down_sum,
    )


def solution(mesh):
    tokens = P(("dp", "expert", "tensor"), None)
    whole = P()
    columns = P(None, "tensor")
    hidden_last = P("expert", None, "tensor")
    hidden_mid = P("expert", "tensor", None)
    mixer = P("tensor", None)
    return jax.shard_map(
        body,
        mesh=mesh,
        in_specs=(
            tokens,
            P(("dp", "expert"), None),
            tokens,
            tokens,
            whole,
            whole,
            columns,
            columns,
            columns,
            mixer,
            hidden_last,
            hidden_last,
            hidden_mid,
            tokens,
        ),
        out_specs=(
            tokens,
            tokens,
            whole,
            whole,
            columns,
            columns,
            columns,
            mixer,
            hidden_last,
            hidden_last,
            hidden_mid,
        ),
        check_vma=False,
    )
```

```python
import functools

import jax
import jax.numpy as jnp
import numpy as np
from jax import lax
from jax.experimental import pallas as pl
from jax.experimental.pallas import tpu as pltpu
from jax.sharding import PartitionSpec as P

HEAD_DIM = 64
EPS = 1e-05
ATTN_SCALE = 0.015625
THETA = 10000.0
NEG_FILL = -1e30
F32 = jnp.float32
BF16 = jnp.bfloat16
NO_COST = pl.CostEstimate(flops=1, bytes_accessed=1, transcendentals=0)


def after(values, token):
    return lax.optimization_barrier((values, token))[0]


def swap(values):
    return lax.ppermute(values, "tensor", [(0, 1), (1, 0)])


def shift_dp(values, step):
    count = lax.axis_size("dp")
    return lax.ppermute(values, "dp", [(i, (i + step) % count) for i in range(count)])


def grid_sizes():
    count = lax.axis_size("expert")
    return 4, count // 4


def shift_outer(values, step=1):
    outer, inner = grid_sizes()
    pairs = [(((o + step) % outer) * inner + i, o * inner + i) for o in range(outer) for i in range(inner)]
    return lax.ppermute(values, "expert", pairs)


def shift_inner(values):
    outer, inner = grid_sizes()
    pairs = [(o * inner + (i + 1) % inner, o * inner + i) for o in range(outer) for i in range(inner)]
    return lax.ppermute(values, "expert", pairs)


def inner_line(block):
    line = [block]
    for _ in range(1, grid_sizes()[1]):
        line.append(shift_inner(line[-1]))
    return line


def inner_sum(parts):
    inner, total = len(parts), parts[1 % len(parts)]
    for j in range(2, inner + 1):
        total = shift_inner(total.astype(BF16)).astype(F32) + parts[j % inner].astype(F32)
    return total


def inner_line_of(parts):
    inner, total = len(parts), parts[1 % len(parts)]
    for j in range(2, inner):
        total = shift_inner(total.astype(BF16)).astype(F32) + parts[j].astype(F32)
    return [parts[0]] if inner == 1 else [shift_inner(total.astype(BF16)), parts[0]]


def together(*values):
    return lax.optimization_barrier(values)


def hops_of_all():
    bits = {}
    for axis in ("tensor", "expert", "dp"):
        count = lax.axis_size(axis)
        bits[axis] = [(axis, 1 << i) for i in range(count.bit_length() - 1)]
    return bits["tensor"] + bits["dp"] + bits["expert"]


def exchange(values, hop):
    axis, bit = hop
    return lax.ppermute(values, axis, [(i, i ^ bit) for i in range(lax.axis_size(axis))])


def norm_forward(values, gain_vector):
    inv_scale = lax.rsqrt(jnp.mean(values * values, axis=-1, keepdims=True) + EPS)
    return (values * inv_scale * gain_vector, inv_scale)


def norm_backward(values, inv_scale, gain_vector, upstream):
    weighted = upstream * gain_vector
    inner = jnp.mean(weighted * values, axis=-1, keepdims=True)
    value_gradient = inv_scale * weighted - values * (inv_scale * inv_scale * inv_scale) * inner
    grad_gain = jnp.sum(upstream * values * inv_scale, axis=0)
    return (value_gradient, grad_gain)


def dot(spec, left, right, kind=F32):
    return jnp.einsum(spec, left, right, preferred_element_type=kind)

def dot_t(left, right):
    return lax.dot_general(left, right, (((1,), (1,)), ((), ())), preferred_element_type=F32)


def full_spec(*shape):
    return pl.BlockSpec(shape, lambda *_: (0,) * len(shape))


def rope_tables(length, width):
    half = HEAD_DIM // 2
    frequency = (THETA ** (-np.arange(half, dtype=np.float32) * 2.0 / HEAD_DIM)).astype(np.float32)
    angle = np.arange(length, dtype=np.float32)[:, None] * frequency[None, :]
    cosine, sine = np.cos(angle.astype(np.float64)), np.sin(angle.astype(np.float64))
    cosine = np.concatenate([cosine, cosine], axis=1)
    sine = np.concatenate([-sine, sine], axis=1)
    copies = width // HEAD_DIM
    return np.tile(cosine, (1, copies)).astype(np.float32), np.tile(sine, (1, copies)).astype(np.float32)


def turn(values, cosine, sine):
    width, half = values.shape[1], HEAD_DIM // 2
    copies = width // cosine.shape[1]
    lane = lax.broadcasted_iota(jnp.int32, values.shape, 1)
    first = lax.rem(lane, HEAD_DIM) < half
    other = jnp.where(first, pltpu.roll(values, width - half, 1), pltpu.roll(values, half, 1))
    return values * jnp.concatenate([cosine] * copies, 1) + other * jnp.concatenate([sine] * copies, 1)


def masked_scores(query, key, allowed):
    return jnp.where(allowed, dot_t(query, key) * ATTN_SCALE, NEG_FILL)


def allowed_pairs(segs):
    length = segs.shape[1]
    row = lax.broadcasted_iota(jnp.int32, (length, length), 0)
    column = lax.broadcasted_iota(jnp.int32, (length, length), 1)
    seg_row = segs.astype(F32)
    seg_column = jnp.sum(jnp.where(row == column, seg_row, 0.0), axis=1, keepdims=True)
    return (column <= row) & (seg_row == seg_column)


def row_places(meta, rows):
    own = pl.ds(pl.multiple_of(meta[0] * rows, rows), rows)
    other = pl.ds(pl.multiple_of((1 - meta[0]) * rows, rows), rows)
    return own, other


def attend_kernel(
    meta, own_ref, other_ref, gain_ref, segs, cos_ref, sin_ref, wq, wk, wv, wo,
    hidden_out, q_out, k_out, v_out, mixed_out, log_out, own_out, other_out, x_s, part_s, wo_s, sem,
):
    rows = own_ref.shape[0]
    late = pltpu.make_async_copy(wo, wo_s, sem)
    late.start()
    own, other = row_places(meta, rows)
    x_s[own, :] = own_ref[...].astype(F32)
    x_s[other, :] = other_ref[...].astype(F32)
    x = x_s[...]
    scale = lax.rsqrt(jnp.mean(x * x, axis=-1, keepdims=True) + EPS)
    hidden = (x * scale * gain_ref[...]).astype(BF16)
    hidden_out[...] = hidden
    cosine, sine = cos_ref[...], sin_ref[...]
    q_out[...] = turn(jnp.dot(hidden, wq[...], preferred_element_type=F32), cosine, sine).astype(BF16)
    k_out[...] = turn(jnp.dot(hidden, wk[...], preferred_element_type=F32), cosine, sine).astype(BF16)
    v_out[...] = jnp.dot(hidden, wv[...], preferred_element_type=F32).astype(BF16)
    allowed = allowed_pairs(segs[...])
    heads, heads_kv = wq.shape[1] // HEAD_DIM, wk.shape[1] // HEAD_DIM
    group = heads // heads_kv
    for g in range(heads_kv):
        key = k_out[:, g * HEAD_DIM : (g + 1) * HEAD_DIM]
        value = v_out[:, g * HEAD_DIM : (g + 1) * HEAD_DIM]
        for h in range(g * group, (g + 1) * group):
            at = slice(h * HEAD_DIM, (h + 1) * HEAD_DIM)
            scores = masked_scores(q_out[:, at], key, allowed)
            top = jnp.max(scores, axis=-1, keepdims=True)
            log_total = top + jnp.log(jnp.sum(jnp.exp(scores - top), axis=-1, keepdims=True))
            log_out[:, h : h + 1] = log_total
            prob = jnp.exp(scores - log_total).astype(BF16)
            mixed_out[:, at] = jnp.dot(prob, value, preferred_element_type=F32).astype(BF16)
    late.wait()
    part_s[...] = jnp.dot(mixed_out[...], wo_s[...], preferred_element_type=F32)
    own_out[...] = part_s[own, :]
    other_out[...] = part_s[other, :]


def attend(meta, own, other, gain, segs, wq, wk, wv, wo):
    rows, width = own.shape
    length = segs.shape[1]
    cosine, sine = rope_tables(length, 128)
    operands = (own, other, gain, segs, cosine, sine, wq, wk, wv, wo)
    shapes = [
        ((length, width), BF16),
        ((length, wq.shape[1]), BF16),
        ((length, wk.shape[1]), BF16),
        ((length, wv.shape[1]), BF16),
        ((length, wq.shape[1]), BF16),
        ((length, 128), F32),
        ((rows, width), F32),
        ((rows, width), F32),
    ]
    return pl.pallas_call(
        attend_kernel,
        out_shape=[jax.ShapeDtypeStruct(*shape) for shape in shapes],
        grid_spec=pltpu.PrefetchScalarGridSpec(
            num_scalar_prefetch=1,
            grid=(1,),
            in_specs=[full_spec(*t.shape) for t in operands[:-1]]
            + [pl.BlockSpec(memory_space=pl.ANY)],
            out_specs=[full_spec(*shape) for shape, _ in shapes],
            scratch_shapes=[pltpu.VMEM((length, width), F32)] * 2
            + [pltpu.VMEM(wo.shape, BF16), pltpu.SemaphoreType.DMA],
        ),
        compiler_params=pltpu.CompilerParams(vmem_limit_bytes=56 * 1024 * 1024),
        cost_estimate=NO_COST,
    )(meta, *operands)


def attend_back_kernel(
    shares, meta, b_ref, segs, cos_ref, sin_ref, wq, wk, wv, wo,
    q_ref, k_ref, v_ref, mixed_ref, log_ref, *refs,
):
    share_outs, (own_out, other_out, grad_s, dq_s, part_s, *late_s, sems) = refs[:shares], refs[shares:]
    late = [
        pltpu.make_async_copy(source, target, sems.at[i])
        for i, (source, target) in enumerate(zip((wq, wk, wv), late_s))
    ]
    for copy in late:
        copy.start()
    own, other = row_places(meta, own_out.shape[0])
    grad_s[...] = dot_t(b_ref[...], wo[...]).astype(BF16)
    cosine, sine = cos_ref[...], -sin_ref[...]
    allowed = allowed_pairs(segs[...])
    wide, narrow = wq.shape[1], wk.shape[1]
    heads, heads_kv = wide // HEAD_DIM, narrow // HEAD_DIM
    group = heads // heads_kv

    def transposed_dot(left, right):
        return lax.dot_general(left, right, (((0,), (0,)), ((), ())), preferred_element_type=F32)

    for g in range(heads_kv):
        there = slice(g * HEAD_DIM, (g + 1) * HEAD_DIM)
        key, value = k_ref[:, there], v_ref[:, there]
        grad_key = grad_value = 0.0
        for h in range(g * group, (g + 1) * group):
            at = slice(h * HEAD_DIM, (h + 1) * HEAD_DIM)
            query, grad = q_ref[:, at], grad_s[:, at]
            prob = jnp.exp(masked_scores(query, key, allowed) - log_ref[:, h : h + 1])
            delta = jnp.sum(grad.astype(F32) * mixed_ref[:, at].astype(F32), axis=-1, keepdims=True)
            grad_scores = (prob * (dot_t(grad, value) - delta) * ATTN_SCALE).astype(BF16)
            dq_s[:, at] = jnp.dot(grad_scores, key, preferred_element_type=F32)
            grad_key = grad_key + transposed_dot(grad_scores, query)
            grad_value = grad_value + transposed_dot(prob.astype(BF16), grad)
        dq_s[:, wide + g * HEAD_DIM : wide + (g + 1) * HEAD_DIM] = grad_key
        at = wide + narrow + g * HEAD_DIM
        dq_s[:, at : at + HEAD_DIM] = grad_value
    dq = turn(dq_s[:, :wide], cosine, sine).astype(BF16)
    dk = turn(dq_s[:, wide : wide + narrow], cosine, sine).astype(BF16)
    dv = dq_s[:, wide + narrow :].astype(BF16)
    for copy in late:
        copy.wait()
    part_s[...] = sum(dot_t(part, held[...]) for part, held in zip((dq, dk, dv), late_s))
    own_out[...] = part_s[own, :]
    other_out[...] = part_s[other, :]
    for r in range(shares):

        @pl.when(meta[1] == r)
        def _():
            for step in range(shares):
                at = 0
                for part in (dq, dk, dv):
                    size = part.shape[1] // shares
                    index = (r + step) % shares
                    share_outs[step][:, at : at + size] = part[:, index * size : (index + 1) * size]
                    at += size


def attend_back(meta, shares, resid, segs, wq, wk, wv, wo, q, k, v, mixed, log_total):
    length, width = resid.shape
    cosine, sine = rope_tables(length, 128)
    operands = (resid, segs, cosine, sine, wq, wk, wv, wo, q, k, v, mixed, log_total)
    columns = wq.shape[1] + wk.shape[1] + wv.shape[1]
    shapes = [((length, columns // shares), BF16)] * shares
    shapes += [((length // 2, width), F32)] * 2
    return pl.pallas_call(
        functools.partial(attend_back_kernel, shares),
        out_shape=[jax.ShapeDtypeStruct(*shape) for shape in shapes],
        grid_spec=pltpu.PrefetchScalarGridSpec(
            num_scalar_prefetch=1,
            grid=(1,),
            in_specs=[
                pl.BlockSpec(memory_space=pl.ANY) if 4 <= i < 7 else full_spec(*t.shape)
                for i, t in enumerate(operands)
            ],
            out_specs=[full_spec(*shape) for shape, _ in shapes],
            scratch_shapes=[
                pltpu.VMEM((length, wq.shape[1]), BF16),
                pltpu.VMEM((length, columns), F32),
                pltpu.VMEM((length, width), F32),
            ]
            + [pltpu.VMEM(t.shape, BF16) for t in (wq, wk, wv)]
            + [pltpu.SemaphoreType.DMA((3,))],
        ),
        compiler_params=pltpu.CompilerParams(vmem_limit_bytes=56 * 1024 * 1024),
        cost_estimate=NO_COST,
    )(meta, *operands)


def expert_kernel(inner, aliased, experts, meta, *refs):
    blocks, ups, tables = (refs[i * inner : (i + 1) * inner] for i in range(3))
    refs = refs[3 * inner :]
    weight_refs, refs = refs[:6], refs[6 + aliased :]
    tokens_out, upstream_out = refs[:2]
    used_out, gate_out, up_out = refs[2:4], refs[4:6], refs[6:8]
    mix_out, in_out = refs[8 : 8 + inner], refs[8 + inner : 8 + 2 * inner]
    table, mix_total, in_total = refs[8 + 2 * inner :]
    rows, width = blocks[0].shape
    expert = pl.program_id(0)

    def place(j):
        return pl.ds(pl.multiple_of(lax.rem(meta[1] + j, inner) * rows, rows), rows)

    @pl.when(expert == 0)
    def _():
        for j in range(inner):
            tokens_out[place(j), :] = blocks[j][...]
            upstream_out[place(j), :] = ups[j][...]
            table[place(j), :] = tables[j][...].astype(F32)
        mix_total[...] = jnp.zeros_like(mix_total)
        in_total[...] = jnp.zeros_like(in_total)

    lane = lax.broadcasted_iota(jnp.int32, table.shape, 1)
    wanted = (lax.rem(lane, experts) == meta[2] + expert) & (lane < 3 * experts)
    weight = jnp.sum(jnp.where(wanted, table[...], 0.0), axis=1, keepdims=True)
    for half in range(2):
        gate, up, down = (weight_refs[2 * i + half][0] for i in range(3))
        pre_gate = jnp.dot(tokens_out[...], gate, preferred_element_type=F32)
        pre_up = jnp.dot(tokens_out[...], up, preferred_element_type=F32)
        grad_act = dot_t(upstream_out[...], down) * weight
        gate_sigmoid = 1.0 / (1.0 + jnp.exp(-pre_gate))
        silu = pre_gate * gate_sigmoid
        used = (silu * pre_up * weight).astype(BF16)
        grad_gate = grad_act * pre_up * gate_sigmoid * (1.0 + pre_gate * (1.0 - gate_sigmoid))
        grad_up = grad_act * silu
        used_out[half][0] = used
        gate_out[half][0] = grad_gate.astype(BF16)
        up_out[half][0] = grad_up.astype(BF16)
        mix_total[...] += jnp.dot(used, down, preferred_element_type=F32)
        in_total[...] += dot_t((grad_gate * weight).astype(BF16), gate) + dot_t(
            (grad_up * weight).astype(BF16), up
        )

    @pl.when(expert == pl.num_programs(0) - 1)
    def _():
        for j in range(inner):
            mix_out[j][...] = mix_total[place(j), :].astype(BF16)
            in_out[j][...] = in_total[place(j), :].astype(BF16)


def run_experts(meta, chunk_index, blocks, payloads, expert_weights, buffers, total, expert_count):
    inner, rows, width = len(blocks), blocks[0].shape[0], expert_weights[0].shape[1]
    firsts = [t.shape[1] // width - 1 for t in payloads]
    experts, half = expert_weights[0].shape[0], expert_weights[0].shape[2]
    chunk = inner * rows
    extra = 128
    by_chunk = pl.BlockSpec((chunk, width), lambda e, m: (m[0], 0))
    per_expert = pl.BlockSpec((1, chunk, half), lambda e, m: (e, m[0], 0))
    spread = pl.BlockSpec((1, width, half), lambda e, m: (e, 0, 0))
    tall = pl.BlockSpec((1, half, width), lambda e, m: (e, 0, 0))
    line = pl.BlockSpec((rows, width), lambda e, m: (chunk_index, 0))
    shapes = [jax.ShapeDtypeStruct((total, width), BF16)] * 2
    shapes += [jax.ShapeDtypeStruct((experts, total, half), BF16)] * 6
    shapes += [jax.ShapeDtypeStruct((total // inner, width), BF16)] * inner
    first = 1 + 3 * inner + 6
    return pl.pallas_call(
        functools.partial(expert_kernel, inner, len(buffers), expert_count),
        out_shape=shapes + [jax.ShapeDtypeStruct((rows, width), BF16)] * inner,
        grid_spec=pltpu.PrefetchScalarGridSpec(
            num_scalar_prefetch=1,
            grid=(experts,),
            in_specs=[full_spec(rows, width)] * inner
            + [pl.BlockSpec((rows, width), lambda e, m, at=at: (0, at)) for at in firsts]
            + [
                pl.BlockSpec((rows, extra), lambda e, m, at=at: (0, (at + 1) * (width // extra)))
                for at in firsts
            ]
            + [spread] * 4
            + [tall] * 2
            + [pl.BlockSpec(memory_space=pl.ANY)] * len(buffers),
            out_specs=[by_chunk] * 2
            + [per_expert] * 6
            + [line] * inner
            + [full_spec(rows, width)] * inner,
            scratch_shapes=[
                pltpu.VMEM((chunk, extra), F32),
                pltpu.VMEM((chunk, width), F32),
                pltpu.VMEM((chunk, width), F32),
            ],
        ),
        input_output_aliases={first + i: i for i in range(len(buffers))},
        compiler_params=pltpu.CompilerParams(vmem_limit_bytes=56 * 1024 * 1024),
        cost_estimate=NO_COST,
    )(meta, *blocks, *payloads, *payloads, *expert_weights, *buffers)


def weight_grads_kernel(count, downs, summed, tokens, *refs):
    sides, down, refs = refs[:count], refs[count : count + downs], refs[count + downs :]
    made = count + (downs > 0)
    added, outs = refs[: made * summed], refs[made * summed :]

    def store(index, at, value):
        if summed:
            value = value + added[index][at].astype(F32)
        outs[index][at] = value.astype(BF16)

    def product(left, right):
        return lax.dot_general(left, right, (((0,), (0,)), ((), ())), preferred_element_type=F32)

    for index, side in enumerate(sides):
        for e in range(side.shape[0]):
            store(index, e, product(tokens[...], side[e]))
    if downs:
        upstream, used = down
        store(count, 0, product(used[0], upstream[...]))


def weight_grads(tokens, sides, down, added):
    (experts, total, half), width = sides[0].shape, tokens.shape[1]
    steps = 2 * experts
    high, low = width // steps, half // 2
    spread = pl.BlockSpec((experts, high, half), lambda r: (0, r, 0))
    tall = pl.BlockSpec((1, low, width), lambda r: (lax.div(r, 2), lax.rem(r, 2), 0))
    specs = [spread] * len(sides) + [tall] * (len(down) > 0)
    shapes = [(experts, width, half)] * len(sides) + [(experts, half, width)] * (len(down) > 0)
    down_specs = [
        full_spec(total, width),
        pl.BlockSpec((1, total, low), lambda r: (lax.div(r, 2), 0, lax.rem(r, 2))),
    ]
    return pl.pallas_call(
        functools.partial(weight_grads_kernel, len(sides), len(down), len(added) > 0),
        out_shape=[jax.ShapeDtypeStruct(shape, BF16) for shape in shapes],
        grid=(steps,),
        in_specs=[pl.BlockSpec((total, high), lambda r: (0, r))]
        + [full_spec(experts, total, half)] * len(sides)
        + down_specs[: len(down)]
        + specs * (len(added) > 0),
        out_specs=specs,
        compiler_params=pltpu.CompilerParams(vmem_limit_bytes=62 * 1024 * 1024),
        cost_estimate=NO_COST,
    )(tokens, *sides, *down, *added)


def place_kernel(sizes, counts, meta, *refs):
    blocks, outs = refs[: len(counts)], refs[-len(sizes) :]
    step, first = pl.program_id(0), 0
    for block_ref, count in zip(blocks, counts):

        @pl.when((step >= first) & (step < first + count))
        def _():
            at = 0
            for size, out in zip(sizes, outs):
                out[...] = block_ref[0, :, at : at + size].astype(F32)
                at += size

        first += count


def place_line(meta, pieces, sizes, shapes, buffers):
    counts, (_, rows, width) = [t.shape[0] for t in pieces], pieces[0].shape
    firsts = [sum(counts[:i]) for i in range(len(counts))]
    taken = [
        pl.BlockSpec(
            (1, rows, width), lambda i, m, at=at, n=n: (jnp.minimum(jnp.maximum(i - at, 0), n - 1), 0, 0)
        )
        for at, n in zip(firsts, counts)
    ]
    low = [pl.BlockSpec((rows, size), lambda i, m: (m[4 * i], m[4 * i + 1])) for size in sizes[:-1]]
    low.append(pl.BlockSpec((rows, sizes[-1]), lambda i, m: (m[4 * i + 2], m[4 * i + 3])))
    return pl.pallas_call(
        functools.partial(place_kernel, sizes, counts),
        out_shape=[jax.ShapeDtypeStruct(shape, F32) for shape in shapes],
        grid_spec=pltpu.PrefetchScalarGridSpec(
            num_scalar_prefetch=1,
            grid=(sum(counts),),
            in_specs=taken + [pl.BlockSpec(memory_space=pl.ANY)] * len(buffers),
            out_specs=low,
        ),
        input_output_aliases={1 + len(pieces) + i: i for i in range(len(buffers))},
        cost_estimate=NO_COST,
    )(meta, *pieces, *buffers)


def dense_kernel(count, inner, meta, *refs):
    hidden, mixed, shares, resids = (refs[i * count : (i + 1) * count] for i in range(4))
    outs, scratch = refs[4 * count : -1], refs[-1]
    size, step = shares[0].shape[1], pl.program_id(0)

    def summed(lefts, rights):
        return sum(
            lax.dot_general(
                left[...], right[...], (((0,), (0,)), ((), ())), preferred_element_type=F32
            )
            for left, right in zip(lefts, rights)
        )

    scratch[:, :size] = summed(hidden, shares).astype(BF16)
    scratch[:, size:] = summed(mixed, resids).astype(BF16)
    rows = outs[0].shape[0]
    for k in range(len(outs) // inner):

        @pl.when(step == k)
        def _():
            for j in range(inner):
                start = pl.multiple_of(lax.rem(meta[0] + j, inner) * rows, rows)
                outs[k * inner + j][...] = scratch[pl.ds(start, rows), :]


def dense_blocks(meta, hidden, mixed, shares, resids, outer, inner):
    count, (length, width), size = len(hidden), hidden[0].shape, shares[0].shape[1]
    high, wide, steps = width // outer, mixed[0].shape[1], meta.shape[0] - 1
    part = resids[0].shape[1] * wide // width
    per = wide // high
    block = (high // inner, size + part)
    made = pl.pallas_call(
        functools.partial(dense_kernel, count, inner),
        out_shape=[jax.ShapeDtypeStruct(block, BF16)] * (steps * inner),
        grid_spec=pltpu.PrefetchScalarGridSpec(
            num_scalar_prefetch=1,
            grid=(steps,),
            in_specs=[pl.BlockSpec((length, high), lambda i, m: (0, m[1 + i]))] * count
            + [pl.BlockSpec((length, high), lambda i, m: (0, lax.rem(m[1 + i], per)))] * count
            + [full_spec(length, size)] * count
            + [pl.BlockSpec((length, part), lambda i, m: (0, lax.div(m[1 + i], per)))] * count,
            out_specs=[full_spec(*block)] * (steps * inner),
            scratch_shapes=[pltpu.VMEM((high, size + part), BF16)],
        ),
        compiler_params=pltpu.CompilerParams(vmem_limit_bytes=56 * 1024 * 1024),
        cost_estimate=NO_COST,
    )(meta, *hidden, *mixed, *shares, *resids)
    return [made[i * inner : (i + 1) * inner] for i in range(steps)]


def body(
    activations,
    segments,
    routes,
    route_weights,
    norm_attn_gain,
    norm_ffn_gain,
    query_weight,
    key_matrix,
    value_matrix,
    output_projection_weight,
    expert_gate,
    expert_up,
    expert_down,
    grad_output,
):
    tensor_rank = lax.axis_index("tensor")
    dp_rank = lax.axis_index("dp")
    dp_count = lax.axis_size("dp")
    outer, inner = grid_sizes()
    outer_rank = lax.axis_index("expert") // inner
    inner_rank = lax.axis_index("expert") % inner
    rows, width = activations.shape
    experts_here = expert_gate.shape[0]
    expert_count = experts_here * lax.axis_size("expert")

    named = routes[:, :, None] == jnp.arange(expert_count, dtype=jnp.int32)
    weight_table = jnp.sum(jnp.where(named, route_weights[:, :, None], 0.0), axis=1)
    high = lax.reduce_precision(weight_table, 8, 7)
    middle = lax.reduce_precision(weight_table - high, 8, 7)
    low = weight_table - high - middle
    table = jnp.concatenate([high, middle, low], axis=1).astype(BF16)
    table = jnp.pad(table, ((0, 0), (0, -table.shape[1] % 128)))
    payload = jnp.concatenate([grad_output, table], axis=1)
    up_one, up_three, up_line = shift_outer(payload, 1), shift_outer(payload, -1), inner_line(payload)
    heads_meta = jnp.stack([tensor_rank, dp_rank]).astype(jnp.int32)
    attn_weights = (query_weight, key_matrix, value_matrix, output_projection_weight)
    hidden, q, k, v, mixed, log_total, attn_own, attn_other = attend(
        heads_meta, activations, swap(activations), norm_attn_gain, segments, *attn_weights
    )
    x_own = activations.astype(F32)
    attn_own, attn_other, up_one, up_three, up_line = together(
        attn_own, attn_other, up_one, up_three, up_line
    )
    up_three = inner_line(up_three)
    residual = x_own + attn_own + swap(attn_other)
    normed_two, scale_two = norm_forward(residual, norm_ffn_gain)

    expert_weights = []
    for weights_own in (expert_gate, expert_up, expert_down):
        expert_weights += [weights_own, swap(weights_own)]
    first_expert = lax.axis_index("expert") * experts_here

    h_own = normed_two.astype(BF16)
    h_one, h_line = shift_outer(h_own, 1), inner_line(h_own)
    h_one, h_line, up_one, up_three = together(h_one, h_line, up_one, up_three)
    both = jnp.concatenate([h_one, up_one], axis=1)

    def experts_on(chunk, buffers, blocks, payloads):
        meta = jnp.stack([(outer_rank + chunk) % outer, inner_rank, first_expert])
        made = run_experts(
            meta.astype(jnp.int32), chunk, blocks, payloads, expert_weights, buffers,
            outer * inner * rows, expert_count,
        )
        return list(made[: 8 + inner]), made[8 + inner :]

    def line_sum(parts):
        return inner_sum(parts).astype(BF16)

    others_rows = [shift_dp(activations, step) for step in range(1, dp_count)]
    line, both = inner_line(both), shift_outer(both, 1)
    made = experts_on(0, [], h_line, up_line)
    made, line, both, others_rows = together(made, line, both, others_rows)
    buffers, in_zero = made
    others_swapped = [swap(t) for t in others_rows]
    made = experts_on(1, buffers, line, line)
    line, both = inner_line(both), shift_outer(both, 1)
    mixed_all = [mixed] + [shift_dp(mixed, step) for step in range(1, dp_count)]
    made, line, both, mixed_all, others_swapped = together(
        made, line, both, mixed_all, others_swapped
    )
    buffers, parts = made
    made = experts_on(2, buffers, line, line)
    line, sum_one = inner_line(both[:, :width]), line_sum(parts)
    hidden_all = [hidden]
    for step in range(1, dp_count):
        other = jnp.concatenate([others_rows[step - 1], others_swapped[step - 1]], axis=0)
        other = jnp.where(tensor_rank == 0, other, jnp.roll(other, rows, 0)).astype(F32)
        hidden_all.append(norm_forward(other, norm_attn_gain)[0].astype(BF16))
    made, line, sum_one, hidden_all = together(made, line, sum_one, hidden_all)
    buffers, parts = made
    sum_one, sum_two = shift_outer(sum_one, -1), line_sum(parts)
    made = experts_on(3, buffers, line, up_three)
    made, sum_one, sum_two, in_zero = together(made, sum_one, sum_two, in_zero)
    buffers, parts = made
    tokens_all, upstream_all, *pairs = buffers
    pairs, mix_lines = pairs[:6], pairs[6:]
    sides = [[pairs[at + half] for at in (0, 2, 4)] for half in range(2)]
    peers = weight_grads(tokens_all, sides[1][1:], (upstream_all, sides[1][0]), [])
    sum_two, sum_three, sum_zero = shift_outer(sum_two, -2), line_sum(parts), inner_sum(in_zero)
    sum_two, sum_three, sum_zero, peers = together(sum_two, sum_three, sum_zero, peers)
    mix_lines = after(mix_lines, sum_three)
    mix_found = inner_line_of(mix_lines)
    sum_three, arrived = together(shift_outer(sum_three, -3), [swap(peer) for peer in peers])
    grad_h_own = sum_zero.astype(F32)
    for term in (sum_one, sum_two, sum_three):
        grad_h_own = grad_h_own + term.astype(F32)

    def sum_dp(half):
        bit, found = 1, []
        while bit < dp_count:
            found.append(lax.ppermute(half, "dp", [(i, i ^ bit) for i in range(dp_count)]))
            bit *= 2
            if bit < dp_count:
                half = (half.astype(F32) + found.pop().astype(F32)).astype(BF16)
        return half, *found

    def total(pair):
        return sum(t.astype(F32) for t in pair)

    grad_norm_part, _ = norm_backward(residual, scale_two, norm_ffn_gain, grad_h_own)
    grad_resid = grad_output.astype(F32) + grad_norm_part
    resid_own = grad_resid.astype(BF16)
    resid_other = swap(resid_own)
    resid_full = jnp.where(
        tensor_rank == 0,
        jnp.concatenate([resid_own, resid_other], axis=0),
        jnp.concatenate([resid_other, resid_own], axis=0),
    )
    *shares, dh_own, dh_other = attend_back(
        heads_meta, dp_count, resid_full, segments, *attn_weights, q, k, v, mixed, log_total,
    )

    length, share_width = resid_full.shape[0], width // dp_count

    def columns(index):
        return lax.dynamic_slice_in_dim(resid_full, index * share_width, share_width, 1)

    resid_shares = [columns(dp_rank)]
    for step in range(1, dp_count):
        resid_shares.append(shift_dp(columns((dp_rank + step) % dp_count), step))
    shares, resid_shares = together(shares, resid_shares)
    all_shares = [shares[0]] + [shift_dp(shares[step], step) for step in range(1, dp_count)]
    parts = width // mixed.shape[1]
    sizes = [t.shape[1] // dp_count for t in (query_weight, key_matrix, value_matrix)]
    sizes.append(share_width // parts)
    aligned = all(size % 128 == 0 for size in sizes)
    (gate_half,) = weight_grads(tokens_all, sides[0][1:2], [], arrived[:1])
    all_shares, gate_half = together(all_shares, gate_half)
    block = width // (outer * inner)
    def row_terms(part, step):
        start = (outer_rank + step) % outer * inner
        return [
            lax.dynamic_slice_in_dim(part, (start + (inner_rank + j) % inner) * block, block, 0)
            for j in range(inner)
        ]

    if aligned:

        def blocks_of(steps, all_shares):
            meta = jnp.stack([inner_rank] + [(outer_rank + k) % outer for k in steps])
            return dense_blocks(
                meta.astype(jnp.int32), hidden_all, mixed_all, all_shares, resid_shares, outer, inner
            )

        terms = [None, None, *blocks_of([2], all_shares), None]
    else:
        qkv_part = dot(
            "sd,sa->da", jnp.concatenate(hidden_all, 0), jnp.concatenate(all_shares, 0), BF16
        )
        mix_part = dot(
            "sa,shb->hab",
            jnp.concatenate(mixed_all, 0),
            jnp.concatenate(resid_shares, 0).reshape(length * dp_count, parts, share_width // parts),
            BF16,
        )
        dense_part = jnp.concatenate([qkv_part, mix_part.reshape(width, -1)], axis=1)
        terms = [row_terms(dense_part, k) for k in range(outer)]
    terms[2], mix_found, arrived = together(terms[2], mix_found, arrived)
    mix_line = [
        sum(t[k * rows : (k + 1) * rows].astype(F32) for t in mix_found) for k in range(outer)
    ]
    two, dh_other = line_sum(terms[2]), swap(dh_other)
    carried = shift_outer(mix_line[2].astype(BF16), -1)
    if aligned:
        terms[1], terms[3], terms[0] = blocks_of([1, 3, 0], after(all_shares, terms[2]))
    two, dh_other, terms, arrived = together(two, dh_other, terms, arrived)
    gate_pair = sum_dp(after(gate_half, two))
    scale_one = lax.rsqrt(jnp.mean(x_own * x_own, axis=-1, keepdims=True) + EPS)
    grad_x_part, grad_attn_gain = norm_backward(
        x_own, scale_one, norm_attn_gain, dh_own + dh_other
    )
    grad_input = grad_resid + grad_x_part
    late = after((grad_h_own, residual, scale_two), terms)
    grad_ffn_gain = jnp.sum(late[0] * late[1] * late[2], axis=0)
    gains, hops = jnp.stack([grad_attn_gain, grad_ffn_gain]), hops_of_all()
    two, one, three = shift_outer(two, -2), line_sum(terms[1]), line_sum(terms[3])
    halves = weight_grads(tokens_all, sides[0][2:], (upstream_all, sides[0][0]), arrived[1:])
    two, one, three, terms, gains, carried, halves = together(
        two, one, three, terms, gains, carried, halves
    )
    mix_line[1] = mix_line[1].astype(F32) + carried.astype(F32)
    up_half, down_half = halves
    one, three, zero = shift_outer(one, -1), shift_outer(three, -3), inner_sum(terms[0])
    one, three, zero, other, grad_input, gate_pair = together(
        one, three, zero, exchange(gains, hops[0]), grad_input, gate_pair
    )
    gains, hops = gains + other, hops[1:]
    reduced = zero.astype(F32)
    for term in (one, two, three):
        reduced = reduced + term.astype(F32)
    reduced = reduced.astype(BF16)
    shapes = [t.shape for t in (query_weight, key_matrix, value_matrix)] + [(width // parts, width)]

    def block_of(from_one, from_three):
        mix = mix_line[0].astype(F32) + from_one.astype(F32) + from_three.astype(F32)
        return (after(residual, reduced) + mix).astype(BF16)

    mix_one, mix_three = mix_line[1].astype(BF16), mix_line[3].astype(BF16)
    if aligned:
        per, dense = outer * inner // parts, []

        def place(pieces, found, dense):
            meta = []
            for k, j, turn in found:
                index = (outer_rank + k) % outer * inner + (inner_rank + j) % inner
                share = (dp_rank - turn) % dp_count
                meta += [index, share, index % per, share * parts + index // per]
            return place_line(jnp.stack(meta).astype(jnp.int32), pieces, sizes, shapes, dense)

        others = range(1, dp_count)
        step = {
            "line": inner_line(reduced[None]),
            "next": shift_outer(reduced[None]),
            "others": [shift_dp(reduced, turn)[None] for turn in others],
            "gains": exchange(gains, hops[0]),
            "done": total(after(gate_pair, reduced)),
        }
        (step,) = together(step)
        gate_sum = step["done"]
        gains, hops = gains + step["gains"], hops[1:]
        lines = [step["line"]]
        held = jnp.concatenate([step["next"], *step["others"]], axis=0)
        up_pair, down_pair = (sum_dp(after(t, step["others"])) for t in (up_half, down_half))
        for k in range(1, outer + 1):
            step = {"line": inner_line(held), "gains": exchange(gains, hops[0]) if hops else gains}
            if k < outer:
                step["next"] = shift_outer(held if k + 1 < outer else held[1:])
            before = [(k - 1, turn) for turn in ([0] if k == 1 else [0, *others])]
            before = [(at - 1 if turn else at, turn) for at, turn in before]
            now = [(k, 0, 0)] * (k < outer) + [(k - 1, 0, turn) for turn in others]
            ready, entries = [held], list(now)
            for j in range(1, inner):
                ready.append(lines[-1][j])
                entries += [(at, j, turn) for at, turn in before]
            if k == 1:
                ready.append(lines[0][0])
                entries.append((0, 0, 0))
            made = place(ready, entries, dense)
            step["dense"] = made
            if k == 3:
                step["done"] = total(after(up_pair, made))
                step["mix"] = shift_outer(after(mix_one, held), -1)
            if k == 4:
                step["done"] = total(after(down_pair, made))
                step["mix"] = shift_outer(after(mix_three, held), -3)
            (step,) = together(step)
            if hops:
                gains, hops = gains + step["gains"], hops[1:]
            if k == 3:
                up_sum, mix_one = step["done"], step["mix"]
            if k == 4:
                down_sum, block_out = step["done"], block_of(mix_one, step["mix"])
            dense, held = step["dense"], step.get("next")
            lines.append(step["line"])
        for j in range(1, inner):
            dense = place([lines[-1][j]], [(outer - 1, j, turn) for turn in others], dense)
    else:
        for hop in hops:
            gains = gains + exchange(gains, hop)
        gate_sum, up_sum, down_sum = (
            total(pair) for pair in (gate_pair, sum_dp(up_half), sum_dp(down_half))
        )
        block_out = block_of(shift_outer(mix_one, -1), shift_outer(mix_three, -3))
        gathered = lax.all_gather(reduced, ("dp", "expert"), axis=0, tiled=True)
        gathered = gathered.reshape(dp_count, width, -1).astype(F32)
        starts = [sum(sizes[:i]) for i in range(len(sizes))]
        dense = [gathered[:, :, at : at + size] for at, size in zip(starts, sizes)]
        dense[:-1] = [t.transpose(1, 0, 2).reshape(width, -1) for t in dense[:-1]]
        mix_w = dense[-1].reshape(dp_count, parts, width // parts, -1)
        dense[-1] = mix_w.transpose(2, 0, 1, 3).reshape(width // parts, width)
    return (
        block_out,
        grad_input,
        gains[0],
        gains[1],
        *dense,
        gate_sum,
        up_sum,
        down_sum,
    )


def solution(mesh):
    tokens = P(("dp", "expert", "tensor"), None)
    whole = P()
    columns = P(None, "tensor")
    hidden_last = P("expert", None, "tensor")
    hidden_mid = P("expert", "tensor", None)
    mixer = P("tensor", None)
    return jax.shard_map(
        body,
        mesh=mesh,
        in_specs=(
            tokens,
            P(("dp", "expert"), None),
            tokens,
            tokens,
            whole,
            whole,
            columns,
            columns,
            columns,
            mixer,
            hidden_last,
            hidden_last,
            hidden_mid,
            tokens,
        ),
        out_specs=(
            tokens,
            tokens,
            whole,
            whole,
            columns,
            columns,
            columns,
            mixer,
            hidden_last,
            hidden_last,
            hidden_mid,
        ),
        check_vma=False,
    )
```

```python
import functools

import jax
import jax.numpy as jnp
import numpy as np
from jax import lax
from jax.experimental import pallas as pl
from jax.experimental.pallas import tpu as pltpu
from jax.sharding import PartitionSpec as P

HEAD_DIM = 64
EPS = 1e-05
ATTN_SCALE = 0.015625
THETA = 10000.0
NEG_FILL = -1e30
F32 = jnp.float32
BF16 = jnp.bfloat16
NO_COST = pl.CostEstimate(flops=1, bytes_accessed=1, transcendentals=0)


def after(values, token):
    return lax.optimization_barrier((values, token))[0]


def swap(values):
    return lax.ppermute(values, "tensor", [(0, 1), (1, 0)])


def shift_dp(values, step):
    count = lax.axis_size("dp")
    return lax.ppermute(values, "dp", [(i, (i + step) % count) for i in range(count)])


def grid_sizes():
    count = lax.axis_size("expert")
    return 4, count // 4


def shift_outer(values, step=1):
    outer, inner = grid_sizes()
    pairs = [(((o + step) % outer) * inner + i, o * inner + i) for o in range(outer) for i in range(inner)]
    return lax.ppermute(values, "expert", pairs)


def shift_inner(values):
    outer, inner = grid_sizes()
    pairs = [(o * inner + (i + 1) % inner, o * inner + i) for o in range(outer) for i in range(inner)]
    return lax.ppermute(values, "expert", pairs)


def inner_line(block):
    line = [block]
    for _ in range(1, grid_sizes()[1]):
        line.append(shift_inner(line[-1]))
    return line


def inner_sum(parts):
    inner, total = len(parts), parts[1 % len(parts)]
    for j in range(2, inner + 1):
        total = shift_inner(total.astype(BF16)).astype(F32) + parts[j % inner].astype(F32)
    return total


def inner_line_of(parts):
    inner, total = len(parts), parts[1 % len(parts)]
    for j in range(2, inner):
        total = shift_inner(total.astype(BF16)).astype(F32) + parts[j].astype(F32)
    return [parts[0]] if inner == 1 else [shift_inner(total.astype(BF16)), parts[0]]


def together(*values):
    return lax.optimization_barrier(values)


def hops_of_all():
    bits = {}
    for axis in ("tensor", "expert", "dp"):
        count = lax.axis_size(axis)
        bits[axis] = [(axis, 1 << i) for i in range(count.bit_length() - 1)]
    return bits["tensor"] + bits["dp"] + bits["expert"]


def exchange(values, hop):
    axis, bit = hop
    return lax.ppermute(values, axis, [(i, i ^ bit) for i in range(lax.axis_size(axis))])


def norm_forward(values, gain_vector):
    inv_scale = lax.rsqrt(jnp.mean(values * values, axis=-1, keepdims=True) + EPS)
    return (values * inv_scale * gain_vector, inv_scale)


def norm_backward(values, inv_scale, gain_vector, upstream):
    weighted = upstream * gain_vector
    inner = jnp.mean(weighted * values, axis=-1, keepdims=True)
    value_gradient = inv_scale * weighted - values * (inv_scale * inv_scale * inv_scale) * inner
    grad_gain = jnp.sum(upstream * values * inv_scale, axis=0)
    return (value_gradient, grad_gain)


def dot(spec, left, right, kind=F32):
    return jnp.einsum(spec, left, right, preferred_element_type=kind)

def dot_t(left, right):
    return lax.dot_general(left, right, (((1,), (1,)), ((), ())), preferred_element_type=F32)


def full_spec(*shape):
    return pl.BlockSpec(shape, lambda *_: (0,) * len(shape))


def rope_tables(length, width):
    half = HEAD_DIM // 2
    frequency = (THETA ** (-np.arange(half, dtype=np.float32) * 2.0 / HEAD_DIM)).astype(np.float32)
    angle = np.arange(length, dtype=np.float32)[:, None] * frequency[None, :]
    cosine, sine = np.cos(angle.astype(np.float64)), np.sin(angle.astype(np.float64))
    cosine = np.concatenate([cosine, cosine], axis=1)
    sine = np.concatenate([-sine, sine], axis=1)
    copies = width // HEAD_DIM
    return np.tile(cosine, (1, copies)).astype(np.float32), np.tile(sine, (1, copies)).astype(np.float32)


def turn(values, cosine, sine):
    width, half = values.shape[1], HEAD_DIM // 2
    copies = width // cosine.shape[1]
    lane = lax.broadcasted_iota(jnp.int32, values.shape, 1)
    first = lax.rem(lane, HEAD_DIM) < half
    other = jnp.where(first, pltpu.roll(values, width - half, 1), pltpu.roll(values, half, 1))
    return values * jnp.concatenate([cosine] * copies, 1) + other * jnp.concatenate([sine] * copies, 1)


def masked_scores(query, key, allowed):
    return jnp.where(allowed, dot_t(query, key) * ATTN_SCALE, NEG_FILL)


def allowed_pairs(segs):
    length = segs.shape[1]
    row = lax.broadcasted_iota(jnp.int32, (length, length), 0)
    column = lax.broadcasted_iota(jnp.int32, (length, length), 1)
    seg_row = segs.astype(F32)
    seg_column = jnp.sum(jnp.where(row == column, seg_row, 0.0), axis=1, keepdims=True)
    return (column <= row) & (seg_row == seg_column)


def row_places(meta, rows):
    own = pl.ds(pl.multiple_of(meta[0] * rows, rows), rows)
    other = pl.ds(pl.multiple_of((1 - meta[0]) * rows, rows), rows)
    return own, other


def attend_kernel(
    meta, own_ref, other_ref, gain_ref, segs, cos_ref, sin_ref, wq, wk, wv, wo,
    hidden_out, q_out, k_out, v_out, mixed_out, log_out, own_out, other_out, x_s, part_s, wo_s, sem,
):
    rows = own_ref.shape[0]
    late = pltpu.make_async_copy(wo, wo_s, sem)
    late.start()
    own, other = row_places(meta, rows)
    x_s[own, :] = own_ref[...].astype(F32)
    x_s[other, :] = other_ref[...].astype(F32)
    x = x_s[...]
    scale = lax.rsqrt(jnp.mean(x * x, axis=-1, keepdims=True) + EPS)
    hidden = (x * scale * gain_ref[...]).astype(BF16)
    hidden_out[...] = hidden
    cosine, sine = cos_ref[...], sin_ref[...]
    q_out[...] = turn(jnp.dot(hidden, wq[...], preferred_element_type=F32), cosine, sine).astype(BF16)
    k_out[...] = turn(jnp.dot(hidden, wk[...], preferred_element_type=F32), cosine, sine).astype(BF16)
    v_out[...] = jnp.dot(hidden, wv[...], preferred_element_type=F32).astype(BF16)
    allowed = allowed_pairs(segs[...])
    heads, heads_kv = wq.shape[1] // HEAD_DIM, wk.shape[1] // HEAD_DIM
    group = heads // heads_kv
    for g in range(heads_kv):
        key = k_out[:, g * HEAD_DIM : (g + 1) * HEAD_DIM]
        value = v_out[:, g * HEAD_DIM : (g + 1) * HEAD_DIM]
        for h in range(g * group, (g + 1) * group):
            at = slice(h * HEAD_DIM, (h + 1) * HEAD_DIM)
            scores = masked_scores(q_out[:, at], key, allowed)
            top = jnp.max(scores, axis=-1, keepdims=True)
            powers = jnp.exp(scores - top)
            power_sum = jnp.sum(powers, axis=-1, keepdims=True)
            log_out[:, h : h + 1] = top + jnp.log(power_sum)
            prob = (powers * (1.0 / power_sum)).astype(BF16)
            mixed_out[:, at] = jnp.dot(prob, value, preferred_element_type=F32).astype(BF16)
    late.wait()
    part_s[...] = jnp.dot(mixed_out[...], wo_s[...], preferred_element_type=F32)
    own_out[...] = part_s[own, :]
    other_out[...] = part_s[other, :]


def attend(meta, own, other, gain, segs, wq, wk, wv, wo):
    rows, width = own.shape
    length = segs.shape[1]
    cosine, sine = rope_tables(length, 128)
    operands = (own, other, gain, segs, cosine, sine, wq, wk, wv, wo)
    shapes = [
        ((length, width), BF16),
        ((length, wq.shape[1]), BF16),
        ((length, wk.shape[1]), BF16),
        ((length, wv.shape[1]), BF16),
        ((length, wq.shape[1]), BF16),
        ((length, 128), F32),
        ((rows, width), F32),
        ((rows, width), F32),
    ]
    return pl.pallas_call(
        attend_kernel,
        out_shape=[jax.ShapeDtypeStruct(*shape) for shape in shapes],
        grid_spec=pltpu.PrefetchScalarGridSpec(
            num_scalar_prefetch=1,
            grid=(1,),
            in_specs=[full_spec(*t.shape) for t in operands[:-1]]
            + [pl.BlockSpec(memory_space=pl.ANY)],
            out_specs=[full_spec(*shape) for shape, _ in shapes],
            scratch_shapes=[pltpu.VMEM((length, width), F32)] * 2
            + [pltpu.VMEM(wo.shape, BF16), pltpu.SemaphoreType.DMA],
        ),
        compiler_params=pltpu.CompilerParams(vmem_limit_bytes=56 * 1024 * 1024),
        cost_estimate=NO_COST,
    )(meta, *operands)


def attend_back_kernel(
    shares, meta, b_ref, segs, cos_ref, sin_ref, wq, wk, wv, wo,
    q_ref, k_ref, v_ref, mixed_ref, log_ref, *refs,
):
    share_outs, (own_out, other_out, grad_s, dq_s, part_s, *late_s, sems) = refs[:shares], refs[shares:]
    late = [
        pltpu.make_async_copy(source, target, sems.at[i])
        for i, (source, target) in enumerate(zip((wq, wk, wv), late_s))
    ]
    for copy in late:
        copy.start()
    own, other = row_places(meta, own_out.shape[0])
    grad_s[...] = dot_t(b_ref[...], wo[...]).astype(BF16)
    cosine, sine = cos_ref[...], -sin_ref[...]
    allowed = allowed_pairs(segs[...])
    wide, narrow = wq.shape[1], wk.shape[1]
    heads, heads_kv = wide // HEAD_DIM, narrow // HEAD_DIM
    group = heads // heads_kv

    def transposed_dot(left, right):
        return lax.dot_general(left, right, (((0,), (0,)), ((), ())), preferred_element_type=F32)

    for g in range(heads_kv):
        there = slice(g * HEAD_DIM, (g + 1) * HEAD_DIM)
        key, value = k_ref[:, there], v_ref[:, there]
        grad_key = grad_value = 0.0
        for h in range(g * group, (g + 1) * group):
            at = slice(h * HEAD_DIM, (h + 1) * HEAD_DIM)
            query, grad = q_ref[:, at], grad_s[:, at]
            prob = jnp.exp(masked_scores(query, key, allowed) - log_ref[:, h : h + 1])
            delta = jnp.sum(grad.astype(F32) * mixed_ref[:, at].astype(F32), axis=-1, keepdims=True)
            grad_scores = (prob * (dot_t(grad, value) - delta) * ATTN_SCALE).astype(BF16)
            dq_s[:, at] = jnp.dot(grad_scores, key, preferred_element_type=F32)
            grad_key = grad_key + transposed_dot(grad_scores, query)
            grad_value = grad_value + transposed_dot(prob.astype(BF16), grad)
        dq_s[:, wide + g * HEAD_DIM : wide + (g + 1) * HEAD_DIM] = grad_key
        at = wide + narrow + g * HEAD_DIM
        dq_s[:, at : at + HEAD_DIM] = grad_value
    dq = turn(dq_s[:, :wide], cosine, sine).astype(BF16)
    dk = turn(dq_s[:, wide : wide + narrow], cosine, sine).astype(BF16)
    dv = dq_s[:, wide + narrow :].astype(BF16)
    for copy in late:
        copy.wait()
    part_s[...] = sum(dot_t(part, held[...]) for part, held in zip((dq, dk, dv), late_s))
    own_out[...] = part_s[own, :]
    other_out[...] = part_s[other, :]
    for r in range(shares):

        @pl.when(meta[1] == r)
        def _():
            for step in range(shares):
                at = 0
                for part in (dq, dk, dv):
                    size = part.shape[1] // shares
                    index = (r + step) % shares
                    share_outs[step][:, at : at + size] = part[:, index * size : (index + 1) * size]
                    at += size


def attend_back(meta, shares, resid, segs, wq, wk, wv, wo, q, k, v, mixed, log_total):
    length, width = resid.shape
    cosine, sine = rope_tables(length, 128)
    operands = (resid, segs, cosine, sine, wq, wk, wv, wo, q, k, v, mixed, log_total)
    columns = wq.shape[1] + wk.shape[1] + wv.shape[1]
    shapes = [((length, columns // shares), BF16)] * shares
    shapes += [((length // 2, width), F32)] * 2
    return pl.pallas_call(
        functools.partial(attend_back_kernel, shares),
        out_shape=[jax.ShapeDtypeStruct(*shape) for shape in shapes],
        grid_spec=pltpu.PrefetchScalarGridSpec(
            num_scalar_prefetch=1,
            grid=(1,),
            in_specs=[
                pl.BlockSpec(memory_space=pl.ANY) if 4 <= i < 7 else full_spec(*t.shape)
                for i, t in enumerate(operands)
            ],
            out_specs=[full_spec(*shape) for shape, _ in shapes],
            scratch_shapes=[
                pltpu.VMEM((length, wq.shape[1]), BF16),
                pltpu.VMEM((length, columns), F32),
                pltpu.VMEM((length, width), F32),
            ]
            + [pltpu.VMEM(t.shape, BF16) for t in (wq, wk, wv)]
            + [pltpu.SemaphoreType.DMA((3,))],
        ),
        compiler_params=pltpu.CompilerParams(vmem_limit_bytes=56 * 1024 * 1024),
        cost_estimate=NO_COST,
    )(meta, *operands)


def expert_kernel(inner, aliased, experts, meta, *refs):
    blocks, ups, tables = (refs[i * inner : (i + 1) * inner] for i in range(3))
    refs = refs[3 * inner :]
    weight_refs, refs = refs[:6], refs[6 + aliased :]
    tokens_out, upstream_out = refs[:2]
    used_out, gate_out, up_out = refs[2:4], refs[4:6], refs[6:8]
    mix_out, in_out = refs[8 : 8 + inner], refs[8 + inner : 8 + 2 * inner]
    table, mix_total, in_total = refs[8 + 2 * inner :]
    rows, width = blocks[0].shape
    expert = pl.program_id(0)

    def place(j):
        return pl.ds(pl.multiple_of(lax.rem(meta[1] + j, inner) * rows, rows), rows)

    @pl.when(expert == 0)
    def _():
        for j in range(inner):
            tokens_out[place(j), :] = blocks[j][...]
            upstream_out[place(j), :] = ups[j][...]
            table[place(j), :] = tables[j][...].astype(F32)
        mix_total[...] = jnp.zeros_like(mix_total)
        in_total[...] = jnp.zeros_like(in_total)

    lane = lax.broadcasted_iota(jnp.int32, table.shape, 1)
    wanted = (lax.rem(lane, experts) == meta[2] + expert) & (lane < 3 * experts)
    weight = jnp.sum(jnp.where(wanted, table[...], 0.0), axis=1, keepdims=True)
    for half in range(2):
        gate, up, down = (weight_refs[2 * i + half][0] for i in range(3))
        pre_gate = jnp.dot(tokens_out[...], gate, preferred_element_type=F32)
        pre_up = jnp.dot(tokens_out[...], up, preferred_element_type=F32)
        grad_act = dot_t(upstream_out[...], down) * weight
        gate_sigmoid = 1.0 / (1.0 + jnp.exp(-pre_gate))
        silu = pre_gate * gate_sigmoid
        used = (silu * pre_up * weight).astype(BF16)
        grad_gate = grad_act * pre_up * gate_sigmoid * (1.0 + pre_gate * (1.0 - gate_sigmoid))
        grad_up = grad_act * silu
        used_out[half][0] = used
        gate_out[half][0] = grad_gate.astype(BF16)
        up_out[half][0] = grad_up.astype(BF16)
        mix_total[...] += jnp.dot(used, down, preferred_element_type=F32)
        in_total[...] += dot_t((grad_gate * weight).astype(BF16), gate) + dot_t(
            (grad_up * weight).astype(BF16), up
        )

    @pl.when(expert == pl.num_programs(0) - 1)
    def _():
        for j in range(inner):
            mix_out[j][...] = mix_total[place(j), :].astype(BF16)
            in_out[j][...] = in_total[place(j), :].astype(BF16)


def run_experts(meta, chunk_index, blocks, payloads, expert_weights, buffers, total, expert_count):
    inner, rows, width = len(blocks), blocks[0].shape[0], expert_weights[0].shape[1]
    firsts = [t.shape[1] // width - 1 for t in payloads]
    experts, half = expert_weights[0].shape[0], expert_weights[0].shape[2]
    chunk = inner * rows
    extra = 128
    by_chunk = pl.BlockSpec((chunk, width), lambda e, m: (m[0], 0))
    per_expert = pl.BlockSpec((1, chunk, half), lambda e, m: (e, m[0], 0))
    spread = pl.BlockSpec((1, width, half), lambda e, m: (e, 0, 0))
    tall = pl.BlockSpec((1, half, width), lambda e, m: (e, 0, 0))
    line = pl.BlockSpec((rows, width), lambda e, m: (chunk_index, 0))
    shapes = [jax.ShapeDtypeStruct((total, width), BF16)] * 2
    shapes += [jax.ShapeDtypeStruct((experts, total, half), BF16)] * 6
    shapes += [jax.ShapeDtypeStruct((total // inner, width), BF16)] * inner
    first = 1 + 3 * inner + 6
    return pl.pallas_call(
        functools.partial(expert_kernel, inner, len(buffers), expert_count),
        out_shape=shapes + [jax.ShapeDtypeStruct((rows, width), BF16)] * inner,
        grid_spec=pltpu.PrefetchScalarGridSpec(
            num_scalar_prefetch=1,
            grid=(experts,),
            in_specs=[full_spec(rows, width)] * inner
            + [pl.BlockSpec((rows, width), lambda e, m, at=at: (0, at)) for at in firsts]
            + [
                pl.BlockSpec((rows, extra), lambda e, m, at=at: (0, (at + 1) * (width // extra)))
                for at in firsts
            ]
            + [spread] * 4
            + [tall] * 2
            + [pl.BlockSpec(memory_space=pl.ANY)] * len(buffers),
            out_specs=[by_chunk] * 2
            + [per_expert] * 6
            + [line] * inner
            + [full_spec(rows, width)] * inner,
            scratch_shapes=[
                pltpu.VMEM((chunk, extra), F32),
                pltpu.VMEM((chunk, width), F32),
                pltpu.VMEM((chunk, width), F32),
            ],
        ),
        input_output_aliases={first + i: i for i in range(len(buffers))},
        compiler_params=pltpu.CompilerParams(vmem_limit_bytes=56 * 1024 * 1024),
        cost_estimate=NO_COST,
    )(meta, *blocks, *payloads, *payloads, *expert_weights, *buffers)


def weight_grads_kernel(count, downs, summed, tokens, *refs):
    sides, down, refs = refs[:count], refs[count : count + downs], refs[count + downs :]
    made = count + (downs > 0)
    added, outs = refs[: made * summed], refs[made * summed :]

    def store(index, at, value):
        if summed:
            value = value + added[index][at].astype(F32)
        outs[index][at] = value.astype(BF16)

    def product(left, right):
        return lax.dot_general(left, right, (((0,), (0,)), ((), ())), preferred_element_type=F32)

    for index, side in enumerate(sides):
        for e in range(side.shape[0]):
            store(index, e, product(tokens[...], side[e]))
    if downs:
        upstream, used = down
        store(count, 0, product(used[0], upstream[...]))


def weight_grads(tokens, sides, down, added):
    (experts, total, half), width = sides[0].shape, tokens.shape[1]
    steps = 2 * experts
    high, low = width // steps, half // 2
    spread = pl.BlockSpec((experts, high, half), lambda r: (0, r, 0))
    tall = pl.BlockSpec((1, low, width), lambda r: (lax.div(r, 2), lax.rem(r, 2), 0))
    specs = [spread] * len(sides) + [tall] * (len(down) > 0)
    shapes = [(experts, width, half)] * len(sides) + [(experts, half, width)] * (len(down) > 0)
    down_specs = [
        full_spec(total, width),
        pl.BlockSpec((1, total, low), lambda r: (lax.div(r, 2), 0, lax.rem(r, 2))),
    ]
    return pl.pallas_call(
        functools.partial(weight_grads_kernel, len(sides), len(down), len(added) > 0),
        out_shape=[jax.ShapeDtypeStruct(shape, BF16) for shape in shapes],
        grid=(steps,),
        in_specs=[pl.BlockSpec((total, high), lambda r: (0, r))]
        + [full_spec(experts, total, half)] * len(sides)
        + down_specs[: len(down)]
        + specs * (len(added) > 0),
        out_specs=specs,
        compiler_params=pltpu.CompilerParams(vmem_limit_bytes=62 * 1024 * 1024),
        cost_estimate=NO_COST,
    )(tokens, *sides, *down, *added)


def place_kernel(sizes, counts, meta, *refs):
    blocks, outs = refs[: len(counts)], refs[-len(sizes) :]
    step, first = pl.program_id(0), 0
    for block_ref, count in zip(blocks, counts):

        @pl.when((step >= first) & (step < first + count))
        def _():
            at = 0
            for size, out in zip(sizes, outs):
                out[...] = block_ref[0, :, at : at + size].astype(F32)
                at += size

        first += count


def place_line(meta, pieces, sizes, shapes, buffers):
    counts, (_, rows, width) = [t.shape[0] for t in pieces], pieces[0].shape
    firsts = [sum(counts[:i]) for i in range(len(counts))]
    taken = [
        pl.BlockSpec(
            (1, rows, width), lambda i, m, at=at, n=n: (jnp.minimum(jnp.maximum(i - at, 0), n - 1), 0, 0)
        )
        for at, n in zip(firsts, counts)
    ]
    low = [pl.BlockSpec((rows, size), lambda i, m: (m[4 * i], m[4 * i + 1])) for size in sizes[:-1]]
    low.append(pl.BlockSpec((rows, sizes[-1]), lambda i, m: (m[4 * i + 2], m[4 * i + 3])))
    return pl.pallas_call(
        functools.partial(place_kernel, sizes, counts),
        out_shape=[jax.ShapeDtypeStruct(shape, F32) for shape in shapes],
        grid_spec=pltpu.PrefetchScalarGridSpec(
            num_scalar_prefetch=1,
            grid=(sum(counts),),
            in_specs=taken + [pl.BlockSpec(memory_space=pl.ANY)] * len(buffers),
            out_specs=low,
        ),
        input_output_aliases={1 + len(pieces) + i: i for i in range(len(buffers))},
        cost_estimate=NO_COST,
    )(meta, *pieces, *buffers)


def dense_kernel(count, inner, meta, *refs):
    hidden, mixed, shares, resids = (refs[i * count : (i + 1) * count] for i in range(4))
    outs, scratch = refs[4 * count : -1], refs[-1]
    size, step = shares[0].shape[1], pl.program_id(0)

    def summed(lefts, rights):
        return sum(
            lax.dot_general(
                left[...], right[...], (((0,), (0,)), ((), ())), preferred_element_type=F32
            )
            for left, right in zip(lefts, rights)
        )

    scratch[:, :size] = summed(hidden, shares).astype(BF16)
    scratch[:, size:] = summed(mixed, resids).astype(BF16)
    rows = outs[0].shape[0]
    for k in range(len(outs) // inner):

        @pl.when(step == k)
        def _():
            for j in range(inner):
                start = pl.multiple_of(lax.rem(meta[0] + j, inner) * rows, rows)
                outs[k * inner + j][...] = scratch[pl.ds(start, rows), :]


def dense_blocks(meta, hidden, mixed, shares, resids, outer, inner):
    count, (length, width), size = len(hidden), hidden[0].shape, shares[0].shape[1]
    high, wide, steps = width // outer, mixed[0].shape[1], meta.shape[0] - 1
    part = resids[0].shape[1] * wide // width
    per = wide // high
    block = (high // inner, size + part)
    made = pl.pallas_call(
        functools.partial(dense_kernel, count, inner),
        out_shape=[jax.ShapeDtypeStruct(block, BF16)] * (steps * inner),
        grid_spec=pltpu.PrefetchScalarGridSpec(
            num_scalar_prefetch=1,
            grid=(steps,),
            in_specs=[pl.BlockSpec((length, high), lambda i, m: (0, m[1 + i]))] * count
            + [pl.BlockSpec((length, high), lambda i, m: (0, lax.rem(m[1 + i], per)))] * count
            + [full_spec(length, size)] * count
            + [pl.BlockSpec((length, part), lambda i, m: (0, lax.div(m[1 + i], per)))] * count,
            out_specs=[full_spec(*block)] * (steps * inner),
            scratch_shapes=[pltpu.VMEM((high, size + part), BF16)],
        ),
        compiler_params=pltpu.CompilerParams(vmem_limit_bytes=56 * 1024 * 1024),
        cost_estimate=NO_COST,
    )(meta, *hidden, *mixed, *shares, *resids)
    return [made[i * inner : (i + 1) * inner] for i in range(steps)]


def body(
    activations,
    segments,
    routes,
    route_weights,
    norm_attn_gain,
    norm_ffn_gain,
    query_weight,
    key_matrix,
    value_matrix,
    output_projection_weight,
    expert_gate,
    expert_up,
    expert_down,
    grad_output,
):
    tensor_rank = lax.axis_index("tensor")
    dp_rank = lax.axis_index("dp")
    dp_count = lax.axis_size("dp")
    outer, inner = grid_sizes()
    outer_rank = lax.axis_index("expert") // inner
    inner_rank = lax.axis_index("expert") % inner
    rows, width = activations.shape
    experts_here = expert_gate.shape[0]
    expert_count = experts_here * lax.axis_size("expert")

    named = routes[:, :, None] == jnp.arange(expert_count, dtype=jnp.int32)
    weight_table = jnp.sum(jnp.where(named, route_weights[:, :, None], 0.0), axis=1)
    high = lax.reduce_precision(weight_table, 8, 7)
    middle = lax.reduce_precision(weight_table - high, 8, 7)
    low = weight_table - high - middle
    table = jnp.concatenate([high, middle, low], axis=1).astype(BF16)
    table = jnp.pad(table, ((0, 0), (0, -table.shape[1] % 128)))
    payload = jnp.concatenate([grad_output, table], axis=1)
    up_one, up_three, up_line = shift_outer(payload, 1), shift_outer(payload, -1), inner_line(payload)
    heads_meta = jnp.stack([tensor_rank, dp_rank]).astype(jnp.int32)
    attn_weights = (query_weight, key_matrix, value_matrix, output_projection_weight)
    hidden, q, k, v, mixed, log_total, attn_own, attn_other = attend(
        heads_meta, activations, swap(activations), norm_attn_gain, segments, *attn_weights
    )
    x_own = activations.astype(F32)
    attn_own, attn_other, up_one, up_three, up_line = together(
        attn_own, attn_other, up_one, up_three, up_line
    )
    up_three = inner_line(up_three)
    residual = x_own + attn_own + swap(attn_other)
    normed_two, scale_two = norm_forward(residual, norm_ffn_gain)

    expert_weights = []
    for weights_own in (expert_gate, expert_up, expert_down):
        expert_weights += [weights_own, swap(weights_own)]
    first_expert = lax.axis_index("expert") * experts_here

    h_own = normed_two.astype(BF16)
    h_one, h_line = shift_outer(h_own, 1), inner_line(h_own)
    h_one, h_line, up_one, up_three = together(h_one, h_line, up_one, up_three)
    both = jnp.concatenate([h_one, up_one], axis=1)

    def experts_on(chunk, buffers, blocks, payloads):
        meta = jnp.stack([(outer_rank + chunk) % outer, inner_rank, first_expert])
        made = run_experts(
            meta.astype(jnp.int32), chunk, blocks, payloads, expert_weights, buffers,
            outer * inner * rows, expert_count,
        )
        return list(made[: 8 + inner]), made[8 + inner :]

    def line_sum(parts):
        return inner_sum(parts).astype(BF16)

    others_rows = [shift_dp(activations, step) for step in range(1, dp_count)]
    line, both = inner_line(both), shift_outer(both, 1)
    made = experts_on(0, [], h_line, up_line)
    made, line, both, others_rows = together(made, line, both, others_rows)
    buffers, in_zero = made
    others_swapped = [swap(t) for t in others_rows]
    made = experts_on(1, buffers, line, line)
    line, both = inner_line(both), shift_outer(both, 1)
    mixed_all = [mixed] + [shift_dp(mixed, step) for step in range(1, dp_count)]
    made, line, both, mixed_all, others_swapped = together(
        made, line, both, mixed_all, others_swapped
    )
    buffers, parts = made
    made = experts_on(2, buffers, line, line)
    line, sum_one = inner_line(both[:, :width]), line_sum(parts)
    hidden_all = [hidden]
    for step in range(1, dp_count):
        other = jnp.concatenate([others_rows[step - 1], others_swapped[step - 1]], axis=0)
        other = jnp.where(tensor_rank == 0, other, jnp.roll(other, rows, 0)).astype(F32)
        hidden_all.append(norm_forward(other, norm_attn_gain)[0].astype(BF16))
    made, line, sum_one, hidden_all = together(made, line, sum_one, hidden_all)
    buffers, parts = made
    sum_one, sum_two = shift_outer(sum_one, -1), line_sum(parts)
    made = experts_on(3, buffers, line, up_three)
    made, sum_one, sum_two, in_zero = together(made, sum_one, sum_two, in_zero)
    buffers, parts = made
    tokens_all, upstream_all, *pairs = buffers
    pairs, mix_lines = pairs[:6], pairs[6:]
    sides = [[pairs[at + half] for at in (0, 2, 4)] for half in range(2)]
    peers = weight_grads(tokens_all, sides[1][1:], (upstream_all, sides[1][0]), [])
    sum_two, sum_three, sum_zero = shift_outer(sum_two, -2), line_sum(parts), inner_sum(in_zero)
    sum_two, sum_three, sum_zero, peers = together(sum_two, sum_three, sum_zero, peers)
    mix_lines = after(mix_lines, sum_three)
    mix_found = inner_line_of(mix_lines)
    sum_three, arrived = shift_outer(sum_three, -3), [swap(peer) for peer in peers]
    grad_h_own = sum_zero.astype(F32)
    for term in (sum_one, sum_two, sum_three):
        grad_h_own = grad_h_own + term.astype(F32)

    def sum_dp(half):
        bit, found = 1, []
        while bit < dp_count:
            found.append(lax.ppermute(half, "dp", [(i, i ^ bit) for i in range(dp_count)]))
            bit *= 2
            if bit < dp_count:
                half = (half.astype(F32) + found.pop().astype(F32)).astype(BF16)
        return half, *found

    def total(pair):
        return sum(t.astype(F32) for t in pair)

    grad_norm_part, _ = norm_backward(residual, scale_two, norm_ffn_gain, grad_h_own)
    grad_resid = grad_output.astype(F32) + grad_norm_part
    resid_own = grad_resid.astype(BF16)
    resid_other = swap(resid_own)
    resid_full = jnp.where(
        tensor_rank == 0,
        jnp.concatenate([resid_own, resid_other], axis=0),
        jnp.concatenate([resid_other, resid_own], axis=0),
    )
    *shares, dh_own, dh_other = attend_back(
        heads_meta, dp_count, resid_full, segments, *attn_weights, q, k, v, mixed, log_total,
    )

    length, share_width = resid_full.shape[0], width // dp_count

    def columns(index):
        return lax.dynamic_slice_in_dim(resid_full, index * share_width, share_width, 1)

    resid_shares = [columns(dp_rank)]
    for step in range(1, dp_count):
        resid_shares.append(shift_dp(columns((dp_rank + step) % dp_count), step))
    shares, resid_shares, arrived = together(shares, resid_shares, arrived)
    all_shares = [shares[0]] + [shift_dp(shares[step], step) for step in range(1, dp_count)]
    parts = width // mixed.shape[1]
    sizes = [t.shape[1] // dp_count for t in (query_weight, key_matrix, value_matrix)]
    sizes.append(share_width // parts)
    aligned = all(size % 128 == 0 for size in sizes)
    (gate_half,) = weight_grads(tokens_all, sides[0][1:2], [], arrived[:1])
    all_shares, gate_half = together(all_shares, gate_half)
    block = width // (outer * inner)
    def row_terms(part, step):
        start = (outer_rank + step) % outer * inner
        return [
            lax.dynamic_slice_in_dim(part, (start + (inner_rank + j) % inner) * block, block, 0)
            for j in range(inner)
        ]

    if aligned:

        def blocks_of(steps, all_shares):
            meta = jnp.stack([inner_rank] + [(outer_rank + k) % outer for k in steps])
            return dense_blocks(
                meta.astype(jnp.int32), hidden_all, mixed_all, all_shares, resid_shares, outer, inner
            )

        terms = [None, None, *blocks_of([2], all_shares), None]
    else:
        qkv_part = dot(
            "sd,sa->da", jnp.concatenate(hidden_all, 0), jnp.concatenate(all_shares, 0), BF16
        )
        mix_part = dot(
            "sa,shb->hab",
            jnp.concatenate(mixed_all, 0),
            jnp.concatenate(resid_shares, 0).reshape(length * dp_count, parts, share_width // parts),
            BF16,
        )
        dense_part = jnp.concatenate([qkv_part, mix_part.reshape(width, -1)], axis=1)
        terms = [row_terms(dense_part, k) for k in range(outer)]
    terms[2], mix_found, arrived = together(terms[2], mix_found, arrived)
    mix_line = [
        sum(t[k * rows : (k + 1) * rows].astype(F32) for t in mix_found) for k in range(outer)
    ]
    two, dh_other = line_sum(terms[2]), swap(dh_other)
    carried = shift_outer(mix_line[2].astype(BF16), -1)
    if aligned:
        terms[1], terms[3], terms[0] = blocks_of([1, 3, 0], after(all_shares, terms[2]))
    two, dh_other, terms, arrived = together(two, dh_other, terms, arrived)
    gate_pair = sum_dp(after(gate_half, two))
    scale_one = lax.rsqrt(jnp.mean(x_own * x_own, axis=-1, keepdims=True) + EPS)
    grad_x_part, grad_attn_gain = norm_backward(
        x_own, scale_one, norm_attn_gain, dh_own + dh_other
    )
    grad_input = grad_resid + grad_x_part
    late = after((grad_h_own, residual, scale_two), terms)
    grad_ffn_gain = jnp.sum(late[0] * late[1] * late[2], axis=0)
    gains, hops = jnp.stack([grad_attn_gain, grad_ffn_gain]), hops_of_all()
    one, three = line_sum(terms[1]), line_sum(terms[3])
    two = shift_outer(two, -2)
    halves = weight_grads(tokens_all, sides[0][2:], (upstream_all, sides[0][0]), arrived[1:])
    one, three, terms, gains, carried, halves, two = together(
        one, three, terms, gains, carried, halves, two
    )
    mix_line[1] = mix_line[1].astype(F32) + carried.astype(F32)
    up_half, down_half = halves
    zero = inner_sum(terms[0])
    one, three = shift_outer(one, -1), shift_outer(three, -3)
    other, grad_input, gate_pair, zero, one, three = together(
        exchange(gains, hops[0]), grad_input, gate_pair, zero, one, three
    )
    gains, hops = gains + other, hops[1:]
    reduced = zero.astype(F32)
    for term in (one, two, three):
        reduced = reduced + term.astype(F32)
    reduced = reduced.astype(BF16)
    shapes = [t.shape for t in (query_weight, key_matrix, value_matrix)] + [(width // parts, width)]

    def block_of(from_one, from_three):
        mix = mix_line[0].astype(F32) + from_one.astype(F32) + from_three.astype(F32)
        return (after(residual, reduced) + mix).astype(BF16)

    mix_one, mix_three = mix_line[1].astype(BF16), mix_line[3].astype(BF16)
    if aligned:
        per, dense = outer * inner // parts, []

        def place(pieces, found, dense):
            meta = []
            for k, j, turn in found:
                index = (outer_rank + k) % outer * inner + (inner_rank + j) % inner
                share = (dp_rank - turn) % dp_count
                meta += [index, share, index % per, share * parts + index // per]
            return place_line(jnp.stack(meta).astype(jnp.int32), pieces, sizes, shapes, dense)

        others = range(1, dp_count)
        step = {
            "line": inner_line(reduced[None]),
            "next": shift_outer(reduced[None]),
            "others": [shift_dp(reduced, turn)[None] for turn in others],
            "gains": exchange(gains, hops[0]),
            "done": total(after(gate_pair, reduced)),
        }
        (step,) = together(step)
        gate_sum = step["done"]
        gains, hops = gains + step["gains"], hops[1:]
        lines = [step["line"]]
        held = jnp.concatenate([step["next"], *step["others"]], axis=0)
        up_pair, down_pair = (sum_dp(after(t, step["others"])) for t in (up_half, down_half))
        for k in range(1, outer + 1):
            step = {"line": inner_line(held), "gains": exchange(gains, hops[0]) if hops else gains}
            if k < outer:
                step["next"] = shift_outer(held if k + 1 < outer else held[1:])
            before = [(k - 1, turn) for turn in ([0] if k == 1 else [0, *others])]
            before = [(at - 1 if turn else at, turn) for at, turn in before]
            now = [(k, 0, 0)] * (k < outer) + [(k - 1, 0, turn) for turn in others]
            ready, entries = [held], list(now)
            for j in range(1, inner):
                ready.append(lines[-1][j])
                entries += [(at, j, turn) for at, turn in before]
            if k == 1:
                ready.append(lines[0][0])
                entries.append((0, 0, 0))
            made = place(ready, entries, dense)
            step["dense"] = made
            if k == 3:
                step["done"] = total(after(up_pair, made))
                step["mix"] = shift_outer(after(mix_one, held), -1)
            if k == 4:
                step["done"] = total(after(down_pair, made))
                step["mix"] = shift_outer(after(mix_three, held), -3)
            (step,) = together(step)
            if hops:
                gains, hops = gains + step["gains"], hops[1:]
            if k == 3:
                up_sum, mix_one = step["done"], step["mix"]
            if k == 4:
                down_sum, block_out = step["done"], block_of(mix_one, step["mix"])
            dense, held = step["dense"], step.get("next")
            lines.append(step["line"])
        for j in range(1, inner):
            dense = place([lines[-1][j]], [(outer - 1, j, turn) for turn in others], dense)
    else:
        for hop in hops:
            gains = gains + exchange(gains, hop)
        gate_sum, up_sum, down_sum = (
            total(pair) for pair in (gate_pair, sum_dp(up_half), sum_dp(down_half))
        )
        block_out = block_of(shift_outer(mix_one, -1), shift_outer(mix_three, -3))
        gathered = lax.all_gather(reduced, ("dp", "expert"), axis=0, tiled=True)
        gathered = gathered.reshape(dp_count, width, -1).astype(F32)
        starts = [sum(sizes[:i]) for i in range(len(sizes))]
        dense = [gathered[:, :, at : at + size] for at, size in zip(starts, sizes)]
        dense[:-1] = [t.transpose(1, 0, 2).reshape(width, -1) for t in dense[:-1]]
        mix_w = dense[-1].reshape(dp_count, parts, width // parts, -1)
        dense[-1] = mix_w.transpose(2, 0, 1, 3).reshape(width // parts, width)
    return (
        block_out,
        grad_input,
        gains[0],
        gains[1],
        *dense,
        gate_sum,
        up_sum,
        down_sum,
    )


def solution(mesh):
    tokens = P(("dp", "expert", "tensor"), None)
    whole = P()
    columns = P(None, "tensor")
    hidden_last = P("expert", None, "tensor")
    hidden_mid = P("expert", "tensor", None)
    mixer = P("tensor", None)
    return jax.shard_map(
        body,
        mesh=mesh,
        in_specs=(
            tokens,
            P(("dp", "expert"), None),
            tokens,
            tokens,
            whole,
            whole,
            columns,
            columns,
            columns,
            mixer,
            hidden_last,
            hidden_last,
            hidden_mid,
            tokens,
        ),
        out_specs=(
            tokens,
            tokens,
            whole,
            whole,
            columns,
            columns,
            columns,
            mixer,
            hidden_last,
            hidden_last,
            hidden_mid,
        ),
        check_vma=False,
    )
```

```python
import functools

import jax
import jax.numpy as jnp
import numpy as np
from jax import lax
from jax.experimental import pallas as pl
from jax.experimental.pallas import tpu as pltpu
from jax.sharding import PartitionSpec as P

HEAD_DIM = 64
EPS = 1e-05
ATTN_SCALE = 0.015625
THETA = 10000.0
NEG_FILL = -1e30
F32 = jnp.float32
BF16 = jnp.bfloat16
NO_COST = pl.CostEstimate(flops=1, bytes_accessed=1, transcendentals=0)


def after(values, token):
    return lax.optimization_barrier((values, token))[0]


def swap(values):
    return lax.ppermute(values, "tensor", [(0, 1), (1, 0)])


def shift_dp(values, step):
    count = lax.axis_size("dp")
    return lax.ppermute(values, "dp", [(i, (i + step) % count) for i in range(count)])


def grid_sizes():
    count = lax.axis_size("expert")
    return 4, count // 4


def shift_outer(values, step=1):
    outer, inner = grid_sizes()
    pairs = [(((o + step) % outer) * inner + i, o * inner + i) for o in range(outer) for i in range(inner)]
    return lax.ppermute(values, "expert", pairs)


def shift_inner(values):
    outer, inner = grid_sizes()
    pairs = [(o * inner + (i + 1) % inner, o * inner + i) for o in range(outer) for i in range(inner)]
    return lax.ppermute(values, "expert", pairs)


def inner_line(block):
    line = [block]
    for _ in range(1, grid_sizes()[1]):
        line.append(shift_inner(line[-1]))
    return line


def inner_sum(parts):
    inner, total = len(parts), parts[1 % len(parts)]
    for j in range(2, inner + 1):
        total = shift_inner(total.astype(BF16)).astype(F32) + parts[j % inner].astype(F32)
    return total


def inner_line_of(parts):
    inner, total = len(parts), parts[1 % len(parts)]
    for j in range(2, inner):
        total = shift_inner(total.astype(BF16)).astype(F32) + parts[j].astype(F32)
    return [parts[0]] if inner == 1 else [shift_inner(total.astype(BF16)), parts[0]]


def together(*values):
    return lax.optimization_barrier(values)


def hops_of_all():
    bits = {}
    for axis in ("tensor", "expert", "dp"):
        count = lax.axis_size(axis)
        bits[axis] = [(axis, 1 << i) for i in range(count.bit_length() - 1)]
    return bits["tensor"] + bits["dp"] + bits["expert"]


def exchange(values, hop):
    axis, bit = hop
    return lax.ppermute(values, axis, [(i, i ^ bit) for i in range(lax.axis_size(axis))])


def norm_forward(values, gain_vector):
    inv_scale = lax.rsqrt(jnp.mean(values * values, axis=-1, keepdims=True) + EPS)
    return (values * inv_scale * gain_vector, inv_scale)


def norm_backward(values, inv_scale, gain_vector, upstream):
    weighted = upstream * gain_vector
    inner = jnp.mean(weighted * values, axis=-1, keepdims=True)
    value_gradient = inv_scale * weighted - values * (inv_scale * inv_scale * inv_scale) * inner
    grad_gain = jnp.sum(upstream * values * inv_scale, axis=0)
    return (value_gradient, grad_gain)


def dot(spec, left, right, kind=F32):
    return jnp.einsum(spec, left, right, preferred_element_type=kind)

def dot_t(left, right):
    return lax.dot_general(left, right, (((1,), (1,)), ((), ())), preferred_element_type=F32)


def full_spec(*shape):
    return pl.BlockSpec(shape, lambda *_: (0,) * len(shape))


def rope_tables(length, width):
    half = HEAD_DIM // 2
    frequency = (THETA ** (-np.arange(half, dtype=np.float32) * 2.0 / HEAD_DIM)).astype(np.float32)
    angle = np.arange(length, dtype=np.float32)[:, None] * frequency[None, :]
    cosine, sine = np.cos(angle.astype(np.float64)), np.sin(angle.astype(np.float64))
    cosine = np.concatenate([cosine, cosine], axis=1)
    sine = np.concatenate([-sine, sine], axis=1)
    copies = width // HEAD_DIM
    return np.tile(cosine, (1, copies)).astype(np.float32), np.tile(sine, (1, copies)).astype(np.float32)


def turn(values, cosine, sine):
    width, half = values.shape[1], HEAD_DIM // 2
    copies = width // cosine.shape[1]
    lane = lax.broadcasted_iota(jnp.int32, values.shape, 1)
    first = lax.rem(lane, HEAD_DIM) < half
    other = jnp.where(first, pltpu.roll(values, width - half, 1), pltpu.roll(values, half, 1))
    return values * jnp.concatenate([cosine] * copies, 1) + other * jnp.concatenate([sine] * copies, 1)


def masked_scores(query, key, allowed):
    return jnp.where(allowed, dot_t(query, key) * ATTN_SCALE, NEG_FILL)


def allowed_pairs(segs):
    length = segs.shape[1]
    row = lax.broadcasted_iota(jnp.int32, (length, length), 0)
    column = lax.broadcasted_iota(jnp.int32, (length, length), 1)
    seg_row = segs.astype(F32)
    seg_column = jnp.sum(jnp.where(row == column, seg_row, 0.0), axis=1, keepdims=True)
    return (column <= row) & (seg_row == seg_column)


def row_places(meta, rows):
    own = pl.ds(pl.multiple_of(meta[0] * rows, rows), rows)
    other = pl.ds(pl.multiple_of((1 - meta[0]) * rows, rows), rows)
    return own, other


def attend_kernel(
    meta, own_ref, other_ref, gain_ref, segs, cos_ref, sin_ref, wq, wk, wv, wo,
    hidden_out, q_out, k_out, v_out, mixed_out, log_out, own_out, other_out, x_s, part_s, wo_s, sem,
):
    rows = own_ref.shape[0]
    late = pltpu.make_async_copy(wo, wo_s, sem)
    late.start()
    own, other = row_places(meta, rows)
    x_s[own, :] = own_ref[...].astype(F32)
    x_s[other, :] = other_ref[...].astype(F32)
    x = x_s[...]
    scale = lax.rsqrt(jnp.mean(x * x, axis=-1, keepdims=True) + EPS)
    hidden = (x * scale * gain_ref[...]).astype(BF16)
    hidden_out[...] = hidden
    cosine, sine = cos_ref[...], sin_ref[...]
    q_out[...] = turn(jnp.dot(hidden, wq[...], preferred_element_type=F32), cosine, sine).astype(BF16)
    k_out[...] = turn(jnp.dot(hidden, wk[...], preferred_element_type=F32), cosine, sine).astype(BF16)
    v_out[...] = jnp.dot(hidden, wv[...], preferred_element_type=F32).astype(BF16)
    allowed = allowed_pairs(segs[...])
    heads, heads_kv = wq.shape[1] // HEAD_DIM, wk.shape[1] // HEAD_DIM
    group = heads // heads_kv
    for g in range(heads_kv):
        key = k_out[:, g * HEAD_DIM : (g + 1) * HEAD_DIM]
        value = v_out[:, g * HEAD_DIM : (g + 1) * HEAD_DIM]
        for h in range(g * group, (g + 1) * group):
            at = slice(h * HEAD_DIM, (h + 1) * HEAD_DIM)
            scores = masked_scores(q_out[:, at], key, allowed)
            top = jnp.max(scores, axis=-1, keepdims=True)
            powers = jnp.exp(scores - top)
            power_sum = jnp.sum(powers, axis=-1, keepdims=True)
            log_out[:, h : h + 1] = top + jnp.log(power_sum)
            prob = (powers * (1.0 / power_sum)).astype(BF16)
            mixed_out[:, at] = jnp.dot(prob, value, preferred_element_type=F32).astype(BF16)
    late.wait()
    part_s[...] = jnp.dot(mixed_out[...], wo_s[...], preferred_element_type=F32)
    own_out[...] = part_s[own, :]
    other_out[...] = part_s[other, :]


def attend(meta, own, other, gain, segs, wq, wk, wv, wo):
    rows, width = own.shape
    length = segs.shape[1]
    cosine, sine = rope_tables(length, 128)
    operands = (own, other, gain, segs, cosine, sine, wq, wk, wv, wo)
    shapes = [
        ((length, width), BF16),
        ((length, wq.shape[1]), BF16),
        ((length, wk.shape[1]), BF16),
        ((length, wv.shape[1]), BF16),
        ((length, wq.shape[1]), BF16),
        ((length, 128), F32),
        ((rows, width), F32),
        ((rows, width), F32),
    ]
    return pl.pallas_call(
        attend_kernel,
        out_shape=[jax.ShapeDtypeStruct(*shape) for shape in shapes],
        grid_spec=pltpu.PrefetchScalarGridSpec(
            num_scalar_prefetch=1,
            grid=(1,),
            in_specs=[full_spec(*t.shape) for t in operands[:-1]]
            + [pl.BlockSpec(memory_space=pl.ANY)],
            out_specs=[full_spec(*shape) for shape, _ in shapes],
            scratch_shapes=[pltpu.VMEM((length, width), F32)] * 2
            + [pltpu.VMEM(wo.shape, BF16), pltpu.SemaphoreType.DMA],
        ),
        compiler_params=pltpu.CompilerParams(vmem_limit_bytes=56 * 1024 * 1024),
        cost_estimate=NO_COST,
    )(meta, *operands)


def attend_back_kernel(
    shares, meta, b_ref, segs, cos_ref, sin_ref, wq, wk, wv, wo,
    q_ref, k_ref, v_ref, mixed_ref, log_ref, *refs,
):
    share_outs, (own_out, other_out, grad_s, dq_s, part_s, *late_s, sems) = refs[:shares], refs[shares:]
    late = [
        pltpu.make_async_copy(source, target, sems.at[i])
        for i, (source, target) in enumerate(zip((wq, wk, wv), late_s))
    ]
    for copy in late:
        copy.start()
    own, other = row_places(meta, own_out.shape[0])
    grad_s[...] = dot_t(b_ref[...], wo[...]).astype(BF16)
    cosine, sine = cos_ref[...], -sin_ref[...]
    allowed = allowed_pairs(segs[...])
    wide, narrow = wq.shape[1], wk.shape[1]
    heads, heads_kv = wide // HEAD_DIM, narrow // HEAD_DIM
    group = heads // heads_kv

    def transposed_dot(left, right):
        return lax.dot_general(left, right, (((0,), (0,)), ((), ())), preferred_element_type=F32)

    for g in range(heads_kv):
        there = slice(g * HEAD_DIM, (g + 1) * HEAD_DIM)
        key, value = k_ref[:, there], v_ref[:, there]
        grad_key = grad_value = 0.0
        for h in range(g * group, (g + 1) * group):
            at = slice(h * HEAD_DIM, (h + 1) * HEAD_DIM)
            query, grad = q_ref[:, at], grad_s[:, at]
            prob = jnp.exp(masked_scores(query, key, allowed) - log_ref[:, h : h + 1])
            delta = jnp.sum(grad.astype(F32) * mixed_ref[:, at].astype(F32), axis=-1, keepdims=True)
            grad_scores = (prob * (dot_t(grad, value) - delta) * ATTN_SCALE).astype(BF16)
            dq_s[:, at] = jnp.dot(grad_scores, key, preferred_element_type=F32)
            grad_key = grad_key + transposed_dot(grad_scores, query)
            grad_value = grad_value + transposed_dot(prob.astype(BF16), grad)
        dq_s[:, wide + g * HEAD_DIM : wide + (g + 1) * HEAD_DIM] = grad_key
        at = wide + narrow + g * HEAD_DIM
        dq_s[:, at : at + HEAD_DIM] = grad_value
    dq = turn(dq_s[:, :wide], cosine, sine).astype(BF16)
    dk = turn(dq_s[:, wide : wide + narrow], cosine, sine).astype(BF16)
    dv = dq_s[:, wide + narrow :].astype(BF16)
    for copy in late:
        copy.wait()
    part_s[...] = sum(dot_t(part, held[...]) for part, held in zip((dq, dk, dv), late_s))
    own_out[...] = part_s[own, :]
    other_out[...] = part_s[other, :]
    for r in range(shares):

        @pl.when(meta[1] == r)
        def _():
            for step in range(shares):
                at = 0
                for part in (dq, dk, dv):
                    size = part.shape[1] // shares
                    index = (r + step) % shares
                    share_outs[step][:, at : at + size] = part[:, index * size : (index + 1) * size]
                    at += size


def attend_back(meta, shares, resid, segs, wq, wk, wv, wo, q, k, v, mixed, log_total):
    length, width = resid.shape
    cosine, sine = rope_tables(length, 128)
    operands = (resid, segs, cosine, sine, wq, wk, wv, wo, q, k, v, mixed, log_total)
    columns = wq.shape[1] + wk.shape[1] + wv.shape[1]
    shapes = [((length, columns // shares), BF16)] * shares
    shapes += [((length // 2, width), F32)] * 2
    return pl.pallas_call(
        functools.partial(attend_back_kernel, shares),
        out_shape=[jax.ShapeDtypeStruct(*shape) for shape in shapes],
        grid_spec=pltpu.PrefetchScalarGridSpec(
            num_scalar_prefetch=1,
            grid=(1,),
            in_specs=[
                pl.BlockSpec(memory_space=pl.ANY) if 4 <= i < 7 else full_spec(*t.shape)
                for i, t in enumerate(operands)
            ],
            out_specs=[full_spec(*shape) for shape, _ in shapes],
            scratch_shapes=[
                pltpu.VMEM((length, wq.shape[1]), BF16),
                pltpu.VMEM((length, columns), F32),
                pltpu.VMEM((length, width), F32),
            ]
            + [pltpu.VMEM(t.shape, BF16) for t in (wq, wk, wv)]
            + [pltpu.SemaphoreType.DMA((3,))],
        ),
        compiler_params=pltpu.CompilerParams(vmem_limit_bytes=56 * 1024 * 1024),
        cost_estimate=NO_COST,
    )(meta, *operands)


def expert_kernel(inner, aliased, experts, meta, *refs):
    blocks, ups, tables = (refs[i * inner : (i + 1) * inner] for i in range(3))
    refs = refs[3 * inner :]
    weight_refs, refs = refs[:6], refs[6 + aliased :]
    tokens_out, upstream_out = refs[:2]
    used_out, gate_out, up_out = refs[2:4], refs[4:6], refs[6:8]
    mix_out, in_out = refs[8 : 8 + inner], refs[8 + inner : 8 + 2 * inner]
    table, mix_total, in_total = refs[8 + 2 * inner :]
    rows, width = blocks[0].shape
    expert = pl.program_id(0)

    def place(j):
        return pl.ds(pl.multiple_of(lax.rem(meta[1] + j, inner) * rows, rows), rows)

    @pl.when(expert == 0)
    def _():
        for j in range(inner):
            tokens_out[place(j), :] = blocks[j][...]
            upstream_out[place(j), :] = ups[j][...]
            table[place(j), :] = tables[j][...].astype(F32)
        mix_total[...] = jnp.zeros_like(mix_total)
        in_total[...] = jnp.zeros_like(in_total)

    lane = lax.broadcasted_iota(jnp.int32, table.shape, 1)
    wanted = (lax.rem(lane, experts) == meta[2] + expert) & (lane < 3 * experts)
    weight = jnp.sum(jnp.where(wanted, table[...], 0.0), axis=1, keepdims=True)
    for half in range(2):
        gate, up, down = (weight_refs[2 * i + half][0] for i in range(3))
        pre_gate = jnp.dot(tokens_out[...], gate, preferred_element_type=F32)
        pre_up = jnp.dot(tokens_out[...], up, preferred_element_type=F32)
        grad_act = dot_t(upstream_out[...], down) * weight
        gate_sigmoid = 1.0 / (1.0 + jnp.exp(-pre_gate))
        silu = pre_gate * gate_sigmoid
        used = (silu * pre_up * weight).astype(BF16)
        grad_gate = grad_act * pre_up * gate_sigmoid * (1.0 + pre_gate * (1.0 - gate_sigmoid))
        grad_up = grad_act * silu
        used_out[half][0] = used
        gate_out[half][0] = grad_gate.astype(BF16)
        up_out[half][0] = grad_up.astype(BF16)
        mix_total[...] += jnp.dot(used, down, preferred_element_type=F32)
        in_total[...] += dot_t((grad_gate * weight).astype(BF16), gate) + dot_t(
            (grad_up * weight).astype(BF16), up
        )

    @pl.when(expert == pl.num_programs(0) - 1)
    def _():
        for j in range(inner):
            mix_out[j][...] = mix_total[place(j), :].astype(BF16)
            in_out[j][...] = in_total[place(j), :].astype(BF16)


def run_experts(meta, chunk_index, blocks, payloads, expert_weights, buffers, total, expert_count):
    inner, rows, width = len(blocks), blocks[0].shape[0], expert_weights[0].shape[1]
    firsts = [t.shape[1] // width - 1 for t in payloads]
    experts, half = expert_weights[0].shape[0], expert_weights[0].shape[2]
    chunk = inner * rows
    extra = 128
    by_chunk = pl.BlockSpec((chunk, width), lambda e, m: (m[0], 0))
    per_expert = pl.BlockSpec((1, chunk, half), lambda e, m: (e, m[0], 0))
    spread = pl.BlockSpec((1, width, half), lambda e, m: (e, 0, 0))
    tall = pl.BlockSpec((1, half, width), lambda e, m: (e, 0, 0))
    line = pl.BlockSpec((rows, width), lambda e, m: (chunk_index, 0))
    shapes = [jax.ShapeDtypeStruct((total, width), BF16)] * 2
    shapes += [jax.ShapeDtypeStruct((experts, total, half), BF16)] * 6
    shapes += [jax.ShapeDtypeStruct((total // inner, width), BF16)] * inner
    first = 1 + 3 * inner + 6
    return pl.pallas_call(
        functools.partial(expert_kernel, inner, len(buffers), expert_count),
        out_shape=shapes + [jax.ShapeDtypeStruct((rows, width), BF16)] * inner,
        grid_spec=pltpu.PrefetchScalarGridSpec(
            num_scalar_prefetch=1,
            grid=(experts,),
            in_specs=[full_spec(rows, width)] * inner
            + [pl.BlockSpec((rows, width), lambda e, m, at=at: (0, at)) for at in firsts]
            + [
                pl.BlockSpec((rows, extra), lambda e, m, at=at: (0, (at + 1) * (width // extra)))
                for at in firsts
            ]
            + [spread] * 4
            + [tall] * 2
            + [pl.BlockSpec(memory_space=pl.ANY)] * len(buffers),
            out_specs=[by_chunk] * 2
            + [per_expert] * 6
            + [line] * inner
            + [full_spec(rows, width)] * inner,
            scratch_shapes=[
                pltpu.VMEM((chunk, extra), F32),
                pltpu.VMEM((chunk, width), F32),
                pltpu.VMEM((chunk, width), F32),
            ],
        ),
        input_output_aliases={first + i: i for i in range(len(buffers))},
        compiler_params=pltpu.CompilerParams(vmem_limit_bytes=56 * 1024 * 1024),
        cost_estimate=NO_COST,
    )(meta, *blocks, *payloads, *payloads, *expert_weights, *buffers)


def weight_grads_kernel(count, downs, summed, tokens, *refs):
    sides, down, refs = refs[:count], refs[count : count + downs], refs[count + downs :]
    made = count + (downs > 0)
    added, outs = refs[: made * summed], refs[made * summed :]

    def store(index, at, value):
        if summed:
            value = value + added[index][at].astype(F32)
        outs[index][at] = value.astype(BF16)

    def product(left, right):
        return lax.dot_general(left, right, (((0,), (0,)), ((), ())), preferred_element_type=F32)

    for index, side in enumerate(sides):
        for e in range(side.shape[0]):
            store(index, e, product(tokens[...], side[e]))
    if downs:
        upstream, used = down
        store(count, 0, product(used[0], upstream[...]))


def weight_grads(tokens, sides, down, added):
    (experts, total, half), width = sides[0].shape, tokens.shape[1]
    steps = 2 * experts
    high, low = width // steps, half // 2
    spread = pl.BlockSpec((experts, high, half), lambda r: (0, r, 0))
    tall = pl.BlockSpec((1, low, width), lambda r: (lax.div(r, 2), lax.rem(r, 2), 0))
    specs = [spread] * len(sides) + [tall] * (len(down) > 0)
    shapes = [(experts, width, half)] * len(sides) + [(experts, half, width)] * (len(down) > 0)
    down_specs = [
        full_spec(total, width),
        pl.BlockSpec((1, total, low), lambda r: (lax.div(r, 2), 0, lax.rem(r, 2))),
    ]
    return pl.pallas_call(
        functools.partial(weight_grads_kernel, len(sides), len(down), len(added) > 0),
        out_shape=[jax.ShapeDtypeStruct(shape, BF16) for shape in shapes],
        grid=(steps,),
        in_specs=[pl.BlockSpec((total, high), lambda r: (0, r))]
        + [full_spec(experts, total, half)] * len(sides)
        + down_specs[: len(down)]
        + specs * (len(added) > 0),
        out_specs=specs,
        compiler_params=pltpu.CompilerParams(vmem_limit_bytes=62 * 1024 * 1024),
        cost_estimate=NO_COST,
    )(tokens, *sides, *down, *added)


def place_kernel(sizes, counts, meta, *refs):
    blocks, outs = refs[: len(counts)], refs[-len(sizes) :]
    step, first = pl.program_id(0), 0
    for block_ref, count in zip(blocks, counts):

        @pl.when((step >= first) & (step < first + count))
        def _():
            at = 0
            for size, out in zip(sizes, outs):
                out[...] = block_ref[0, :, at : at + size].astype(F32)
                at += size

        first += count


def place_line(meta, pieces, sizes, shapes, buffers):
    counts, (_, rows, width) = [t.shape[0] for t in pieces], pieces[0].shape
    firsts = [sum(counts[:i]) for i in range(len(counts))]
    taken = [
        pl.BlockSpec(
            (1, rows, width), lambda i, m, at=at, n=n: (jnp.minimum(jnp.maximum(i - at, 0), n - 1), 0, 0)
        )
        for at, n in zip(firsts, counts)
    ]
    low = [pl.BlockSpec((rows, size), lambda i, m: (m[4 * i], m[4 * i + 1])) for size in sizes[:-1]]
    low.append(pl.BlockSpec((rows, sizes[-1]), lambda i, m: (m[4 * i + 2], m[4 * i + 3])))
    return pl.pallas_call(
        functools.partial(place_kernel, sizes, counts),
        out_shape=[jax.ShapeDtypeStruct(shape, F32) for shape in shapes],
        grid_spec=pltpu.PrefetchScalarGridSpec(
            num_scalar_prefetch=1,
            grid=(sum(counts),),
            in_specs=taken + [pl.BlockSpec(memory_space=pl.ANY)] * len(buffers),
            out_specs=low,
        ),
        input_output_aliases={1 + len(pieces) + i: i for i in range(len(buffers))},
        cost_estimate=NO_COST,
    )(meta, *pieces, *buffers)


def dense_kernel(count, inner, meta, *refs):
    hidden, mixed, shares, resids = (refs[i * count : (i + 1) * count] for i in range(4))
    outs, scratch = refs[4 * count : -1], refs[-1]
    size, step = shares[0].shape[1], pl.program_id(0)

    def summed(lefts, rights):
        return sum(
            lax.dot_general(
                left[...], right[...], (((0,), (0,)), ((), ())), preferred_element_type=F32
            )
            for left, right in zip(lefts, rights)
        )

    scratch[:, :size] = summed(hidden, shares).astype(BF16)
    scratch[:, size:] = summed(mixed, resids).astype(BF16)
    rows = outs[0].shape[0]
    for k in range(len(outs) // inner):

        @pl.when(step == k)
        def _():
            for j in range(inner):
                start = pl.multiple_of(lax.rem(meta[0] + j, inner) * rows, rows)
                outs[k * inner + j][...] = scratch[pl.ds(start, rows), :]


def dense_blocks(meta, hidden, mixed, shares, resids, outer, inner):
    count, (length, width), size = len(hidden), hidden[0].shape, shares[0].shape[1]
    high, wide, steps = width // outer, mixed[0].shape[1], meta.shape[0] - 1
    part = resids[0].shape[1] * wide // width
    per = wide // high
    block = (high // inner, size + part)
    made = pl.pallas_call(
        functools.partial(dense_kernel, count, inner),
        out_shape=[jax.ShapeDtypeStruct(block, BF16)] * (steps * inner),
        grid_spec=pltpu.PrefetchScalarGridSpec(
            num_scalar_prefetch=1,
            grid=(steps,),
            in_specs=[pl.BlockSpec((length, high), lambda i, m: (0, m[1 + i]))] * count
            + [pl.BlockSpec((length, high), lambda i, m: (0, lax.rem(m[1 + i], per)))] * count
            + [full_spec(length, size)] * count
            + [pl.BlockSpec((length, part), lambda i, m: (0, lax.div(m[1 + i], per)))] * count,
            out_specs=[full_spec(*block)] * (steps * inner),
            scratch_shapes=[pltpu.VMEM((high, size + part), BF16)],
        ),
        compiler_params=pltpu.CompilerParams(vmem_limit_bytes=56 * 1024 * 1024),
        cost_estimate=NO_COST,
    )(meta, *hidden, *mixed, *shares, *resids)
    return [made[i * inner : (i + 1) * inner] for i in range(steps)]


def body(
    activations,
    segments,
    routes,
    route_weights,
    norm_attn_gain,
    norm_ffn_gain,
    query_weight,
    key_matrix,
    value_matrix,
    output_projection_weight,
    expert_gate,
    expert_up,
    expert_down,
    grad_output,
):
    tensor_rank = lax.axis_index("tensor")
    dp_rank = lax.axis_index("dp")
    dp_count = lax.axis_size("dp")
    outer, inner = grid_sizes()
    outer_rank = lax.axis_index("expert") // inner
    inner_rank = lax.axis_index("expert") % inner
    rows, width = activations.shape
    experts_here = expert_gate.shape[0]
    expert_count = experts_here * lax.axis_size("expert")

    named = routes[:, :, None] == jnp.arange(expert_count, dtype=jnp.int32)
    weight_table = jnp.sum(jnp.where(named, route_weights[:, :, None], 0.0), axis=1)
    high = lax.reduce_precision(weight_table, 8, 7)
    middle = lax.reduce_precision(weight_table - high, 8, 7)
    low = weight_table - high - middle
    table = jnp.concatenate([high, middle, low], axis=1).astype(BF16)
    table = jnp.pad(table, ((0, 0), (0, -table.shape[1] % 128)))
    payload = jnp.concatenate([grad_output, table], axis=1)
    up_one, up_three, up_line = shift_outer(payload, 1), shift_outer(payload, -1), inner_line(payload)
    heads_meta = jnp.stack([tensor_rank, dp_rank]).astype(jnp.int32)
    attn_weights = (query_weight, key_matrix, value_matrix, output_projection_weight)
    hidden, q, k, v, mixed, log_total, attn_own, attn_other = attend(
        heads_meta, activations, swap(activations), norm_attn_gain, segments, *attn_weights
    )
    x_own = activations.astype(F32)
    attn_own, attn_other, up_one, up_three, up_line = together(
        attn_own, attn_other, up_one, up_three, up_line
    )
    up_three = inner_line(up_three)
    residual = x_own + attn_own + swap(attn_other)
    normed_two, scale_two = norm_forward(residual, norm_ffn_gain)

    expert_weights = []
    for weights_own in (expert_gate, expert_up, expert_down):
        expert_weights += [weights_own, swap(weights_own)]
    first_expert = lax.axis_index("expert") * experts_here

    h_own = normed_two.astype(BF16)
    h_one, h_line = shift_outer(h_own, 1), inner_line(h_own)
    h_one, h_line, up_one, up_three = together(h_one, h_line, up_one, up_three)
    both = jnp.concatenate([h_one, up_one], axis=1)

    def experts_on(chunk, buffers, blocks, payloads):
        meta = jnp.stack([(outer_rank + chunk) % outer, inner_rank, first_expert])
        made = run_experts(
            meta.astype(jnp.int32), chunk, blocks, payloads, expert_weights, buffers,
            outer * inner * rows, expert_count,
        )
        return list(made[: 8 + inner]), made[8 + inner :]

    def line_sum(parts):
        return inner_sum(parts).astype(BF16)

    others_rows = [shift_dp(activations, step) for step in range(1, dp_count)]
    line, both = inner_line(both), shift_outer(both, 1)
    made = experts_on(0, [], h_line, up_line)
    made, line, both, others_rows = together(made, line, both, others_rows)
    buffers, in_zero = made
    others_swapped = [swap(t) for t in others_rows]
    made = experts_on(1, buffers, line, line)
    line, both = inner_line(both), shift_outer(both, 1)
    mixed_all = [mixed] + [shift_dp(mixed, step) for step in range(1, dp_count)]
    made, line, both, mixed_all, others_swapped = together(
        made, line, both, mixed_all, others_swapped
    )
    buffers, parts = made
    made = experts_on(2, buffers, line, line)
    line, sum_one = inner_line(both[:, :width]), line_sum(parts)
    hidden_all = [hidden]
    for step in range(1, dp_count):
        other = jnp.concatenate([others_rows[step - 1], others_swapped[step - 1]], axis=0)
        other = jnp.where(tensor_rank == 0, other, jnp.roll(other, rows, 0)).astype(F32)
        hidden_all.append(norm_forward(other, norm_attn_gain)[0].astype(BF16))
    made, line, sum_one, hidden_all = together(made, line, sum_one, hidden_all)
    buffers, parts = made
    sum_one, sum_two = shift_outer(sum_one, -1), line_sum(parts)
    made = experts_on(3, buffers, line, up_three)
    made, sum_one, sum_two, in_zero = together(made, sum_one, sum_two, in_zero)
    buffers, parts = made
    tokens_all, upstream_all, *pairs = buffers
    pairs, mix_lines = pairs[:6], pairs[6:]
    sides = [[pairs[at + half] for at in (0, 2, 4)] for half in range(2)]
    peers = weight_grads(tokens_all, sides[1][1:], (upstream_all, sides[1][0]), [])
    sum_two, sum_three, sum_zero = shift_outer(sum_two, -2), line_sum(parts), inner_sum(in_zero)
    sum_two, sum_three, sum_zero, peers = together(sum_two, sum_three, sum_zero, peers)
    mix_lines = after(mix_lines, sum_three)
    mix_found = inner_line_of(mix_lines)
    sum_three, arrived = shift_outer(sum_three, -3), [swap(peer) for peer in peers]
    grad_h_own = sum_zero.astype(F32)
    for term in (sum_one, sum_two, sum_three):
        grad_h_own = grad_h_own + term.astype(F32)

    def sum_dp(half):
        bit, found = 1, []
        while bit < dp_count:
            found.append(lax.ppermute(half, "dp", [(i, i ^ bit) for i in range(dp_count)]))
            bit *= 2
            if bit < dp_count:
                half = (half.astype(F32) + found.pop().astype(F32)).astype(BF16)
        return half, *found

    def total(pair):
        return sum(t.astype(F32) for t in pair)

    grad_norm_part, _ = norm_backward(residual, scale_two, norm_ffn_gain, grad_h_own)
    grad_resid = grad_output.astype(F32) + grad_norm_part
    resid_own = grad_resid.astype(BF16)
    resid_other = swap(resid_own)
    resid_full = jnp.where(
        tensor_rank == 0,
        jnp.concatenate([resid_own, resid_other], axis=0),
        jnp.concatenate([resid_other, resid_own], axis=0),
    )
    *shares, dh_own, dh_other = attend_back(
        heads_meta, dp_count, resid_full, segments, *attn_weights, q, k, v, mixed, log_total,
    )

    length, share_width = resid_full.shape[0], width // dp_count

    def columns(index):
        return lax.dynamic_slice_in_dim(resid_full, index * share_width, share_width, 1)

    resid_shares = [columns(dp_rank)]
    for step in range(1, dp_count):
        resid_shares.append(shift_dp(columns((dp_rank + step) % dp_count), step))
    shares, resid_shares, arrived = together(shares, resid_shares, arrived)
    all_shares = [shares[0]] + [shift_dp(shares[step], step) for step in range(1, dp_count)]
    parts = width // mixed.shape[1]
    sizes = [t.shape[1] // dp_count for t in (query_weight, key_matrix, value_matrix)]
    sizes.append(share_width // parts)
    aligned = all(size % 128 == 0 for size in sizes)
    (gate_half,) = weight_grads(tokens_all, sides[0][1:2], [], arrived[:1])
    all_shares, gate_half = together(all_shares, gate_half)
    block = width // (outer * inner)
    def row_terms(part, step):
        start = (outer_rank + step) % outer * inner
        return [
            lax.dynamic_slice_in_dim(part, (start + (inner_rank + j) % inner) * block, block, 0)
            for j in range(inner)
        ]

    if aligned:

        def blocks_of(steps, all_shares):
            meta = jnp.stack([inner_rank] + [(outer_rank + k) % outer for k in steps])
            return dense_blocks(
                meta.astype(jnp.int32), hidden_all, mixed_all, all_shares, resid_shares, outer, inner
            )

        terms = [None, None, *blocks_of([2], all_shares), None]
    else:
        qkv_part = dot(
            "sd,sa->da", jnp.concatenate(hidden_all, 0), jnp.concatenate(all_shares, 0), BF16
        )
        mix_part = dot(
            "sa,shb->hab",
            jnp.concatenate(mixed_all, 0),
            jnp.concatenate(resid_shares, 0).reshape(length * dp_count, parts, share_width // parts),
            BF16,
        )
        dense_part = jnp.concatenate([qkv_part, mix_part.reshape(width, -1)], axis=1)
        terms = [row_terms(dense_part, k) for k in range(outer)]
    terms[2], mix_found, arrived = together(terms[2], mix_found, arrived)
    mix_line = [
        sum(t[k * rows : (k + 1) * rows].astype(F32) for t in mix_found) for k in range(outer)
    ]
    two, dh_other = line_sum(terms[2]), swap(dh_other)
    carried = shift_outer(mix_line[2].astype(BF16), -1)
    if aligned:
        terms[1], terms[3], terms[0] = blocks_of([1, 3, 0], after(all_shares, terms[2]))
    two, dh_other, terms, arrived = together(two, dh_other, terms, arrived)
    gate_pair = sum_dp(after(gate_half, two))
    scale_one = lax.rsqrt(jnp.mean(x_own * x_own, axis=-1, keepdims=True) + EPS)
    grad_x_part, grad_attn_gain = norm_backward(
        x_own, scale_one, norm_attn_gain, dh_own + dh_other
    )
    grad_input = grad_resid + grad_x_part
    late = after((grad_h_own, residual, scale_two), terms)
    grad_ffn_gain = jnp.sum(late[0] * late[1] * late[2], axis=0)
    gains, hops = jnp.stack([grad_attn_gain, grad_ffn_gain]), hops_of_all()
    one, three = line_sum(terms[1]), line_sum(terms[3])
    two = shift_outer(two, -2)
    halves = weight_grads(tokens_all, sides[0][2:], (upstream_all, sides[0][0]), arrived[1:])
    one, three, terms, gains, carried, halves, two = together(
        one, three, terms, gains, carried, halves, two
    )
    mix_line[1] = mix_line[1].astype(F32) + carried.astype(F32)
    up_half, down_half = halves
    zero = inner_sum(terms[0])
    one, three = shift_outer(one, -1), shift_outer(three, -3)
    other, grad_input, gate_pair, zero, one, three = together(
        exchange(gains, hops[0]), grad_input, gate_pair, zero, one, three
    )
    gains, hops = gains + other, hops[1:]
    reduced = zero.astype(F32)
    for term in (one, two, three):
        reduced = reduced + term.astype(F32)
    reduced = reduced.astype(BF16)
    shapes = [t.shape for t in (query_weight, key_matrix, value_matrix)] + [(width // parts, width)]

    def block_before(from_one):
        return after(residual, reduced) + (mix_line[0].astype(F32) + from_one.astype(F32))

    def block_of(before, from_three):
        return (before + from_three.astype(F32)).astype(BF16)

    mix_one, mix_three = mix_line[1].astype(BF16), mix_line[3].astype(BF16)
    if aligned:
        per, dense = outer * inner // parts, []

        def place(pieces, found, dense):
            meta = []
            for k, j, turn in found:
                index = (outer_rank + k) % outer * inner + (inner_rank + j) % inner
                share = (dp_rank - turn) % dp_count
                meta += [index, share, index % per, share * parts + index // per]
            return place_line(jnp.stack(meta).astype(jnp.int32), pieces, sizes, shapes, dense)

        others = range(1, dp_count)
        step = {
            "line": inner_line(reduced[None]),
            "next": shift_outer(reduced[None]),
            "others": [shift_dp(reduced, turn)[None] for turn in others],
            "gains": exchange(gains, hops[0]),
            "done": total(after(gate_pair, reduced)),
        }
        (step,) = together(step)
        gate_sum = step["done"]
        gains, hops = gains + step["gains"], hops[1:]
        lines = [step["line"]]
        held = jnp.concatenate([step["next"], *step["others"]], axis=0)
        up_pair, down_pair = (sum_dp(after(t, step["others"])) for t in (up_half, down_half))
        for k in range(1, outer + 1):
            step = {"line": inner_line(held), "gains": exchange(gains, hops[0]) if hops else gains}
            if k < outer:
                step["next"] = shift_outer(held if k + 1 < outer else held[1:])
            before = [(k - 1, turn) for turn in ([0] if k == 1 else [0, *others])]
            before = [(at - 1 if turn else at, turn) for at, turn in before]
            now = [(k, 0, 0)] * (k < outer) + [(k - 1, 0, turn) for turn in others]
            ready, entries = [held], list(now)
            for j in range(1, inner):
                ready.append(lines[-1][j])
                entries += [(at, j, turn) for at, turn in before]
            if k == 1:
                ready.append(lines[0][0])
                entries.append((0, 0, 0))
            made = place(ready, entries, dense)
            step["dense"] = made
            if k == 3:
                step["done"] = total(after(up_pair, made))
                step["mix"] = shift_outer(after(mix_one, held), -1)
            if k == 4:
                step["done"] = total(after(down_pair, made))
                step["mix"] = shift_outer(after(mix_three, held), -3)
                step["block"] = block_before(mix_one)
            (step,) = together(step)
            if hops:
                gains, hops = gains + step["gains"], hops[1:]
            if k == 3:
                up_sum, mix_one = step["done"], step["mix"]
            if k == 4:
                down_sum, block_out = step["done"], block_of(step["block"], step["mix"])
            dense, held = step["dense"], step.get("next")
            lines.append(step["line"])
        for j in range(1, inner):
            dense = place([lines[-1][j]], [(outer - 1, j, turn) for turn in others], dense)
    else:
        for hop in hops:
            gains = gains + exchange(gains, hop)
        gate_sum, up_sum, down_sum = (
            total(pair) for pair in (gate_pair, sum_dp(up_half), sum_dp(down_half))
        )
        block_out = block_of(block_before(shift_outer(mix_one, -1)), shift_outer(mix_three, -3))
        gathered = lax.all_gather(reduced, ("dp", "expert"), axis=0, tiled=True)
        gathered = gathered.reshape(dp_count, width, -1).astype(F32)
        starts = [sum(sizes[:i]) for i in range(len(sizes))]
        dense = [gathered[:, :, at : at + size] for at, size in zip(starts, sizes)]
        dense[:-1] = [t.transpose(1, 0, 2).reshape(width, -1) for t in dense[:-1]]
        mix_w = dense[-1].reshape(dp_count, parts, width // parts, -1)
        dense[-1] = mix_w.transpose(2, 0, 1, 3).reshape(width // parts, width)
    return (
        block_out,
        grad_input,
        gains[0],
        gains[1],
        *dense,
        gate_sum,
        up_sum,
        down_sum,
    )


def solution(mesh):
    tokens = P(("dp", "expert", "tensor"), None)
    whole = P()
    columns = P(None, "tensor")
    hidden_last = P("expert", None, "tensor")
    hidden_mid = P("expert", "tensor", None)
    mixer = P("tensor", None)
    return jax.shard_map(
        body,
        mesh=mesh,
        in_specs=(
            tokens,
            P(("dp", "expert"), None),
            tokens,
            tokens,
            whole,
            whole,
            columns,
            columns,
            columns,
            mixer,
            hidden_last,
            hidden_last,
            hidden_mid,
            tokens,
        ),
        out_specs=(
            tokens,
            tokens,
            whole,
            whole,
            columns,
            columns,
            columns,
            mixer,
            hidden_last,
            hidden_last,
            hidden_mid,
        ),
        check_vma=False,
    )
```

```python
import functools

import jax
import jax.numpy as jnp
import numpy as np
from jax import lax
from jax.experimental import pallas as pl
from jax.experimental.pallas import tpu as pltpu
from jax.sharding import PartitionSpec as P

HEAD_DIM = 64
EPS = 1e-05
ATTN_SCALE = 0.015625
THETA = 10000.0
NEG_FILL = -1e30
F32 = jnp.float32
BF16 = jnp.bfloat16
NO_COST = pl.CostEstimate(flops=1, bytes_accessed=1, transcendentals=0)


def after(values, token):
    return lax.optimization_barrier((values, token))[0]


def swap(values):
    return lax.ppermute(values, "tensor", [(0, 1), (1, 0)])


def shift_dp(values, step):
    count = lax.axis_size("dp")
    return lax.ppermute(values, "dp", [(i, (i + step) % count) for i in range(count)])


def grid_sizes():
    count = lax.axis_size("expert")
    return 4, count // 4


def shift_outer(values, step=1):
    outer, inner = grid_sizes()
    pairs = [(((o + step) % outer) * inner + i, o * inner + i) for o in range(outer) for i in range(inner)]
    return lax.ppermute(values, "expert", pairs)


def shift_inner(values):
    outer, inner = grid_sizes()
    pairs = [(o * inner + (i + 1) % inner, o * inner + i) for o in range(outer) for i in range(inner)]
    return lax.ppermute(values, "expert", pairs)


def inner_line(block):
    line = [block]
    for _ in range(1, grid_sizes()[1]):
        line.append(shift_inner(line[-1]))
    return line


def inner_sum(parts):
    inner, total = len(parts), parts[1 % len(parts)]
    for j in range(2, inner + 1):
        total = shift_inner(total.astype(BF16)).astype(F32) + parts[j % inner].astype(F32)
    return total


def inner_line_of(parts):
    inner, total = len(parts), parts[1 % len(parts)]
    for j in range(2, inner):
        total = shift_inner(total.astype(BF16)).astype(F32) + parts[j].astype(F32)
    return [parts[0]] if inner == 1 else [shift_inner(total.astype(BF16)), parts[0]]


def together(*values):
    return lax.optimization_barrier(values)


def hops_of_all():
    bits = {}
    for axis in ("tensor", "expert", "dp"):
        count = lax.axis_size(axis)
        bits[axis] = [(axis, 1 << i) for i in range(count.bit_length() - 1)]
    return bits["tensor"] + bits["dp"] + bits["expert"]


def exchange(values, hop):
    axis, bit = hop
    return lax.ppermute(values, axis, [(i, i ^ bit) for i in range(lax.axis_size(axis))])


def norm_forward(values, gain_vector):
    inv_scale = lax.rsqrt(jnp.mean(values * values, axis=-1, keepdims=True) + EPS)
    return (values * inv_scale * gain_vector, inv_scale)


def norm_backward(values, inv_scale, gain_vector, upstream):
    weighted = upstream * gain_vector
    inner = jnp.mean(weighted * values, axis=-1, keepdims=True)
    value_gradient = inv_scale * weighted - values * (inv_scale * inv_scale * inv_scale) * inner
    grad_gain = jnp.sum(upstream * values * inv_scale, axis=0)
    return (value_gradient, grad_gain)


def dot(spec, left, right, kind=F32):
    return jnp.einsum(spec, left, right, preferred_element_type=kind)

def dot_t(left, right):
    return lax.dot_general(left, right, (((1,), (1,)), ((), ())), preferred_element_type=F32)


def full_spec(*shape):
    return pl.BlockSpec(shape, lambda *_: (0,) * len(shape))


def rope_tables(length, width):
    half = HEAD_DIM // 2
    frequency = (THETA ** (-np.arange(half, dtype=np.float32) * 2.0 / HEAD_DIM)).astype(np.float32)
    angle = np.arange(length, dtype=np.float32)[:, None] * frequency[None, :]
    cosine, sine = np.cos(angle.astype(np.float64)), np.sin(angle.astype(np.float64))
    cosine = np.concatenate([cosine, cosine], axis=1)
    sine = np.concatenate([-sine, sine], axis=1)
    copies = width // HEAD_DIM
    return np.tile(cosine, (1, copies)).astype(np.float32), np.tile(sine, (1, copies)).astype(np.float32)


def turn(values, cosine, sine):
    width, half = values.shape[1], HEAD_DIM // 2
    copies = width // cosine.shape[1]
    lane = lax.broadcasted_iota(jnp.int32, values.shape, 1)
    first = lax.rem(lane, HEAD_DIM) < half
    other = jnp.where(first, pltpu.roll(values, width - half, 1), pltpu.roll(values, half, 1))
    return values * jnp.concatenate([cosine] * copies, 1) + other * jnp.concatenate([sine] * copies, 1)


def masked_scores(query, key, allowed):
    return jnp.where(allowed, dot_t(query, key) * ATTN_SCALE, NEG_FILL)


def allowed_pairs(segs):
    length = segs.shape[1]
    row = lax.broadcasted_iota(jnp.int32, (length, length), 0)
    column = lax.broadcasted_iota(jnp.int32, (length, length), 1)
    seg_row = segs.astype(F32)
    seg_column = jnp.sum(jnp.where(row == column, seg_row, 0.0), axis=1, keepdims=True)
    return (column <= row) & (seg_row == seg_column)


def row_places(meta, rows):
    own = pl.ds(pl.multiple_of(meta[0] * rows, rows), rows)
    other = pl.ds(pl.multiple_of((1 - meta[0]) * rows, rows), rows)
    return own, other


def attend_kernel(
    meta, own_ref, other_ref, gain_ref, segs, cos_ref, sin_ref, wq, wk, wv, wo,
    hidden_out, q_out, k_out, v_out, mixed_out, log_out, own_out, other_out, x_s, part_s,
    wk_s, wv_s, wo_s, sems,
):
    rows = own_ref.shape[0]
    late = [
        pltpu.make_async_copy(source, target, sems.at[i])
        for i, (source, target) in enumerate(zip((wk, wv, wo), (wk_s, wv_s, wo_s)))
    ]
    for copy in late:
        copy.start()
    own, other = row_places(meta, rows)
    x_s[own, :] = own_ref[...].astype(F32)
    x_s[other, :] = other_ref[...].astype(F32)
    x = x_s[...]
    scale = lax.rsqrt(jnp.mean(x * x, axis=-1, keepdims=True) + EPS)
    hidden = (x * scale * gain_ref[...]).astype(BF16)
    hidden_out[...] = hidden
    cosine, sine = cos_ref[...], sin_ref[...]
    q_out[...] = turn(jnp.dot(hidden, wq[...], preferred_element_type=F32), cosine, sine).astype(BF16)
    late[0].wait()
    late[1].wait()
    k_out[...] = turn(jnp.dot(hidden, wk_s[...], preferred_element_type=F32), cosine, sine).astype(BF16)
    v_out[...] = jnp.dot(hidden, wv_s[...], preferred_element_type=F32).astype(BF16)
    allowed = allowed_pairs(segs[...])
    heads, heads_kv = wq.shape[1] // HEAD_DIM, wk.shape[1] // HEAD_DIM
    group = heads // heads_kv
    for g in range(heads_kv):
        key = k_out[:, g * HEAD_DIM : (g + 1) * HEAD_DIM]
        value = v_out[:, g * HEAD_DIM : (g + 1) * HEAD_DIM]
        for h in range(g * group, (g + 1) * group):
            at = slice(h * HEAD_DIM, (h + 1) * HEAD_DIM)
            scores = masked_scores(q_out[:, at], key, allowed)
            top = jnp.max(scores, axis=-1, keepdims=True)
            powers = jnp.exp(scores - top)
            power_sum = jnp.sum(powers, axis=-1, keepdims=True)
            log_out[:, h : h + 1] = top + jnp.log(power_sum)
            prob = (powers * (1.0 / power_sum)).astype(BF16)
            mixed_out[:, at] = jnp.dot(prob, value, preferred_element_type=F32).astype(BF16)
    late[2].wait()
    part_s[...] = jnp.dot(mixed_out[...], wo_s[...], preferred_element_type=F32)
    own_out[...] = part_s[own, :]
    other_out[...] = part_s[other, :]


def attend(meta, own, other, gain, segs, wq, wk, wv, wo):
    rows, width = own.shape
    length = segs.shape[1]
    cosine, sine = rope_tables(length, 128)
    operands = (own, other, gain, segs, cosine, sine, wq, wk, wv, wo)
    shapes = [
        ((length, width), BF16),
        ((length, wq.shape[1]), BF16),
        ((length, wk.shape[1]), BF16),
        ((length, wv.shape[1]), BF16),
        ((length, wq.shape[1]), BF16),
        ((length, 128), F32),
        ((rows, width), F32),
        ((rows, width), F32),
    ]
    return pl.pallas_call(
        attend_kernel,
        out_shape=[jax.ShapeDtypeStruct(*shape) for shape in shapes],
        grid_spec=pltpu.PrefetchScalarGridSpec(
            num_scalar_prefetch=1,
            grid=(1,),
            in_specs=[full_spec(*t.shape) for t in operands[:-3]]
            + [pl.BlockSpec(memory_space=pl.ANY)] * 3,
            out_specs=[full_spec(*shape) for shape, _ in shapes],
            scratch_shapes=[pltpu.VMEM((length, width), F32)] * 2
            + [pltpu.VMEM(t.shape, BF16) for t in (wk, wv, wo)]
            + [pltpu.SemaphoreType.DMA((3,))],
        ),
        compiler_params=pltpu.CompilerParams(vmem_limit_bytes=56 * 1024 * 1024),
        cost_estimate=NO_COST,
    )(meta, *operands)


def attend_back_kernel(
    shares, meta, b_ref, segs, cos_ref, sin_ref, wq, wk, wv, wo,
    q_ref, k_ref, v_ref, mixed_ref, log_ref, *refs,
):
    share_outs, (own_out, other_out, grad_s, dq_s, part_s, *late_s, sems) = refs[:shares], refs[shares:]
    late = [
        pltpu.make_async_copy(source, target, sems.at[i])
        for i, (source, target) in enumerate(zip((wq, wk, wv), late_s))
    ]
    for copy in late:
        copy.start()
    own, other = row_places(meta, own_out.shape[0])
    grad_s[...] = dot_t(b_ref[...], wo[...]).astype(BF16)
    cosine, sine = cos_ref[...], -sin_ref[...]
    allowed = allowed_pairs(segs[...])
    wide, narrow = wq.shape[1], wk.shape[1]
    heads, heads_kv = wide // HEAD_DIM, narrow // HEAD_DIM
    group = heads // heads_kv

    def transposed_dot(left, right):
        return lax.dot_general(left, right, (((0,), (0,)), ((), ())), preferred_element_type=F32)

    for g in range(heads_kv):
        there = slice(g * HEAD_DIM, (g + 1) * HEAD_DIM)
        key, value = k_ref[:, there], v_ref[:, there]
        grad_key = grad_value = 0.0
        for h in range(g * group, (g + 1) * group):
            at = slice(h * HEAD_DIM, (h + 1) * HEAD_DIM)
            query, grad = q_ref[:, at], grad_s[:, at]
            prob = jnp.exp(masked_scores(query, key, allowed) - log_ref[:, h : h + 1])
            delta = jnp.sum(grad.astype(F32) * mixed_ref[:, at].astype(F32), axis=-1, keepdims=True)
            grad_scores = (prob * (dot_t(grad, value) - delta) * ATTN_SCALE).astype(BF16)
            dq_s[:, at] = jnp.dot(grad_scores, key, preferred_element_type=F32)
            grad_key = grad_key + transposed_dot(grad_scores, query)
            grad_value = grad_value + transposed_dot(prob.astype(BF16), grad)
        dq_s[:, wide + g * HEAD_DIM : wide + (g + 1) * HEAD_DIM] = grad_key
        at = wide + narrow + g * HEAD_DIM
        dq_s[:, at : at + HEAD_DIM] = grad_value
    dq = turn(dq_s[:, :wide], cosine, sine).astype(BF16)
    dk = turn(dq_s[:, wide : wide + narrow], cosine, sine).astype(BF16)
    dv = dq_s[:, wide + narrow :].astype(BF16)
    for copy in late:
        copy.wait()
    part_s[...] = sum(dot_t(part, held[...]) for part, held in zip((dq, dk, dv), late_s))
    own_out[...] = part_s[own, :]
    other_out[...] = part_s[other, :]
    for r in range(shares):

        @pl.when(meta[1] == r)
        def _():
            for step in range(shares):
                at = 0
                for part in (dq, dk, dv):
                    size = part.shape[1] // shares
                    index = (r + step) % shares
                    share_outs[step][:, at : at + size] = part[:, index * size : (index + 1) * size]
                    at += size


def attend_back(meta, shares, resid, segs, wq, wk, wv, wo, q, k, v, mixed, log_total):
    length, width = resid.shape
    cosine, sine = rope_tables(length, 128)
    operands = (resid, segs, cosine, sine, wq, wk, wv, wo, q, k, v, mixed, log_total)
    columns = wq.shape[1] + wk.shape[1] + wv.shape[1]
    shapes = [((length, columns // shares), BF16)] * shares
    shapes += [((length // 2, width), F32)] * 2
    return pl.pallas_call(
        functools.partial(attend_back_kernel, shares),
        out_shape=[jax.ShapeDtypeStruct(*shape) for shape in shapes],
        grid_spec=pltpu.PrefetchScalarGridSpec(
            num_scalar_prefetch=1,
            grid=(1,),
            in_specs=[
                pl.BlockSpec(memory_space=pl.ANY) if 4 <= i < 7 else full_spec(*t.shape)
                for i, t in enumerate(operands)
            ],
            out_specs=[full_spec(*shape) for shape, _ in shapes],
            scratch_shapes=[
                pltpu.VMEM((length, wq.shape[1]), BF16),
                pltpu.VMEM((length, columns), F32),
                pltpu.VMEM((length, width), F32),
            ]
            + [pltpu.VMEM(t.shape, BF16) for t in (wq, wk, wv)]
            + [pltpu.SemaphoreType.DMA((3,))],
        ),
        compiler_params=pltpu.CompilerParams(vmem_limit_bytes=56 * 1024 * 1024),
        cost_estimate=NO_COST,
    )(meta, *operands)


def expert_kernel(inner, aliased, experts, meta, *refs):
    blocks, ups, tables = (refs[i * inner : (i + 1) * inner] for i in range(3))
    refs = refs[3 * inner :]
    weight_refs, refs = refs[:6], refs[6 + aliased :]
    tokens_out, upstream_out = refs[:2]
    used_out, gate_out, up_out = refs[2:4], refs[4:6], refs[6:8]
    mix_out, in_out = refs[8 : 8 + inner], refs[8 + inner : 8 + 2 * inner]
    table, mix_total, in_total = refs[8 + 2 * inner :]
    rows, width = blocks[0].shape
    expert = pl.program_id(0)

    def place(j):
        return pl.ds(pl.multiple_of(lax.rem(meta[1] + j, inner) * rows, rows), rows)

    @pl.when(expert == 0)
    def _():
        for j in range(inner):
            tokens_out[place(j), :] = blocks[j][...]
            upstream_out[place(j), :] = ups[j][...]
            table[place(j), :] = tables[j][...].astype(F32)
        mix_total[...] = jnp.zeros_like(mix_total)
        in_total[...] = jnp.zeros_like(in_total)

    lane = lax.broadcasted_iota(jnp.int32, table.shape, 1)
    wanted = (lax.rem(lane, experts) == meta[2] + expert) & (lane < 3 * experts)
    weight = jnp.sum(jnp.where(wanted, table[...], 0.0), axis=1, keepdims=True)
    for half in range(2):
        gate, up, down = (weight_refs[2 * i + half][0] for i in range(3))
        pre_gate = jnp.dot(tokens_out[...], gate, preferred_element_type=F32)
        pre_up = jnp.dot(tokens_out[...], up, preferred_element_type=F32)
        grad_act = dot_t(upstream_out[...], down) * weight
        gate_sigmoid = 1.0 / (1.0 + jnp.exp(-pre_gate))
        silu = pre_gate * gate_sigmoid
        used = (silu * pre_up * weight).astype(BF16)
        grad_gate = grad_act * pre_up * gate_sigmoid * (1.0 + pre_gate * (1.0 - gate_sigmoid))
        grad_up = grad_act * silu
        used_out[half][0] = used
        gate_out[half][0] = grad_gate.astype(BF16)
        up_out[half][0] = grad_up.astype(BF16)
        mix_total[...] += jnp.dot(used, down, preferred_element_type=F32)
        in_total[...] += dot_t((grad_gate * weight).astype(BF16), gate) + dot_t(
            (grad_up * weight).astype(BF16), up
        )

    @pl.when(expert == pl.num_programs(0) - 1)
    def _():
        for j in range(inner):
            mix_out[j][...] = mix_total[place(j), :].astype(BF16)
            in_out[j][...] = in_total[place(j), :].astype(BF16)


def run_experts(meta, chunk_index, blocks, payloads, expert_weights, buffers, total, expert_count):
    inner, rows, width = len(blocks), blocks[0].shape[0], expert_weights[0].shape[1]
    firsts = [t.shape[1] // width - 1 for t in payloads]
    experts, half = expert_weights[0].shape[0], expert_weights[0].shape[2]
    chunk = inner * rows
    extra = 128
    by_chunk = pl.BlockSpec((chunk, width), lambda e, m: (m[0], 0))
    per_expert = pl.BlockSpec((1, chunk, half), lambda e, m: (e, m[0], 0))
    spread = pl.BlockSpec((1, width, half), lambda e, m: (e, 0, 0))
    tall = pl.BlockSpec((1, half, width), lambda e, m: (e, 0, 0))
    line = pl.BlockSpec((rows, width), lambda e, m: (chunk_index, 0))
    shapes = [jax.ShapeDtypeStruct((total, width), BF16)] * 2
    shapes += [jax.ShapeDtypeStruct((experts, total, half), BF16)] * 6
    shapes += [jax.ShapeDtypeStruct((total // inner, width), BF16)] * inner
    first = 1 + 3 * inner + 6
    return pl.pallas_call(
        functools.partial(expert_kernel, inner, len(buffers), expert_count),
        out_shape=shapes + [jax.ShapeDtypeStruct((rows, width), BF16)] * inner,
        grid_spec=pltpu.PrefetchScalarGridSpec(
            num_scalar_prefetch=1,
            grid=(experts,),
            in_specs=[full_spec(rows, width)] * inner
            + [pl.BlockSpec((rows, width), lambda e, m, at=at: (0, at)) for at in firsts]
            + [
                pl.BlockSpec((rows, extra), lambda e, m, at=at: (0, (at + 1) * (width // extra)))
                for at in firsts
            ]
            + [spread] * 4
            + [tall] * 2
            + [pl.BlockSpec(memory_space=pl.ANY)] * len(buffers),
            out_specs=[by_chunk] * 2
            + [per_expert] * 6
            + [line] * inner
            + [full_spec(rows, width)] * inner,
            scratch_shapes=[
                pltpu.VMEM((chunk, extra), F32),
                pltpu.VMEM((chunk, width), F32),
                pltpu.VMEM((chunk, width), F32),
            ],
        ),
        input_output_aliases={first + i: i for i in range(len(buffers))},
        compiler_params=pltpu.CompilerParams(vmem_limit_bytes=56 * 1024 * 1024),
        cost_estimate=NO_COST,
    )(meta, *blocks, *payloads, *payloads, *expert_weights, *buffers)


def weight_grads_kernel(count, downs, summed, tokens, *refs):
    sides, down, refs = refs[:count], refs[count : count + downs], refs[count + downs :]
    made = count + (downs > 0)
    added, outs = refs[: made * summed], refs[made * summed :]

    def store(index, at, value):
        if summed:
            value = value + added[index][at].astype(F32)
        outs[index][at] = value.astype(BF16)

    def product(left, right):
        return lax.dot_general(left, right, (((0,), (0,)), ((), ())), preferred_element_type=F32)

    for index, side in enumerate(sides):
        for e in range(side.shape[0]):
            store(index, e, product(tokens[...], side[e]))
    if downs:
        upstream, used = down
        store(count, 0, product(used[0], upstream[...]))


def weight_grads(tokens, sides, down, added):
    (experts, total, half), width = sides[0].shape, tokens.shape[1]
    steps = 2 * experts
    high, low = width // steps, half // 2
    spread = pl.BlockSpec((experts, high, half), lambda r: (0, r, 0))
    tall = pl.BlockSpec((1, low, width), lambda r: (lax.div(r, 2), lax.rem(r, 2), 0))
    specs = [spread] * len(sides) + [tall] * (len(down) > 0)
    shapes = [(experts, width, half)] * len(sides) + [(experts, half, width)] * (len(down) > 0)
    down_specs = [
        full_spec(total, width),
        pl.BlockSpec((1, total, low), lambda r: (lax.div(r, 2), 0, lax.rem(r, 2))),
    ]
    return pl.pallas_call(
        functools.partial(weight_grads_kernel, len(sides), len(down), len(added) > 0),
        out_shape=[jax.ShapeDtypeStruct(shape, BF16) for shape in shapes],
        grid=(steps,),
        in_specs=[pl.BlockSpec((total, high), lambda r: (0, r))]
        + [full_spec(experts, total, half)] * len(sides)
        + down_specs[: len(down)]
        + specs * (len(added) > 0),
        out_specs=specs,
        compiler_params=pltpu.CompilerParams(vmem_limit_bytes=62 * 1024 * 1024),
        cost_estimate=NO_COST,
    )(tokens, *sides, *down, *added)


def place_kernel(sizes, counts, meta, *refs):
    blocks, outs = refs[: len(counts)], refs[-len(sizes) :]
    step, first = pl.program_id(0), 0
    for block_ref, count in zip(blocks, counts):

        @pl.when((step >= first) & (step < first + count))
        def _():
            at = 0
            for size, out in zip(sizes, outs):
                out[...] = block_ref[0, :, at : at + size].astype(F32)
                at += size

        first += count


def place_line(meta, pieces, sizes, shapes, buffers):
    counts, (_, rows, width) = [t.shape[0] for t in pieces], pieces[0].shape
    firsts = [sum(counts[:i]) for i in range(len(counts))]
    taken = [
        pl.BlockSpec(
            (1, rows, width), lambda i, m, at=at, n=n: (jnp.minimum(jnp.maximum(i - at, 0), n - 1), 0, 0)
        )
        for at, n in zip(firsts, counts)
    ]
    low = [pl.BlockSpec((rows, size), lambda i, m: (m[4 * i], m[4 * i + 1])) for size in sizes[:-1]]
    low.append(pl.BlockSpec((rows, sizes[-1]), lambda i, m: (m[4 * i + 2], m[4 * i + 3])))
    return pl.pallas_call(
        functools.partial(place_kernel, sizes, counts),
        out_shape=[jax.ShapeDtypeStruct(shape, F32) for shape in shapes],
        grid_spec=pltpu.PrefetchScalarGridSpec(
            num_scalar_prefetch=1,
            grid=(sum(counts),),
            in_specs=taken + [pl.BlockSpec(memory_space=pl.ANY)] * len(buffers),
            out_specs=low,
        ),
        input_output_aliases={1 + len(pieces) + i: i for i in range(len(buffers))},
        cost_estimate=NO_COST,
    )(meta, *pieces, *buffers)


def dense_kernel(count, inner, meta, *refs):
    hidden, mixed, shares, resids = (refs[i * count : (i + 1) * count] for i in range(4))
    outs, scratch = refs[4 * count : -1], refs[-1]
    size, step = shares[0].shape[1], pl.program_id(0)

    def summed(lefts, rights):
        return sum(
            lax.dot_general(
                left[...], right[...], (((0,), (0,)), ((), ())), preferred_element_type=F32
            )
            for left, right in zip(lefts, rights)
        )

    scratch[:, :size] = summed(hidden, shares).astype(BF16)
    scratch[:, size:] = summed(mixed, resids).astype(BF16)
    rows = outs[0].shape[0]
    for k in range(len(outs) // inner):

        @pl.when(step == k)
        def _():
            for j in range(inner):
                start = pl.multiple_of(lax.rem(meta[0] + j, inner) * rows, rows)
                outs[k * inner + j][...] = scratch[pl.ds(start, rows), :]


def dense_blocks(meta, hidden, mixed, shares, resids, outer, inner):
    count, (length, width), size = len(hidden), hidden[0].shape, shares[0].shape[1]
    high, wide, steps = width // outer, mixed[0].shape[1], meta.shape[0] - 1
    part = resids[0].shape[1] * wide // width
    per = wide // high
    block = (high // inner, size + part)
    made = pl.pallas_call(
        functools.partial(dense_kernel, count, inner),
        out_shape=[jax.ShapeDtypeStruct(block, BF16)] * (steps * inner),
        grid_spec=pltpu.PrefetchScalarGridSpec(
            num_scalar_prefetch=1,
            grid=(steps,),
            in_specs=[pl.BlockSpec((length, high), lambda i, m: (0, m[1 + i]))] * count
            + [pl.BlockSpec((length, high), lambda i, m: (0, lax.rem(m[1 + i], per)))] * count
            + [full_spec(length, size)] * count
            + [pl.BlockSpec((length, part), lambda i, m: (0, lax.div(m[1 + i], per)))] * count,
            out_specs=[full_spec(*block)] * (steps * inner),
            scratch_shapes=[pltpu.VMEM((high, size + part), BF16)],
        ),
        compiler_params=pltpu.CompilerParams(vmem_limit_bytes=56 * 1024 * 1024),
        cost_estimate=NO_COST,
    )(meta, *hidden, *mixed, *shares, *resids)
    return [made[i * inner : (i + 1) * inner] for i in range(steps)]


def body(
    activations,
    segments,
    routes,
    route_weights,
    norm_attn_gain,
    norm_ffn_gain,
    query_weight,
    key_matrix,
    value_matrix,
    output_projection_weight,
    expert_gate,
    expert_up,
    expert_down,
    grad_output,
):
    tensor_rank = lax.axis_index("tensor")
    dp_rank = lax.axis_index("dp")
    dp_count = lax.axis_size("dp")
    outer, inner = grid_sizes()
    outer_rank = lax.axis_index("expert") // inner
    inner_rank = lax.axis_index("expert") % inner
    rows, width = activations.shape
    experts_here = expert_gate.shape[0]
    expert_count = experts_here * lax.axis_size("expert")

    named = routes[:, :, None] == jnp.arange(expert_count, dtype=jnp.int32)
    weight_table = jnp.sum(jnp.where(named, route_weights[:, :, None], 0.0), axis=1)
    high = lax.reduce_precision(weight_table, 8, 7)
    middle = lax.reduce_precision(weight_table - high, 8, 7)
    low = weight_table - high - middle
    table = jnp.concatenate([high, middle, low], axis=1).astype(BF16)
    table = jnp.pad(table, ((0, 0), (0, -table.shape[1] % 128)))
    payload = jnp.concatenate([grad_output, table], axis=1)
    up_one, up_three, up_line = shift_outer(payload, 1), shift_outer(payload, -1), inner_line(payload)
    heads_meta = jnp.stack([tensor_rank, dp_rank]).astype(jnp.int32)
    attn_weights = (query_weight, key_matrix, value_matrix, output_projection_weight)
    hidden, q, k, v, mixed, log_total, attn_own, attn_other = attend(
        heads_meta, activations, swap(activations), norm_attn_gain, segments, *attn_weights
    )
    x_own = activations.astype(F32)
    attn_own, attn_other, up_one, up_three, up_line = together(
        attn_own, attn_other, up_one, up_three, up_line
    )
    up_three = inner_line(up_three)
    residual = x_own + attn_own + swap(attn_other)
    normed_two, scale_two = norm_forward(residual, norm_ffn_gain)

    expert_weights = []
    for weights_own in (expert_gate, expert_up, expert_down):
        expert_weights += [weights_own, swap(weights_own)]
    first_expert = lax.axis_index("expert") * experts_here

    h_own = normed_two.astype(BF16)
    h_one, h_line = shift_outer(h_own, 1), inner_line(h_own)
    h_one, h_line, up_one, up_three = together(h_one, h_line, up_one, up_three)
    both = jnp.concatenate([h_one, up_one], axis=1)

    def experts_on(chunk, buffers, blocks, payloads):
        meta = jnp.stack([(outer_rank + chunk) % outer, inner_rank, first_expert])
        made = run_experts(
            meta.astype(jnp.int32), chunk, blocks, payloads, expert_weights, buffers,
            outer * inner * rows, expert_count,
        )
        return list(made[: 8 + inner]), made[8 + inner :]

    def line_sum(parts):
        return inner_sum(parts).astype(BF16)

    others_rows = [shift_dp(activations, step) for step in range(1, dp_count)]
    line, both = inner_line(both), shift_outer(both, 1)
    made = experts_on(0, [], h_line, up_line)
    made, line, both, others_rows = together(made, line, both, others_rows)
    buffers, in_zero = made
    others_swapped = [swap(t) for t in others_rows]
    made = experts_on(1, buffers, line, line)
    line, both = inner_line(both), shift_outer(both, 1)
    mixed_all = [mixed] + [shift_dp(mixed, step) for step in range(1, dp_count)]
    made, line, both, mixed_all, others_swapped = together(
        made, line, both, mixed_all, others_swapped
    )
    buffers, parts = made
    made = experts_on(2, buffers, line, line)
    line, sum_one = inner_line(both[:, :width]), line_sum(parts)
    hidden_all = [hidden]
    for step in range(1, dp_count):
        other = jnp.concatenate([others_rows[step - 1], others_swapped[step - 1]], axis=0)
        other = jnp.where(tensor_rank == 0, other, jnp.roll(other, rows, 0)).astype(F32)
        hidden_all.append(norm_forward(other, norm_attn_gain)[0].astype(BF16))
    made, line, sum_one, hidden_all = together(made, line, sum_one, hidden_all)
    buffers, parts = made
    sum_one, sum_two = shift_outer(sum_one, -1), line_sum(parts)
    made = experts_on(3, buffers, line, up_three)
    made, sum_one, sum_two, in_zero = together(made, sum_one, sum_two, in_zero)
    buffers, parts = made
    tokens_all, upstream_all, *pairs = buffers
    pairs, mix_lines = pairs[:6], pairs[6:]
    sides = [[pairs[at + half] for at in (0, 2, 4)] for half in range(2)]
    peers = weight_grads(tokens_all, sides[1][1:], (upstream_all, sides[1][0]), [])
    sum_two, sum_three, sum_zero = shift_outer(sum_two, -2), line_sum(parts), inner_sum(in_zero)
    sum_two, sum_three, sum_zero, peers = together(sum_two, sum_three, sum_zero, peers)
    mix_lines = after(mix_lines, sum_three)
    mix_found = inner_line_of(mix_lines)
    sum_three, arrived = shift_outer(sum_three, -3), [swap(peer) for peer in peers]
    grad_h_own = sum_zero.astype(F32)
    for term in (sum_one, sum_two, sum_three):
        grad_h_own = grad_h_own + term.astype(F32)

    def sum_dp(half):
        bit, found = 1, []
        while bit < dp_count:
            found.append(lax.ppermute(half, "dp", [(i, i ^ bit) for i in range(dp_count)]))
            bit *= 2
            if bit < dp_count:
                half = (half.astype(F32) + found.pop().astype(F32)).astype(BF16)
        return half, *found

    def total(pair):
        return sum(t.astype(F32) for t in pair)

    grad_norm_part, _ = norm_backward(residual, scale_two, norm_ffn_gain, grad_h_own)
    grad_resid = grad_output.astype(F32) + grad_norm_part
    resid_own = grad_resid.astype(BF16)
    resid_other = swap(resid_own)
    resid_full = jnp.where(
        tensor_rank == 0,
        jnp.concatenate([resid_own, resid_other], axis=0),
        jnp.concatenate([resid_other, resid_own], axis=0),
    )
    *shares, dh_own, dh_other = attend_back(
        heads_meta, dp_count, resid_full, segments, *attn_weights, q, k, v, mixed, log_total,
    )

    length, share_width = resid_full.shape[0], width // dp_count

    def columns(index):
        return lax.dynamic_slice_in_dim(resid_full, index * share_width, share_width, 1)

    resid_shares = [columns(dp_rank)]
    for step in range(1, dp_count):
        resid_shares.append(shift_dp(columns((dp_rank + step) % dp_count), step))
    shares, resid_shares, arrived = together(shares, resid_shares, arrived)
    all_shares = [shares[0]] + [shift_dp(shares[step], step) for step in range(1, dp_count)]
    parts = width // mixed.shape[1]
    sizes = [t.shape[1] // dp_count for t in (query_weight, key_matrix, value_matrix)]
    sizes.append(share_width // parts)
    aligned = all(size % 128 == 0 for size in sizes)
    (gate_half,) = weight_grads(tokens_all, sides[0][1:2], [], arrived[:1])
    all_shares, gate_half = together(all_shares, gate_half)
    block = width // (outer * inner)
    def row_terms(part, step):
        start = (outer_rank + step) % outer * inner
        return [
            lax.dynamic_slice_in_dim(part, (start + (inner_rank + j) % inner) * block, block, 0)
            for j in range(inner)
        ]

    if aligned:

        def blocks_of(steps, all_shares):
            meta = jnp.stack([inner_rank] + [(outer_rank + k) % outer for k in steps])
            return dense_blocks(
                meta.astype(jnp.int32), hidden_all, mixed_all, all_shares, resid_shares, outer, inner
            )

        terms = [None, None, *blocks_of([2], all_shares), None]
    else:
        qkv_part = dot(
            "sd,sa->da", jnp.concatenate(hidden_all, 0), jnp.concatenate(all_shares, 0), BF16
        )
        mix_part = dot(
            "sa,shb->hab",
            jnp.concatenate(mixed_all, 0),
            jnp.concatenate(resid_shares, 0).reshape(length * dp_count, parts, share_width // parts),
            BF16,
        )
        dense_part = jnp.concatenate([qkv_part, mix_part.reshape(width, -1)], axis=1)
        terms = [row_terms(dense_part, k) for k in range(outer)]
    terms[2], mix_found, arrived = together(terms[2], mix_found, arrived)
    mix_line = [
        sum(t[k * rows : (k + 1) * rows].astype(F32) for t in mix_found) for k in range(outer)
    ]
    two, dh_other = line_sum(terms[2]), swap(dh_other)
    carried = shift_outer(mix_line[2].astype(BF16), -1)
    if aligned:
        terms[1], terms[3], terms[0] = blocks_of([1, 3, 0], after(all_shares, terms[2]))
    two, dh_other, terms, arrived = together(two, dh_other, terms, arrived)
    gate_pair = sum_dp(after(gate_half, two))
    scale_one = lax.rsqrt(jnp.mean(x_own * x_own, axis=-1, keepdims=True) + EPS)
    grad_x_part, grad_attn_gain = norm_backward(
        x_own, scale_one, norm_attn_gain, dh_own + dh_other
    )
    grad_input = grad_resid + grad_x_part
    late = after((grad_h_own, residual, scale_two), terms)
    grad_ffn_gain = jnp.sum(late[0] * late[1] * late[2], axis=0)
    gains, hops = jnp.stack([grad_attn_gain, grad_ffn_gain]), hops_of_all()
    one, three = line_sum(terms[1]), line_sum(terms[3])
    two = shift_outer(two, -2)
    halves = weight_grads(tokens_all, sides[0][2:], (upstream_all, sides[0][0]), arrived[1:])
    one, three, terms, gains, carried, halves, two = together(
        one, three, terms, gains, carried, halves, two
    )
    mix_line[1] = mix_line[1].astype(F32) + carried.astype(F32)
    up_half, down_half = halves
    zero = inner_sum(terms[0])
    one, three = shift_outer(one, -1), shift_outer(three, -3)
    other, grad_input, gate_pair, zero, one, three = together(
        exchange(gains, hops[0]), grad_input, gate_pair, zero, one, three
    )
    gains, hops = gains + other, hops[1:]
    reduced = zero.astype(F32)
    for term in (one, two, three):
        reduced = reduced + term.astype(F32)
    reduced = reduced.astype(BF16)
    shapes = [t.shape for t in (query_weight, key_matrix, value_matrix)] + [(width // parts, width)]

    def block_of(from_one, from_three):
        mix = mix_line[0].astype(F32) + from_one.astype(F32) + from_three.astype(F32)
        return (after(residual, reduced) + mix).astype(BF16)

    mix_one, mix_three = mix_line[1].astype(BF16), mix_line[3].astype(BF16)
    if aligned:
        per, dense = outer * inner // parts, []

        def place(pieces, found, dense):
            meta = []
            for k, j, turn in found:
                index = (outer_rank + k) % outer * inner + (inner_rank + j) % inner
                share = (dp_rank - turn) % dp_count
                meta += [index, share, index % per, share * parts + index // per]
            return place_line(jnp.stack(meta).astype(jnp.int32), pieces, sizes, shapes, dense)

        others = range(1, dp_count)
        step = {
            "line": inner_line(reduced[None]),
            "next": shift_outer(reduced[None]),
            "others": [shift_dp(reduced, turn)[None] for turn in others],
            "gains": exchange(gains, hops[0]),
            "done": total(after(gate_pair, reduced)),
        }
        (step,) = together(step)
        gate_sum = step["done"]
        gains, hops = gains + step["gains"], hops[1:]
        lines = [step["line"]]
        held = jnp.concatenate([step["next"], *step["others"]], axis=0)
        up_pair, down_pair = (sum_dp(after(t, step["others"])) for t in (up_half, down_half))
        for k in range(1, outer + 1):
            step = {"line": inner_line(held), "gains": exchange(gains, hops[0]) if hops else gains}
            if k < outer:
                step["next"] = shift_outer(held if k + 1 < outer else held[1:])
            before = [(k - 1, turn) for turn in ([0] if k == 1 else [0, *others])]
            before = [(at - 1 if turn else at, turn) for at, turn in before]
            now = [(k, 0, 0)] * (k < outer) + [(k - 1, 0, turn) for turn in others]
            ready, entries = [held], list(now)
            for j in range(1, inner):
                ready.append(lines[-1][j])
                entries += [(at, j, turn) for at, turn in before]
            if k == 1:
                ready.append(lines[0][0])
                entries.append((0, 0, 0))
            made = place(ready, entries, dense)
            step["dense"] = made
            if k == 3:
                step["done"] = total(after(up_pair, made))
                step["mix"] = shift_outer(after(mix_one, held), -1)
            if k == 4:
                step["done"] = total(after(down_pair, made))
                step["mix"] = shift_outer(after(mix_three, held), -3)
            (step,) = together(step)
            if hops:
                gains, hops = gains + step["gains"], hops[1:]
            if k == 3:
                up_sum, mix_one = step["done"], step["mix"]
            if k == 4:
                down_sum, block_out = step["done"], block_of(mix_one, step["mix"])
            dense, held = step["dense"], step.get("next")
            lines.append(step["line"])
        for j in range(1, inner):
            dense = place([lines[-1][j]], [(outer - 1, j, turn) for turn in others], dense)
    else:
        for hop in hops:
            gains = gains + exchange(gains, hop)
        gate_sum, up_sum, down_sum = (
            total(pair) for pair in (gate_pair, sum_dp(up_half), sum_dp(down_half))
        )
        block_out = block_of(shift_outer(mix_one, -1), shift_outer(mix_three, -3))
        gathered = lax.all_gather(reduced, ("dp", "expert"), axis=0, tiled=True)
        gathered = gathered.reshape(dp_count, width, -1).astype(F32)
        starts = [sum(sizes[:i]) for i in range(len(sizes))]
        dense = [gathered[:, :, at : at + size] for at, size in zip(starts, sizes)]
        dense[:-1] = [t.transpose(1, 0, 2).reshape(width, -1) for t in dense[:-1]]
        mix_w = dense[-1].reshape(dp_count, parts, width // parts, -1)
        dense[-1] = mix_w.transpose(2, 0, 1, 3).reshape(width // parts, width)
    return (
        block_out,
        grad_input,
        gains[0],
        gains[1],
        *dense,
        gate_sum,
        up_sum,
        down_sum,
    )


def solution(mesh):
    tokens = P(("dp", "expert", "tensor"), None)
    whole = P()
    columns = P(None, "tensor")
    hidden_last = P("expert", None, "tensor")
    hidden_mid = P("expert", "tensor", None)
    mixer = P("tensor", None)
    return jax.shard_map(
        body,
        mesh=mesh,
        in_specs=(
            tokens,
            P(("dp", "expert"), None),
            tokens,
            tokens,
            whole,
            whole,
            columns,
            columns,
            columns,
            mixer,
            hidden_last,
            hidden_last,
            hidden_mid,
            tokens,
        ),
        out_specs=(
            tokens,
            tokens,
            whole,
            whole,
            columns,
            columns,
            columns,
            mixer,
            hidden_last,
            hidden_last,
            hidden_mid,
        ),
        check_vma=False,
    )
```
